32 devices in a mesh: bra: 8 (over z, y), ket: 4 (over x, core).
Axes of the slice: x: 2, y: 2, z: 4, core: 2. Of those that a mesh axis runs over, the one named last changes fastest.
Arguments:
- integrals: bfloat16 [256, 1024, 1024], P(('bra', 'ket')), may hold values from -0.1875 to 0.1875
- quartets: int32 [256, 4], P(('bra', 'ket')), may hold values from 0 to 127, as said below
- density: bfloat16 [128, 128, 12, 1024], P(('bra', 'ket')), may hold values from -6 to 6
- owner_map: int32 [128], replicated, may hold values from 0 to 127, each once
Outputs:
- fock_rows: bfloat16 [128, 128, 12, 1024], P(('bra', 'ket'))
The draws below stay inside these ranges and needn't reach their ends.
Inputs may be any that keep to these rules, and one draw needn't show every extreme that they name: `quartets`: the 32 block indices in the 8 rows of one device are distinct, and one block index is the first entry of some row on every device. Block row X of density and of fock_rows is stored at row owner_map[X]; each device holds 4 consecutive storage rows, in device order.
All inputs are finite; a program needn't handle non-finite values.
Results may differ from the reference program's by a relative error of at most 0.001.
Values may be sent and summed in bfloat16 or wider, within the bound.
No kernel may reach another device: no remote copies, remote signals or barrier semaphores. Data moves between devices by JAX's collectives and lax.ppermute only.
A program may use at most 384 MiB of HBM per device.

```python
import jax
import jax.numpy as jnp
from jax import lax

BF = 32
NDENS = 12
QB_DEV = 8
NB = 128
QUARTETS = 256


def draw_quartets(key, part):
    hot_block = jax.random.randint(jax.random.fold_in(key, 7), (), 0, NB)

    def device_rows(device_key):
        shuffled = jax.random.permutation(device_key, NB)
        ordering = jnp.argsort((shuffled == hot_block).astype(jnp.int32), stable=True)
        others = shuffled[ordering]
        chosen = jnp.concatenate([hot_block[None], others[:4 * QB_DEV - 1]])
        grouped = chosen.reshape(QB_DEV, 4)
        placement = jax.random.permutation(jax.random.fold_in(device_key, 3), QB_DEV)
        return grouped[placement]
    device_keys = jax.random.split(jax.random.fold_in(key, 11), QUARTETS // QB_DEV)
    return jax.vmap(device_rows)(device_keys).reshape(QUARTETS, 4).astype(jnp.int32)


def block_scale(key, extent, pieces, smallest, top_value):
    def one(dim, blocks):
        heights = jax.random.uniform(jax.random.fold_in(jax.random.fold_in(key, 6), dim), (blocks,), jnp.float32, smallest / len(pieces), top_value / len(pieces))
        return jnp.repeat(jnp.exp(heights), extent[dim] // blocks).reshape((-1,) + (1,) * (len(extent) - dim - 1))

    factor_of = one(*pieces[0])
    for cut in pieces[1:]:
        factor_of = factor_of * one(*cut)
    return factor_of


def gaussian(stream_key, shape, scale, most, cuts=(), dtype=jnp.bfloat16):
    result = scale * jax.random.normal(stream_key, shape, jnp.float32)
    if cuts:
        result = result * block_scale(stream_key, shape, cuts, -0.22, 0.18)
    return jnp.clip(result, -most, most).astype(dtype)


def setup_inputs(seed: int = 0) -> dict:
    streams_of = jax.random.split(jax.random.key(seed), 5)
    return {
        "integrals": gaussian(streams_of[0], (QUARTETS, BF * BF, BF * BF), (BF * BF) ** -0.5, 0.1875, ((0, 32),)),
        "quartets": draw_quartets(jax.random.fold_in(streams_of[4], 71), 0),
        "density": gaussian(streams_of[2], (NB, NB, NDENS, BF * BF), 1.0, 6.0, ((0, 32),)),
        "owner_map": jax.random.permutation(streams_of[3], NB).astype(jnp.int32),
    }


ROLE_ROW = (0, 0, 1, 1, 2, 3)
ROLE_COL = (1, 2, 2, 3, 3, 0)
SOURCE_ROLE = (4, 3, 5, 1, 0, 2)
TERM_WEIGHT = (2.0, -1.0, -1.0, -1.0, 2.0, -1.0)
EINSUM_FORMS = ("pqrs,nrs->npq", "pqrs,nqs->npr", "pqrs,nsp->nqr", "pqrs,npr->nqs", "pqrs,npq->nrs", "pqrs,nqr->nsp")


def contract_quartet(operands):
    quartet_block, read_tiles = operands
    integral = quartet_block.astype(jnp.float32).reshape(BF, BF, BF, BF)
    density_tiles = read_tiles.astype(jnp.float32).reshape(6, NDENS, BF, BF)
    results = []
    for which_role in range(6):
        contraction = jnp.einsum(EINSUM_FORMS[which_role], integral, density_tiles[SOURCE_ROLE[which_role]])
        results.append(TERM_WEIGHT[which_role] * contraction.reshape(NDENS, BF * BF))
    return jnp.stack(results)


def reference(integrals, quartets, density, owner_map):
    row_blocks = quartets[:, jnp.array(ROLE_ROW, jnp.int32)]
    col_blocks = quartets[:, jnp.array(ROLE_COL, jnp.int32)]
    storage_rows = owner_map[row_blocks]
    read_tiles = density[storage_rows, col_blocks]
    contributions = lax.map(contract_quartet, (integrals, read_tiles))
    fock_rows = jnp.zeros(density.shape, jnp.float32).at[storage_rows, col_blocks].add(contributions)
    return fock_rows.astype(jnp.bfloat16)
```

```python
import functools
import math

import jax
import jax.numpy as jnp
from jax import lax
from jax.experimental import pallas as pl
from jax.experimental.pallas import tpu as pltpu
from jax.sharding import PartitionSpec as P

ROLE_ROW = (0, 0, 1, 1, 2, 3)
ROLE_COL = (1, 2, 2, 3, 3, 0)
ROLES = 6
PAD_N = 16
ROWS = 16
AXES = ("bra", "ket")
BF16 = jnp.bfloat16
F32 = jnp.float32
VMEM_BYTES = 60 * 1024 * 1024


def params(axes=1):
    return pltpu.CompilerParams(
        dimension_semantics=("arbitrary",) * axes, vmem_limit_bytes=VMEM_BYTES
    )


def cost(flops, moved):
    return pl.CostEstimate(flops=int(flops), bytes_accessed=int(moved), transcendentals=0)


def hot_rows(target, width, base=0):
    columns = lax.broadcasted_iota(jnp.int32, (target.shape[0], width), 1) + base
    return jnp.where(columns == target, 1.0, 0.0).astype(BF16)


def hot_columns(target, height, base=0):
    rows = lax.broadcasted_iota(jnp.int32, (height, target.shape[1]), 0) + base
    return jnp.where(rows == target, 1.0, 0.0).astype(BF16)


def dot_nn(left, right):
    return jnp.dot(left, right, preferred_element_type=F32)


def dot_nt(left, right):
    return lax.dot_general(left, right, (((1,), (1,)), ((), ())), preferred_element_type=F32)


def gather_body(target_ref, density_ref, out_ref, hot_ref):
    peers, _, rows, lanes = out_ref.shape
    depth = hot_ref.shape[1]

    @pl.when(pl.program_id(0) == 0)
    def _():
        hot_ref[...] = hot_rows(target_ref[...], depth)

    source = density_ref[...].reshape(depth, lanes)
    half = lanes // 2
    for part in range(2):
        span = slice(part * half, (part + 1) * half)
        picked = dot_nn(hot_ref[...], source[:, span]).astype(BF16)
        out_ref[:, 0, :, span] = picked.reshape(peers, rows, half)


def gather_tiles(wanted, density_rows, slots):
    peers = wanted.shape[0]
    rows_dev, dens, blocks, lanes = density_rows.shape
    per = ROWS // slots
    groups = dens // per
    depth = rows_dev * per * blocks
    tile_row, tile_col = wanted // blocks, wanted % blocks
    inner = jnp.arange(per, dtype=jnp.int32)[None, :, None]
    target = tile_row[:, None, :] * (per * blocks) + inner * blocks + tile_col[:, None, :]
    target = jnp.where(wanted[:, None, :] >= 0, target, -1).reshape(peers * ROWS, 1)
    return pl.pallas_call(
        gather_body,
        grid=(groups,),
        in_specs=[
            pl.BlockSpec((peers * ROWS, 1), lambda g: (0, 0)),
            pl.BlockSpec((rows_dev, per, blocks, lanes), lambda g: (0, g, 0, 0)),
        ],
        out_specs=pl.BlockSpec((peers, 1, ROWS, lanes), lambda g: (0, g, 0, 0)),
        out_shape=jax.ShapeDtypeStruct((peers, groups, ROWS, lanes), BF16),
        scratch_shapes=[pltpu.VMEM((peers * ROWS, depth), BF16)],
        compiler_params=params(),
        name="gather_tiles",
    )(target, density_rows)


def select_body(target_ref, swap_ref, slots_ref, out_ref, total_ref):
    step = pl.program_id(0)
    depth, lanes = slots_ref.shape

    @pl.when(step == 0)
    def _():
        total_ref[...] = jnp.zeros_like(total_ref)

    total_ref[...] += dot_nn(hot_rows(target_ref[...], depth, step * depth), slots_ref[...])

    @pl.when(step == pl.num_programs(0) - 1)
    def _():
        span = out_ref.shape[0] // ROLES
        for role in range(ROLES):
            rows = slice(role * span, (role + 1) * span)
            tiles = total_ref[rows, :].astype(BF16)
            if role in (2, 3, 5):
                tiles = dot_nn(tiles, swap_ref[...]).astype(BF16)
            out_ref[rows, :] = tiles


def select_tiles(row_of, swap, received):
    depth, lanes = received.shape
    chunk = math.gcd(depth, 1024) if depth % 1024 == 0 else math.gcd(depth, 512)
    wanted = row_of.shape[0]
    return pl.pallas_call(
        select_body,
        grid=(depth // chunk,),
        in_specs=[
            pl.BlockSpec((wanted, 1), lambda k: (0, 0)),
            pl.BlockSpec((lanes, lanes), lambda k: (0, 0)),
            pl.BlockSpec((chunk, lanes), lambda k: (k, 0)),
        ],
        out_specs=pl.BlockSpec((wanted, lanes), lambda k: (0, 0)),
        out_shape=jax.ShapeDtypeStruct((wanted, lanes), BF16),
        scratch_shapes=[pltpu.VMEM((wanted, lanes), F32)],
        compiler_params=params(),
        name="select_tiles",
    )(row_of.reshape(wanted, 1), swap, received)


def exchange(read_lanes, trade, write, width):
    lanes = width * width
    blocks = lanes // 128
    low = 128 // width
    high = width // low
    for block in range(blocks):
        piece = read_lanes(block).reshape(high, low, width, 128)
        wide = jnp.concatenate(
            [piece[:, part].reshape(high * width, 128) for part in range(low)], axis=1
        )
        traded = dot_nn(wide, trade).astype(BF16)
        for part in range(low):
            group = traded[:, part * 128 : (part + 1) * 128].reshape(high, width, 128)
            for lead in range(high):
                write(block * low + part, lead, group[lead])


def regroup_body(swap_ref, trade_ref, block_ref, first_ref, second_ref, swapped_ref, *, width):
    lanes = width * width
    half = lanes // 2
    for part in range(2):
        span = slice(part * half, (part + 1) * half)
        swapped_ref[:, span] = dot_nn(block_ref[0], swap_ref[:, span]).astype(BF16)

    def writer(out_ref):
        def write(row_block, lane_block, value):
            out_ref[
                0,
                row_block * width : (row_block + 1) * width,
                lane_block * 128 : (lane_block + 1) * 128,
            ] = value

        return write

    exchange(
        lambda b: swapped_ref[:, b * 128 : (b + 1) * 128],
        trade_ref[...],
        writer(first_ref),
        width,
    )
    exchange(
        lambda b: block_ref[0, :, b * 128 : (b + 1) * 128],
        trade_ref[...],
        writer(second_ref),
        width,
    )


def regroup(integrals, swap, trade):
    count, lanes, _ = integrals.shape
    width = math.isqrt(lanes)
    whole = pl.BlockSpec((1, lanes, lanes), lambda i: (i, 0, 0))
    out = jax.ShapeDtypeStruct(integrals.shape, BF16)
    return pl.pallas_call(
        functools.partial(regroup_body, width=width),
        grid=(count,),
        in_specs=[
            pl.BlockSpec(swap.shape, lambda i: (0, 0)),
            pl.BlockSpec(trade.shape, lambda i: (0, 0)),
            whole,
        ],
        out_specs=[whole, whole],
        out_shape=[out, out],
        scratch_shapes=[pltpu.VMEM((lanes, lanes), BF16)],
        compiler_params=params(),
        cost_estimate=cost(count * 4 * lanes**3, count * 6 * lanes**2),
        name="regroup",
    )(swap, trade, integrals)


def contract_body(tiles_ref, block_ref, first_ref, second_ref, high_ref, low_ref):
    block, first, second = block_ref[0], first_ref[0], second_ref[0]

    def tile(role):
        return tiles_ref[role, 0]

    def put(role, term):
        top = term.astype(BF16)
        high_ref[role, 0] = top
        low_ref[role, 0] = (term - top.astype(F32)).astype(BF16)

    put(0, 2.0 * dot_nt(tile(4), block))
    put(4, 2.0 * dot_nn(tile(0), block))
    put(1, -dot_nn(tile(3), first))
    put(3, -dot_nt(tile(1), first))
    put(2, -dot_nt(tile(5), second))
    put(5, -dot_nn(tile(2), second))


def contract(tiles, integrals, first, second):
    count, lanes, _ = integrals.shape
    whole = pl.BlockSpec((1, lanes, lanes), lambda i: (i, 0, 0))
    part = pl.BlockSpec((ROLES, 1, PAD_N, lanes), lambda i: (0, i, 0, 0))
    out = jax.ShapeDtypeStruct((ROLES, count, PAD_N, lanes), BF16)
    return pl.pallas_call(
        contract_body,
        grid=(count,),
        in_specs=[part, whole, whole, whole],
        out_specs=[part, part],
        out_shape=[out, out],
        compiler_params=params(),
        name="contract",
    )(tiles, integrals, first, second)


def pack_body(target_ref, swap_ref, high_ref, low_ref, out_ref, terms_ref):
    half = high_ref.shape[0]

    @pl.when(pl.program_id(0) == 0)
    def _():
        span = half // ROLES
        for which, source in enumerate((high_ref, low_ref)):
            for role in range(ROLES):
                rows = source[role * span : (role + 1) * span, :]
                if role in (2, 3, 5):
                    rows = dot_nn(rows, swap_ref[...]).astype(BF16)
                start = which * half + role * span
                terms_ref[start : start + span, :] = rows

    out_ref[...] = dot_nn(hot_rows(target_ref[...], 2 * half), terms_ref[...]).astype(BF16)


def pack_terms(row_of, swap, high, low):
    count = row_of.shape[0]
    half, lanes = high.shape
    chunk = math.gcd(count, 512)
    return pl.pallas_call(
        pack_body,
        grid=(count // chunk,),
        in_specs=[
            pl.BlockSpec((chunk, 1), lambda k: (k, 0)),
            pl.BlockSpec((lanes, lanes), lambda k: (0, 0)),
            pl.BlockSpec((half, lanes), lambda k: (0, 0)),
            pl.BlockSpec((half, lanes), lambda k: (0, 0)),
        ],
        out_specs=pl.BlockSpec((chunk, lanes), lambda k: (k, 0)),
        out_shape=jax.ShapeDtypeStruct((count, lanes), BF16),
        scratch_shapes=[pltpu.VMEM((2 * half, lanes), BF16)],
        compiler_params=params(),
        name="pack_terms",
    )(row_of.reshape(count, 1), swap, high, low)


def scatter_body(target_ref, slots_ref, out_ref, hot_ref):
    rows_dev, per, blocks, lanes = out_ref.shape
    height = per * blocks
    depth = hot_ref.shape[1]

    @pl.when(pl.program_id(0) == 0)
    def _():
        hot_ref[...] = hot_columns(target_ref[...], rows_dev * height)

    slots = slots_ref[...].reshape(depth, lanes)
    for row in range(rows_dev):
        total = dot_nn(hot_ref[row * height : (row + 1) * height, :], slots)
        out_ref[row] = total.astype(BF16).reshape(per, blocks, lanes)


def scatter_terms(landing, arrived, rows_dev, blocks):
    peers, slots = landing.shape
    _, groups, _, lanes = arrived.shape
    per = ROWS // slots
    inner = jnp.arange(per, dtype=jnp.int32)[None, :, None]
    target = (landing // blocks)[:, None, :] * (per * blocks) + inner * blocks
    target = target + (landing % blocks)[:, None, :]
    target = jnp.where(landing[:, None, :] >= 0, target, -1).reshape(1, peers * ROWS)
    return pl.pallas_call(
        scatter_body,
        grid=(groups,),
        in_specs=[
            pl.BlockSpec((1, peers * ROWS), lambda g: (0, 0)),
            pl.BlockSpec((peers, 1, ROWS, lanes), lambda g: (0, g, 0, 0)),
        ],
        out_specs=pl.BlockSpec((rows_dev, per, blocks, lanes), lambda g: (0, g, 0, 0)),
        out_shape=jax.ShapeDtypeStruct((rows_dev, groups * per, blocks, lanes), BF16),
        scratch_shapes=[pltpu.VMEM((rows_dev * per * blocks, peers * ROWS), BF16)],
        compiler_params=params(),
        name="scatter_terms",
    )(target, arrived)


def tile_slots(quartets, owner_map, rows_dev):
    blocks_total = owner_map.shape[0]
    lead_shape = quartets.shape[:-2]
    row_blocks = jnp.stack([quartets[..., pick] for pick in ROLE_ROW], -2)
    col_blocks = jnp.stack([quartets[..., pick] for pick in ROLE_COL], -2)
    row_blocks = row_blocks.reshape(lead_shape + (-1,))
    col_blocks = col_blocks.reshape(lead_shape + (-1,))
    block_ids = jnp.arange(blocks_total, dtype=jnp.int32)
    storage = jnp.sum(jnp.where(row_blocks[..., None] == block_ids, owner_map, 0), axis=-1)
    target = storage // rows_dev
    local_tile = storage % rows_dev * blocks_total + col_blocks
    positions = jnp.arange(target.shape[-1])
    earlier = (target[..., None, :] == target[..., :, None]) & (
        positions[None, :] < positions[:, None]
    )
    slot_rank = jnp.sum(earlier.astype(jnp.int32), axis=-1)
    return target, slot_rank, local_tile


def permutation_tables(width):
    lanes = width * width
    low = 128 // width
    index = jnp.arange(lanes, dtype=jnp.int32)
    partner = index % width * width + index // width
    swap = (index[:, None] == partner[None, :]).astype(BF16)
    span = jnp.arange(low * 128, dtype=jnp.int32)
    lead, group, inner = span // 128, span % 128 // width, span % width
    partner = group * 128 + lead * width + inner
    trade = (span[None, :] == partner[:, None]).astype(BF16)
    return swap, trade


def slot_count(most):
    for slots in (4, 8, 16):
        if most <= slots:
            return slots
    raise ValueError(most)


def exchange_slots(array):
    return lax.all_to_all(array, AXES, split_axis=0, concat_axis=0, tiled=True)


def local(integrals, quartets, density, owner_map):
    rows_dev, blocks_total, dens_count, tile_len = density.shape
    devices = lax.axis_size(AXES)
    quartet_count = quartets.shape[0]
    tile_count = ROLES * quartet_count
    width = math.isqrt(tile_len)
    peer_most = 2 * rows_dev
    slots = slot_count(peer_most)
    per = ROWS // slots
    target, slot_rank, local_tile = tile_slots(quartets, owner_map, rows_dev)
    slot_index = target * slots + slot_rank
    slot_hit = slot_index[None, :] == jnp.arange(devices * slots)[:, None]
    requests = jnp.sum(jnp.where(slot_hit, local_tile[None, :] + 1, 0), axis=1) - 1
    tile_ids = jnp.arange(tile_count, dtype=jnp.int32)
    tile_of_slot = jnp.sum(jnp.where(slot_hit, tile_ids[None, :] + 1, 0), axis=1) - 1
    incoming = exchange_slots(requests.reshape(devices, slots))

    swap, trade = permutation_tables(width)
    density_rows = jnp.transpose(density, (0, 2, 1, 3))
    sent = gather_tiles(incoming, density_rows, slots)
    returned = exchange_slots(sent)
    first, second = regroup(integrals, swap, trade)

    dens_ids = jnp.arange(PAD_N, dtype=jnp.int32)[None, :]
    row_of = (
        target[:, None] * (dens_count * slots)
        + dens_ids // per * ROWS
        + dens_ids % per * slots
        + slot_rank[:, None]
    )
    row_of = jnp.where(dens_ids < dens_count, row_of, -1).reshape(-1)
    tiles = select_tiles(row_of, swap, returned.reshape(-1, tile_len))
    tiles = tiles.reshape(ROLES, quartet_count, PAD_N, tile_len)
    high, low = contract(tiles, integrals, first, second)

    out_slots = slot_count(2 * slots)
    out_per = ROWS // out_slots
    shape = (devices, dens_count // out_per, out_per, out_slots)
    tile_of_slot = tile_of_slot.reshape(devices, slots)
    none = jnp.full((devices, out_slots // 2 - slots), -1, jnp.int32)
    low_tile = jnp.where(tile_of_slot >= 0, tile_of_slot + tile_count, -1)
    term_of_slot = jnp.concatenate([tile_of_slot, none, low_tile, none], axis=1)
    dens_of = jnp.arange(dens_count, dtype=jnp.int32).reshape(1, shape[1], out_per, 1)
    term_row = term_of_slot[:, None, None, :] * PAD_N + dens_of
    term_row = jnp.where(term_of_slot[:, None, None, :] >= 0, term_row, -1)
    outgoing = pack_terms(
        term_row.reshape(-1),
        swap,
        high.reshape(tile_count * PAD_N, tile_len),
        low.reshape(tile_count * PAD_N, tile_len),
    )
    arrived = exchange_slots(outgoing.reshape(devices, shape[1], ROWS, tile_len))
    landing = jnp.concatenate([incoming, none, incoming, none], axis=1)
    fock = scatter_terms(landing, arrived, rows_dev, blocks_total)
    return jnp.transpose(fock, (0, 2, 1, 3))


def solution(mesh):
    return jax.shard_map(
        local,
        mesh=mesh,
        in_specs=(
            P(AXES, None, None),
            P(AXES, None),
            P(AXES, None, None, None),
            P(),
        ),
        out_specs=P(AXES, None, None, None),
        check_vma=False,
    )
```

```python
import functools
import math

import jax
import jax.numpy as jnp
from jax import lax
from jax.experimental import pallas as pl
from jax.experimental.pallas import tpu as pltpu
from jax.sharding import PartitionSpec as P

ROLE_ROW = (0, 0, 1, 1, 2, 3)
ROLE_COL = (1, 2, 2, 3, 3, 0)
ROLES = 6
PAD_N = 16
ROWS = 16
AXES = ("bra", "ket")
BF16 = jnp.bfloat16
F32 = jnp.float32
VMEM_BYTES = 60 * 1024 * 1024
FIRST_SLOTS = 4
RELAY_ROWS = 4
READ_SPARE = 8
TERM_SPARE = 16


def params(axes=1):
    return pltpu.CompilerParams(
        dimension_semantics=("arbitrary",) * axes, vmem_limit_bytes=VMEM_BYTES
    )


def cost(flops, moved):
    return pl.CostEstimate(flops=int(flops), bytes_accessed=int(moved), transcendentals=0)


def hot_rows(target, width, base=0):
    columns = lax.broadcasted_iota(jnp.int32, (target.shape[0], width), 1) + base
    return jnp.where(columns == target, 1.0, 0.0).astype(BF16)


def hot_columns(target, height, base=0):
    rows = lax.broadcasted_iota(jnp.int32, (height, target.shape[1]), 0) + base
    return jnp.where(rows == target, 1.0, 0.0).astype(BF16)


def dot_nn(left, right):
    return jnp.dot(left, right, preferred_element_type=F32)


def dot_nt(left, right):
    return lax.dot_general(left, right, (((1,), (1,)), ((), ())), preferred_element_type=F32)


def tile_rows(tiles, per, blocks):
    inner = jnp.arange(per, dtype=jnp.int32)[None, :, None]
    rows = (tiles // blocks * (per * blocks) + tiles % blocks)[:, None, :] + inner * blocks
    return jnp.where(tiles[:, None, :] >= 0, rows, -1)


def slot_rows(slot, slots, dens):
    per = ROWS // slots
    ids = jnp.arange(dens, dtype=jnp.int32)
    rows = (slot // slots * (dens * slots) + slot % slots)[..., None]
    rows = rows + ids // per * ROWS + ids % per * slots
    return jnp.where(slot[..., None] >= 0, rows, -1)


def relay_rows(peer, peers, dens):
    ids = jnp.arange(dens, dtype=jnp.int32)
    rows = peer[..., None] * RELAY_ROWS + ids // RELAY_ROWS * (peers * RELAY_ROWS) + ids % RELAY_ROWS
    return jnp.where(peer[..., None] >= 0, rows, -1)


def pad_rows(rows):
    pad = [(0, 0)] * (rows.ndim - 1) + [(0, PAD_N - rows.shape[-1])]
    return jnp.pad(rows, pad, constant_values=-1).reshape(-1)


def gather_body(target_ref, density_ref, out_ref, hot_ref):
    peers, _, rows, lanes = out_ref.shape
    depth = hot_ref.shape[1]

    @pl.when(pl.program_id(0) == 0)
    def _():
        hot_ref[...] = hot_rows(target_ref[...], depth)

    source = density_ref[...].reshape(depth, lanes)
    half = lanes // 2
    for part in range(2):
        span = slice(part * half, (part + 1) * half)
        picked = dot_nn(hot_ref[...], source[:, span]).astype(BF16)
        out_ref[:, 0, :, span] = picked.reshape(peers, rows, half)


def gather_tiles(wanted, density_rows, slots):
    peers = wanted.shape[0]
    rows_dev, dens, blocks, lanes = density_rows.shape
    per = ROWS // slots
    groups = dens // per
    depth = rows_dev * per * blocks
    target = tile_rows(wanted, per, blocks).reshape(peers * ROWS, 1)
    return pl.pallas_call(
        gather_body,
        grid=(groups,),
        in_specs=[
            pl.BlockSpec((peers * ROWS, 1), lambda g: (0, 0)),
            pl.BlockSpec((rows_dev, per, blocks, lanes), lambda g: (0, g, 0, 0)),
        ],
        out_specs=pl.BlockSpec((peers, 1, ROWS, lanes), lambda g: (0, g, 0, 0)),
        out_shape=jax.ShapeDtypeStruct((peers, groups, ROWS, lanes), BF16),
        scratch_shapes=[pltpu.VMEM((peers * ROWS, depth), BF16)],
        compiler_params=params(),
        name="gather_tiles",
    )(target, density_rows)


def pick_body(*refs, relay, swapped):
    if relay:
        relay_target_ref, relayed_ref, *refs = refs
    if swapped:
        swap_ref, *refs = refs
    target_ref, slots_ref, out_ref, total_ref = refs
    step = pl.program_id(0)
    depth = slots_ref.shape[0]

    @pl.when(step == 0)
    def _():
        if relay:
            hot = hot_rows(relay_target_ref[...], relayed_ref.shape[0])
            total_ref[...] = dot_nn(hot, relayed_ref[...])
        else:
            total_ref[...] = jnp.zeros_like(total_ref)

    total_ref[...] += dot_nn(hot_rows(target_ref[...], depth, step * depth), slots_ref[...])

    @pl.when(step == pl.num_programs(0) - 1)
    def _():
        if not swapped:
            out_ref[...] = total_ref[...].astype(BF16)
            return
        span = out_ref.shape[0] // ROLES
        for role in range(ROLES):
            rows = slice(role * span, (role + 1) * span)
            tiles = total_ref[rows, :].astype(BF16)
            if role in (2, 3, 5):
                tiles = dot_nn(tiles, swap_ref[...]).astype(BF16)
            out_ref[rows, :] = tiles


def pick_rows(row_of, received, swap=None, relay_row_of=None, relayed=None):
    depth, lanes = received.shape
    chunk = math.gcd(depth, 1024) if depth % 1024 == 0 else math.gcd(depth, 512)
    wanted = row_of.shape[0]
    column = pl.BlockSpec((wanted, 1), lambda k: (0, 0))
    specs, operands = [], []
    if relayed is not None:
        specs += [column, pl.BlockSpec(relayed.shape, lambda k: (0, 0))]
        operands += [relay_row_of.reshape(wanted, 1), relayed]
    if swap is not None:
        specs += [pl.BlockSpec(swap.shape, lambda k: (0, 0))]
        operands += [swap]
    return pl.pallas_call(
        functools.partial(pick_body, relay=relayed is not None, swapped=swap is not None),
        grid=(depth // chunk,),
        in_specs=[*specs, column, pl.BlockSpec((chunk, lanes), lambda k: (k, 0))],
        out_specs=pl.BlockSpec((wanted, lanes), lambda k: (0, 0)),
        out_shape=jax.ShapeDtypeStruct((wanted, lanes), BF16),
        scratch_shapes=[pltpu.VMEM((wanted, lanes), F32)],
        compiler_params=params(),
        name="pick_rows",
    )(*operands, row_of.reshape(wanted, 1), received)


def exchange(read_lanes, trade, write, width):
    lanes = width * width
    blocks = lanes // 128
    low = 128 // width
    high = width // low
    for block in range(blocks):
        piece = read_lanes(block).reshape(high, low, width, 128)
        wide = jnp.concatenate(
            [piece[:, part].reshape(high * width, 128) for part in range(low)], axis=1
        )
        traded = dot_nn(wide, trade).astype(BF16)
        for part in range(low):
            group = traded[:, part * 128 : (part + 1) * 128].reshape(high, width, 128)
            for lead in range(high):
                write(block * low + part, lead, group[lead])


def regroup_body(swap_ref, trade_ref, block_ref, first_ref, second_ref, swapped_ref, *, width):
    lanes = width * width
    half = lanes // 2
    for part in range(2):
        span = slice(part * half, (part + 1) * half)
        swapped_ref[:, span] = dot_nn(block_ref[0], swap_ref[:, span]).astype(BF16)

    def writer(out_ref):
        def write(row_block, lane_block, value):
            out_ref[
                0,
                row_block * width : (row_block + 1) * width,
                lane_block * 128 : (lane_block + 1) * 128,
            ] = value

        return write

    exchange(
        lambda b: swapped_ref[:, b * 128 : (b + 1) * 128],
        trade_ref[...],
        writer(first_ref),
        width,
    )
    exchange(
        lambda b: block_ref[0, :, b * 128 : (b + 1) * 128],
        trade_ref[...],
        writer(second_ref),
        width,
    )


def regroup(integrals, swap, trade):
    count, lanes, _ = integrals.shape
    width = math.isqrt(lanes)
    whole = pl.BlockSpec((1, lanes, lanes), lambda i: (i, 0, 0))
    out = jax.ShapeDtypeStruct(integrals.shape, BF16)
    return pl.pallas_call(
        functools.partial(regroup_body, width=width),
        grid=(count,),
        in_specs=[
            pl.BlockSpec(swap.shape, lambda i: (0, 0)),
            pl.BlockSpec(trade.shape, lambda i: (0, 0)),
            whole,
        ],
        out_specs=[whole, whole],
        out_shape=[out, out],
        scratch_shapes=[pltpu.VMEM((lanes, lanes), BF16)],
        compiler_params=params(),
        cost_estimate=cost(count * 4 * lanes**3, count * 6 * lanes**2),
        name="regroup",
    )(swap, trade, integrals)


def contract_body(tiles_ref, block_ref, first_ref, second_ref, high_ref, low_ref):
    block, first, second = block_ref[0], first_ref[0], second_ref[0]

    def tile(role):
        return tiles_ref[role, 0]

    def put(role, term):
        top = term.astype(BF16)
        high_ref[role, 0] = top
        low_ref[role, 0] = (term - top.astype(F32)).astype(BF16)

    put(0, 2.0 * dot_nt(tile(4), block))
    put(4, 2.0 * dot_nn(tile(0), block))
    put(1, -dot_nn(tile(3), first))
    put(3, -dot_nt(tile(1), first))
    put(2, -dot_nt(tile(5), second))
    put(5, -dot_nn(tile(2), second))


def contract(tiles, integrals, first, second):
    count, lanes, _ = integrals.shape
    whole = pl.BlockSpec((1, lanes, lanes), lambda i: (i, 0, 0))
    part = pl.BlockSpec((ROLES, 1, PAD_N, lanes), lambda i: (0, i, 0, 0))
    out = jax.ShapeDtypeStruct((ROLES, count, PAD_N, lanes), BF16)
    return pl.pallas_call(
        contract_body,
        grid=(count,),
        in_specs=[part, whole, whole, whole],
        out_specs=[part, part],
        out_shape=[out, out],
        compiler_params=params(),
        name="contract",
    )(tiles, integrals, first, second)


def pack_body(target_ref, swap_ref, high_ref, low_ref, out_ref, terms_ref):
    half = high_ref.shape[0]

    @pl.when(pl.program_id(0) == 0)
    def _():
        span = half // ROLES
        for which, source in enumerate((high_ref, low_ref)):
            for role in range(ROLES):
                rows = source[role * span : (role + 1) * span, :]
                if role in (2, 3, 5):
                    rows = dot_nn(rows, swap_ref[...]).astype(BF16)
                start = which * half + role * span
                terms_ref[start : start + span, :] = rows

    out_ref[...] = dot_nn(hot_rows(target_ref[...], 2 * half), terms_ref[...]).astype(BF16)


def pack_terms(row_of, swap, high, low):
    count = row_of.shape[0]
    half, lanes = high.shape
    chunk = math.gcd(count, 512)
    return pl.pallas_call(
        pack_body,
        grid=(count // chunk,),
        in_specs=[
            pl.BlockSpec((chunk, 1), lambda k: (k, 0)),
            pl.BlockSpec((lanes, lanes), lambda k: (0, 0)),
            pl.BlockSpec((half, lanes), lambda k: (0, 0)),
            pl.BlockSpec((half, lanes), lambda k: (0, 0)),
        ],
        out_specs=pl.BlockSpec((chunk, lanes), lambda k: (k, 0)),
        out_shape=jax.ShapeDtypeStruct((count, lanes), BF16),
        scratch_shapes=[pltpu.VMEM((2 * half, lanes), BF16)],
        compiler_params=params(),
        name="pack_terms",
    )(row_of.reshape(count, 1), swap, high, low)


def scatter_body(*refs, relay):
    if relay:
        relay_target_ref, relayed_ref, *refs, relay_hot_ref = refs
    target_ref, slots_ref, out_ref, hot_ref = refs
    rows_dev, per, blocks, lanes = out_ref.shape
    height = per * blocks
    depth = hot_ref.shape[1]

    @pl.when(pl.program_id(0) == 0)
    def _():
        hot_ref[...] = hot_columns(target_ref[...], rows_dev * height)
        if relay:
            relay_hot_ref[...] = hot_columns(relay_target_ref[...], rows_dev * height)

    slots = slots_ref[...].reshape(depth, lanes)
    for row in range(rows_dev):
        span = slice(row * height, (row + 1) * height)
        total = dot_nn(hot_ref[span, :], slots)
        if relay:
            total += dot_nn(relay_hot_ref[span, :], relayed_ref[0])
        out_ref[row] = total.astype(BF16).reshape(per, blocks, lanes)


def scatter_terms(landing, arrived, rows_dev, blocks, relay_landing=None, relayed=None):
    peers, slots = landing.shape
    _, groups, _, lanes = arrived.shape
    per = ROWS // slots
    high = rows_dev * per * blocks
    specs, operands = [], []
    scratch = [pltpu.VMEM((high, peers * ROWS), BF16)]
    if relayed is not None:
        depth = relayed.shape[1]
        specs = [
            pl.BlockSpec((1, depth), lambda g: (0, 0)),
            pl.BlockSpec((1, depth, lanes), lambda g: (g, 0, 0)),
        ]
        operands = [tile_rows(relay_landing[:, None], per, blocks).reshape(1, depth), relayed]
        scratch += [pltpu.VMEM((high, depth), BF16)]
    return pl.pallas_call(
        functools.partial(scatter_body, relay=relayed is not None),
        grid=(groups,),
        in_specs=[
            *specs,
            pl.BlockSpec((1, peers * ROWS), lambda g: (0, 0)),
            pl.BlockSpec((peers, 1, ROWS, lanes), lambda g: (0, g, 0, 0)),
        ],
        out_specs=pl.BlockSpec((rows_dev, per, blocks, lanes), lambda g: (0, g, 0, 0)),
        out_shape=jax.ShapeDtypeStruct((rows_dev, groups * per, blocks, lanes), BF16),
        scratch_shapes=scratch,
        compiler_params=params(),
        name="scatter_terms",
    )(*operands, tile_rows(landing, per, blocks).reshape(1, peers * ROWS), arrived)


def route_body(list_ref, state_hbm, out_ref, state_ref, sem, *, peers, spare, scale, outward):
    copy = pltpu.make_async_copy(state_hbm, state_ref, sem)
    copy.start()
    copy.wait()
    used_at = peers * peers

    def count_at(source, middle):
        return source * peers + middle if outward else middle * peers + source

    def one(index, failed):
        value = list_ref[index]
        row = index // spare
        other = jnp.maximum(value, 0) // scale
        source, last = (row, other) if outward else (other, row)

        def search(carry):
            tries, middle, found = carry
            full = state_ref[count_at(source, middle)] >= FIRST_SLOTS
            taken = state_ref[used_at + middle * peers + last] > 0
            found = jnp.where(full | taken, found, middle)
            following = jnp.where(middle + 1 == peers, 0, middle + 1)
            return tries + 1, following, found

        start = source + last
        start = jnp.where(start >= peers, start - peers, start)
        tries = jnp.where(value >= 0, 0, peers)
        _, _, found = lax.while_loop(
            lambda carry: (carry[0] < peers) & (carry[2] < 0), search, (tries, start, jnp.int32(-1))
        )
        out_ref[index] = -1

        @pl.when(found >= 0)
        def _():
            place = count_at(source, found)
            count = state_ref[place]
            out_ref[index] = found * FIRST_SLOTS + count
            state_ref[place] = count + 1
            state_ref[used_at + found * peers + last] = 1

        return failed + jnp.where((value >= 0) & (found < 0), 1, 0)

    out_ref[peers * spare] = lax.fori_loop(0, peers * spare, one, jnp.int32(0))


def route(lists, counts, scale, outward):
    peers, spare = lists.shape
    state = jnp.concatenate([counts, jnp.zeros_like(counts)]).reshape(-1)
    smem = pl.BlockSpec(memory_space=pltpu.SMEM)
    out = pl.pallas_call(
        functools.partial(
            route_body, peers=peers, spare=spare, scale=scale, outward=outward
        ),
        in_specs=[smem, pl.BlockSpec(memory_space=pl.ANY)],
        out_specs=smem,
        out_shape=jax.ShapeDtypeStruct((peers * spare + 1,), jnp.int32),
        scratch_shapes=[pltpu.SMEM((2 * peers * peers,), jnp.int32), pltpu.SemaphoreType.DMA],
        name="route",
    )(lists.reshape(-1), state)
    return out[:-1].reshape(peers, spare), out[-1]


def tile_keys(quartets, owner_map):
    blocks = owner_map.shape[0]
    row_blocks = jnp.stack([quartets[:, pick] for pick in ROLE_ROW]).reshape(-1)
    col_blocks = jnp.stack([quartets[:, pick] for pick in ROLE_COL]).reshape(-1)
    ids = jnp.arange(blocks, dtype=jnp.int32)
    storage = jnp.sum(jnp.where(row_blocks[:, None] == ids, owner_map, 0), axis=-1)
    return storage * blocks + col_blocks


def earlier(flags):
    ids = jnp.arange(flags.shape[-1])
    ahead = ids[:, None] < ids[None, :]
    return jnp.sum((flags[..., :, None] & ahead).astype(jnp.int32), axis=-2)


def choose(hit, values, axis):
    return jnp.sum(jnp.where(hit, values + 1, 0), axis=axis) - 1


def spilled(flags, values, spare):
    place = earlier(flags)
    hit = flags[..., None] & (place[..., None] == jnp.arange(spare))
    return choose(hit, values[..., None], -2), jnp.sum(flags.astype(jnp.int32), axis=-1)


def permutation_tables(width):
    lanes = width * width
    low = 128 // width
    index = jnp.arange(lanes, dtype=jnp.int32)
    partner = index % width * width + index // width
    swap = (index[:, None] == partner[None, :]).astype(BF16)
    span = jnp.arange(low * 128, dtype=jnp.int32)
    lead, group, inner = span // 128, span % 128 // width, span % width
    partner = group * 128 + lead * width + inner
    trade = (span[None, :] == partner[:, None]).astype(BF16)
    return swap, trade


def slot_count(most):
    for slots in (4, 8, 16):
        if most <= slots:
            return slots
    raise ValueError(most)


def exchange_slots(array):
    return lax.all_to_all(array, AXES, split_axis=0, concat_axis=0, tiled=True)


def slot_count(most):
    for slots in (4, 8, 16):
        if most <= slots:
            return slots
    raise ValueError(most)


def exchange_slots(array, axis=0):
    return lax.all_to_all(array, AXES, split_axis=axis, concat_axis=axis, tiled=True)


def relay(slot_of, received, dens):
    peers = slot_of.shape[0]
    lanes = received.shape[-1]
    groups = dens // RELAY_ROWS
    rows = slot_rows(slot_of, FIRST_SLOTS, dens).reshape(peers, groups, RELAY_ROWS)
    rows = jnp.transpose(rows, (1, 0, 2)).reshape(-1)
    sent = pick_rows(rows, received.reshape(-1, lanes))
    got = exchange_slots(sent.reshape(groups, peers, RELAY_ROWS, lanes), 1)
    return got.reshape(groups, peers * RELAY_ROWS, lanes)


def local(integrals, quartets, density, owner_map):
    rows_dev, blocks, dens, lanes = density.shape
    devices = lax.axis_size(AXES)
    me = lax.axis_index(AXES)
    quartet_count = quartets.shape[0]
    tile_count = ROLES * quartet_count
    span = rows_dev * blocks
    most = 2 * rows_dev
    tag = 1 << (2 * tile_count - 1).bit_length()
    scale = span * tag
    device_ids = jnp.arange(devices, dtype=jnp.int32)
    tile_ids = jnp.arange(tile_count, dtype=jnp.int32)
    place_ids = jnp.arange(FIRST_SLOTS, dtype=jnp.int32)

    key = tile_keys(quartets, owner_map)
    holder = key // span
    rank = jnp.sum(
        ((holder[:, None] == holder) & (tile_ids[:, None] < tile_ids)).astype(jnp.int32), axis=0
    )
    asked = jnp.sum((holder[:, None] == device_ids).astype(jnp.int32), axis=0)
    spare, spare_count = spilled(rank >= FIRST_SLOTS, key * tag + tile_ids, READ_SPARE)
    message = jnp.concatenate([key * 16 + rank, spare, asked, spare_count[None]])
    message = jnp.pad(message, (0, -message.shape[0] % 128))
    told = exchange_slots(jnp.broadcast_to(message, (devices,) + message.shape))
    keys, ranks = told[:, :tile_count] // 16, told[:, :tile_count] % 16
    read_list = told[:, tile_count : tile_count + READ_SPARE]
    counts = told[:, tile_count + READ_SPARE :][:, :devices]
    spare_counts = told[:, tile_count + READ_SPARE + devices]
    read_routes, read_misses = route(read_list, counts, scale, False)
    read_fits = (read_misses == 0) & (jnp.max(spare_counts) <= READ_SPARE)

    homes = keys // span
    mine = homes == me
    local_tile = keys - me * span
    swap, trade = permutation_tables(math.isqrt(lanes))

    def plan_terms():
        flat = keys.reshape(-1)
        shared = jnp.sum((flat[:, None] == flat).astype(jnp.int32), axis=0) > 1
        shared = shared.reshape(keys.shape)
        ahead = tile_ids[:, None] < tile_ids
        together = homes[:, :, None] == homes[:, None, :]
        before = 1 + (shared[:, :, None] & ahead).astype(jnp.int32)
        low_ranks = jnp.where(shared, jnp.sum(jnp.where(together, before, 0), axis=1), -1)
        at_home = homes[:, :, None] == device_ids
        low_counts = jnp.sum((at_home & shared[:, :, None]).astype(jnp.int32), axis=1)
        both_ranks = jnp.concatenate([ranks, low_ranks], axis=1)
        values = keys * tag + tile_ids
        values = jnp.concatenate([values, values + tile_count], axis=1)
        term_list, term_counts = spilled(both_ranks >= FIRST_SLOTS, values, TERM_SPARE)
        term_routes, misses = route(term_list, counts + low_counts, scale, True)
        fits = (misses == 0) & (jnp.max(term_counts) <= TERM_SPARE)
        return low_ranks, term_list, term_routes, fits

    def requests(slots):
        hit = mine[:, :, None] & (ranks[:, :, None] == jnp.arange(slots))
        return choose(hit, local_tile[:, :, None], 1)

    density_rows = jnp.transpose(density, (0, 2, 1, 3))

    def read_two_step():
        list_home = read_list // scale
        to_send = (read_list >= 0) & (list_home == me)
        slot_ids = jnp.arange(devices * FIRST_SLOTS, dtype=jnp.int32)
        hit = to_send.reshape(-1, 1) & (read_routes.reshape(-1, 1) == slot_ids)
        extra = choose(hit, (read_list // tag - me * span).reshape(-1, 1), 0)
        wanted = jnp.maximum(requests(FIRST_SLOTS), extra.reshape(devices, FIRST_SLOTS))
        received = exchange_slots(gather_tiles(wanted, density_rows, FIRST_SLOTS))
        groups = regroup(integrals, swap, trade)
        plan = plan_terms()
        middle, place = read_routes // FIRST_SLOTS, read_routes % FIRST_SLOTS
        passing = (read_list >= 0) & (middle == me)
        passed = choose(passing, list_home * FIRST_SLOTS + place, 1)
        relayed = relay(passed, received, dens)
        slot = jnp.where(rank < FIRST_SLOTS, holder * FIRST_SLOTS + rank, -1)
        my_middle = lax.dynamic_index_in_dim(middle, me, 0, keepdims=False)
        last = (spare[:, None] >= 0) & (spare[:, None] % tag == tile_ids)
        via = choose(last, my_middle[:, None], 0)
        tiles = pick_rows(
            pad_rows(slot_rows(slot, FIRST_SLOTS, dens)),
            received.reshape(-1, lanes),
            swap,
            pad_rows(relay_rows(via, devices, dens)),
            relayed.reshape(-1, lanes),
        )
        return tiles, groups, plan

    def read_one_step():
        slots = slot_count(most)
        received = exchange_slots(gather_tiles(requests(slots), density_rows, slots))
        groups = regroup(integrals, swap, trade)
        plan = plan_terms()
        rows = pad_rows(slot_rows(holder * slots + rank, slots, dens))
        return pick_rows(rows, received.reshape(-1, lanes), swap), groups, plan

    tiles, groups, plan = lax.cond(read_fits, read_two_step, read_one_step)
    low_ranks, term_list, term_routes, term_fits = plan
    tiles = tiles.reshape(ROLES, quartet_count, PAD_N, lanes)
    high, low = contract(tiles, integrals, *groups)
    high = high.reshape(tile_count * PAD_N, lanes)
    low = low.reshape(tile_count * PAD_N, lanes)

    def term_rows(term_of_slot, slots):
        per = ROWS // slots
        ids = jnp.arange(dens, dtype=jnp.int32).reshape(1, dens // per, per, 1)
        term = term_of_slot[:, None, None, :]
        return jnp.where(term >= 0, term * PAD_N + ids, -1).reshape(-1)

    def send(term_of_slot, slots):
        packed = pack_terms(term_rows(term_of_slot, slots), swap, high, low)
        return exchange_slots(packed.reshape(devices, dens * slots // ROWS, ROWS, lanes))

    to_holder = holder[:, None] == device_ids

    def write_two_step():
        my_low = lax.dynamic_index_in_dim(low_ranks, me, 0, keepdims=False)
        my_list = lax.dynamic_index_in_dim(term_list, me, 0, keepdims=False)
        my_routes = lax.dynamic_index_in_dim(term_routes, me, 0, keepdims=False)
        ends = jnp.concatenate([to_holder, to_holder])[:, :, None]
        places = jnp.concatenate([rank, my_low])[:, None, None] == place_ids
        both_ids = jnp.arange(2 * tile_count, dtype=jnp.int32)
        term_of_slot = choose(ends & places, both_ids[:, None, None], 0)
        slot_ids = jnp.arange(devices * FIRST_SLOTS, dtype=jnp.int32)
        hit = (my_list[:, None] >= 0) & (my_routes[:, None] == slot_ids)
        extra = choose(hit, (my_list % tag)[:, None], 0).reshape(devices, FIRST_SLOTS)
        arrived = send(jnp.maximum(term_of_slot, extra), FIRST_SLOTS)
        listed = term_list.reshape(-1, 1) >= 0
        middle = (term_routes // FIRST_SLOTS).reshape(-1, 1)
        list_home = term_list // scale
        came = device_ids[:, None] * FIRST_SLOTS + term_routes % FIRST_SLOTS
        passing = listed & (middle == me) & (list_home.reshape(-1, 1) == device_ids)
        relayed = relay(choose(passing, came.reshape(-1, 1), 0), arrived, dens)
        hit = mine[:, :, None] & (ranks[:, :, None] == place_ids)
        low_hit = mine[:, :, None] & (low_ranks[:, :, None] == place_ids)
        landing = choose(hit | low_hit, local_tile[:, :, None], 1)
        ending = listed & (list_home.reshape(-1, 1) == me) & (middle == device_ids)
        last = choose(ending, (term_list // tag - me * span).reshape(-1, 1), 0)
        return scatter_terms(landing, arrived, rows_dev, blocks, last, relayed)

    def write_one_step():
        slots = slot_count(most)
        wide = slot_count(2 * slots)
        places = rank[:, None, None] == jnp.arange(slots)
        term_of_slot = choose(to_holder[:, :, None] & places, tile_ids[:, None, None], 0)
        none = jnp.full((devices, wide // 2 - slots), -1, jnp.int32)
        low_term = jnp.where(term_of_slot >= 0, term_of_slot + tile_count, -1)
        arrived = send(jnp.concatenate([term_of_slot, none, low_term, none], axis=1), wide)
        wanted = requests(slots)
        landing = jnp.concatenate([wanted, none, wanted, none], axis=1)
        return scatter_terms(landing, arrived, rows_dev, blocks)

    fock = lax.cond(term_fits, write_two_step, write_one_step)
    return jnp.transpose(fock, (0, 2, 1, 3))


def solution(mesh):
    return jax.shard_map(
        local,
        mesh=mesh,
        in_specs=(
            P(AXES, None, None),
            P(AXES, None),
            P(AXES, None, None, None),
            P(),
        ),
        out_specs=P(AXES, None, None, None),
        check_vma=False,
    )
```

```python
import functools
import math

import jax
import jax.numpy as jnp
from jax import lax
from jax.experimental import pallas as pl
from jax.experimental.pallas import tpu as pltpu
from jax.sharding import PartitionSpec as P

ROLE_ROW = (0, 0, 1, 1, 2, 3)
ROLE_COL = (1, 2, 2, 3, 3, 0)
ROLES = 6
PAD_N = 16
ROWS = 16
AXES = ("bra", "ket")
BF16 = jnp.bfloat16
F32 = jnp.float32
VMEM_BYTES = 60 * 1024 * 1024
READ_SLOTS = 2
FIRST_SLOTS = 4
RELAY_ROWS = 4
READ_SPARE = 8
TERM_SPARE = 16


def params(axes=1):
    return pltpu.CompilerParams(
        dimension_semantics=("arbitrary",) * axes, vmem_limit_bytes=VMEM_BYTES
    )


def cost(flops, moved):
    return pl.CostEstimate(flops=int(flops), bytes_accessed=int(moved), transcendentals=0)


def hot_rows(target, width, base=0):
    columns = lax.broadcasted_iota(jnp.int32, (target.shape[0], width), 1) + base
    return jnp.where(columns == target, 1.0, 0.0).astype(BF16)


def hot_columns(target, height, base=0):
    rows = lax.broadcasted_iota(jnp.int32, (height, target.shape[1]), 0) + base
    return jnp.where(rows == target, 1.0, 0.0).astype(BF16)


def dot_nn(left, right):
    return jnp.dot(left, right, preferred_element_type=F32)


def dot_nt(left, right):
    return lax.dot_general(left, right, (((1,), (1,)), ((), ())), preferred_element_type=F32)


def rows_per_group(slots):
    return min(4, ROWS // slots)


def tile_rows(tiles, per, blocks):
    inner = jnp.arange(per, dtype=jnp.int32)[None, :, None]
    rows = (tiles // blocks * (per * blocks) + tiles % blocks)[:, None, :] + inner * blocks
    return jnp.where(tiles[:, None, :] >= 0, rows, -1)


def slot_rows(slot, slots, dens):
    ids = jnp.arange(dens, dtype=jnp.int32)
    per = rows_per_group(slots)
    rows = (slot // slots * (dens * slots) + slot % slots)[..., None]
    rows = rows + ids // per * (per * slots) + ids % per * slots
    return jnp.where(slot[..., None] >= 0, rows, -1)


def pad_rows(rows):
    pad = [(0, 0)] * (rows.ndim - 1) + [(0, PAD_N - rows.shape[-1])]
    return jnp.pad(rows, pad, constant_values=-1).reshape(-1)


def gather_body(target_ref, density_ref, *refs):
    *out_refs, hot_ref = refs
    peers, _, rows, lanes = out_refs[0].shape
    depth = hot_ref.shape[1]

    @pl.when(pl.program_id(0) == 0)
    def _():
        hot_ref[...] = hot_rows(target_ref[...], depth)

    source = density_ref[...].reshape(depth, lanes)
    half = lanes // 2
    for part in range(2):
        span = slice(part * half, (part + 1) * half)
        picked = dot_nn(hot_ref[...], source[:, span]).reshape(-1, rows, half)
        for which, out_ref in enumerate(out_refs):
            mine = picked[which * peers : (which + 1) * peers]
            out_ref[:, 0, :, span] = mine.astype(BF16)


def gather_tiles(wanted, density_rows):
    peers, slots = wanted[0].shape
    rows_dev, dens, blocks, lanes = density_rows.shape
    per = rows_per_group(slots)
    groups, rows = dens // per, per * slots
    depth = rows_dev * per * blocks
    target = jnp.concatenate([tile_rows(each, per, blocks).reshape(-1, 1) for each in wanted])
    out = jax.ShapeDtypeStruct((peers, groups, rows, lanes), BF16)
    return pl.pallas_call(
        gather_body,
        grid=(groups,),
        in_specs=[
            pl.BlockSpec(target.shape, lambda g: (0, 0)),
            pl.BlockSpec((rows_dev, per, blocks, lanes), lambda g: (0, g, 0, 0)),
        ],
        out_specs=[pl.BlockSpec((peers, 1, rows, lanes), lambda g: (0, g, 0, 0))] * len(wanted),
        out_shape=[out] * len(wanted),
        scratch_shapes=[pltpu.VMEM((target.shape[0], depth), BF16)],
        compiler_params=params(),
        name="gather_tiles",
    )(target, density_rows)


def pick_body(*refs, relay, swapped, based):
    if relay:
        relay_target_ref, relayed_ref, *refs = refs
    if based:
        base_ref, *refs = refs
    if swapped:
        swap_ref, *refs = refs
    target_ref, slots_ref, out_ref, total_ref = refs
    step = pl.program_id(0)
    depth = slots_ref.shape[0]

    @pl.when(step == 0)
    def _():
        if relay:
            hot = hot_rows(relay_target_ref[...], relayed_ref.shape[0])
            total_ref[...] = dot_nn(hot, relayed_ref[...])
        elif based:
            total_ref[...] = base_ref[...].astype(F32)
        else:
            total_ref[...] = jnp.zeros_like(total_ref)

    total_ref[...] += dot_nn(hot_rows(target_ref[...], depth, step * depth), slots_ref[...])

    @pl.when(step == pl.num_programs(0) - 1)
    def _():
        if not swapped:
            out_ref[...] = total_ref[...].astype(BF16)
            return
        span = out_ref.shape[0] // ROLES
        for role in range(ROLES):
            rows = slice(role * span, (role + 1) * span)
            tiles = total_ref[rows, :].astype(BF16)
            if role in (2, 3, 5):
                tiles = dot_nn(tiles, swap_ref[...]).astype(BF16)
            out_ref[rows, :] = tiles


def pick_rows(row_of, received, swap=None, relay_row_of=None, relayed=None, base=None):
    depth, lanes = received.shape
    chunk = math.gcd(depth, 1024) if depth % 1024 == 0 else math.gcd(depth, 512)
    wanted = row_of.shape[0]
    column = pl.BlockSpec((wanted, 1), lambda k: (0, 0))
    specs, operands = [], []
    if relayed is not None:
        specs += [column, pl.BlockSpec(relayed.shape, lambda k: (0, 0))]
        operands += [relay_row_of.reshape(wanted, 1), relayed]
    if base is not None:
        specs += [pl.BlockSpec(base.shape, lambda k: (0, 0))]
        operands += [base]
    if swap is not None:
        specs += [pl.BlockSpec(swap.shape, lambda k: (0, 0))]
        operands += [swap]
    return pl.pallas_call(
        functools.partial(
            pick_body,
            relay=relayed is not None,
            swapped=swap is not None,
            based=base is not None,
        ),
        grid=(depth // chunk,),
        in_specs=[*specs, column, pl.BlockSpec((chunk, lanes), lambda k: (k, 0))],
        out_specs=pl.BlockSpec((wanted, lanes), lambda k: (0, 0)),
        out_shape=jax.ShapeDtypeStruct((wanted, lanes), BF16),
        scratch_shapes=[pltpu.VMEM((wanted, lanes), F32)],
        compiler_params=params(),
        name="pick_rows",
    )(*operands, row_of.reshape(wanted, 1), received)


def exchange(read_lanes, trade, write, width):
    lanes = width * width
    blocks = lanes // 128
    low = 128 // width
    high = width // low
    for block in range(blocks):
        piece = read_lanes(block).reshape(high, low, width, 128)
        wide = jnp.concatenate(
            [piece[:, part].reshape(high * width, 128) for part in range(low)], axis=1
        )
        traded = dot_nn(wide, trade).astype(BF16)
        for part in range(low):
            group = traded[:, part * 128 : (part + 1) * 128].reshape(high, width, 128)
            for lead in range(high):
                write(block * low + part, lead, group[lead])


def regroup_body(swap_ref, trade_ref, block_ref, first_ref, second_ref, swapped_ref, *, width):
    lanes = width * width
    half = lanes // 2
    for part in range(2):
        span = slice(part * half, (part + 1) * half)
        swapped_ref[:, span] = dot_nn(block_ref[0], swap_ref[:, span]).astype(BF16)

    def writer(out_ref):
        def write(row_block, lane_block, value):
            out_ref[
                0,
                row_block * width : (row_block + 1) * width,
                lane_block * 128 : (lane_block + 1) * 128,
            ] = value

        return write

    exchange(
        lambda b: swapped_ref[:, b * 128 : (b + 1) * 128],
        trade_ref[...],
        writer(first_ref),
        width,
    )
    exchange(
        lambda b: block_ref[0, :, b * 128 : (b + 1) * 128],
        trade_ref[...],
        writer(second_ref),
        width,
    )


def regroup(integrals, swap, trade):
    count, lanes, _ = integrals.shape
    width = math.isqrt(lanes)
    whole = pl.BlockSpec((1, lanes, lanes), lambda i: (i, 0, 0))
    out = jax.ShapeDtypeStruct(integrals.shape, BF16)
    return pl.pallas_call(
        functools.partial(regroup_body, width=width),
        grid=(count,),
        in_specs=[
            pl.BlockSpec(swap.shape, lambda i: (0, 0)),
            pl.BlockSpec(trade.shape, lambda i: (0, 0)),
            whole,
        ],
        out_specs=[whole, whole],
        out_shape=[out, out],
        scratch_shapes=[pltpu.VMEM((lanes, lanes), BF16)],
        compiler_params=params(),
        cost_estimate=cost(count * 4 * lanes**3, count * 6 * lanes**2),
        name="regroup",
    )(swap, trade, integrals)


def contract_body(tiles_ref, block_ref, first_ref, second_ref, high_ref, low_ref):
    block, first, second = block_ref[0], first_ref[0], second_ref[0]

    def tile(role):
        return tiles_ref[role, 0]

    def put(role, term):
        top = term.astype(BF16)
        high_ref[role, 0] = top
        low_ref[role, 0] = (term - top.astype(F32)).astype(BF16)

    put(0, 2.0 * dot_nt(tile(4), block))
    put(4, 2.0 * dot_nn(tile(0), block))
    put(1, -dot_nn(tile(3), first))
    put(3, -dot_nt(tile(1), first))
    put(2, -dot_nt(tile(5), second))
    put(5, -dot_nn(tile(2), second))


def contract(tiles, integrals, first, second):
    count, lanes, _ = integrals.shape
    whole = pl.BlockSpec((1, lanes, lanes), lambda i: (i, 0, 0))
    part = pl.BlockSpec((ROLES, 1, PAD_N, lanes), lambda i: (0, i, 0, 0))
    out = jax.ShapeDtypeStruct((ROLES, count, PAD_N, lanes), BF16)
    return pl.pallas_call(
        contract_body,
        grid=(count,),
        in_specs=[part, whole, whole, whole],
        out_specs=[part, part],
        out_shape=[out, out],
        compiler_params=params(),
        name="contract",
    )(tiles, integrals, first, second)


def pack_body(target_ref, swap_ref, high_ref, low_ref, out_ref, terms_ref):
    half = high_ref.shape[0]

    @pl.when(pl.program_id(0) == 0)
    def _():
        span = half // ROLES
        for which, source in enumerate((high_ref, low_ref)):
            for role in range(ROLES):
                rows = source[role * span : (role + 1) * span, :]
                if role in (2, 3, 5):
                    rows = dot_nn(rows, swap_ref[...]).astype(BF16)
                start = which * half + role * span
                terms_ref[start : start + span, :] = rows

    out_ref[...] = dot_nn(hot_rows(target_ref[...], 2 * half), terms_ref[...]).astype(BF16)


def pack_terms(row_of, swap, high, low):
    count = row_of.shape[0]
    half, lanes = high.shape
    chunk = math.gcd(count, 512)
    return pl.pallas_call(
        pack_body,
        grid=(count // chunk,),
        in_specs=[
            pl.BlockSpec((chunk, 1), lambda k: (k, 0)),
            pl.BlockSpec((lanes, lanes), lambda k: (0, 0)),
            pl.BlockSpec((half, lanes), lambda k: (0, 0)),
            pl.BlockSpec((half, lanes), lambda k: (0, 0)),
        ],
        out_specs=pl.BlockSpec((chunk, lanes), lambda k: (k, 0)),
        out_shape=jax.ShapeDtypeStruct((count, lanes), BF16),
        scratch_shapes=[pltpu.VMEM((2 * half, lanes), BF16)],
        compiler_params=params(),
        name="pack_terms",
    )(row_of.reshape(count, 1), swap, high, low)


def scatter_body(*refs, relay):
    if relay:
        relay_target_ref, relayed_ref, *refs, relay_hot_ref = refs
    target_ref, slots_ref, out_ref, hot_ref = refs
    rows_dev, per, blocks, lanes = out_ref.shape
    height = per * blocks
    depth = hot_ref.shape[1]

    @pl.when(pl.program_id(0) == 0)
    def _():
        hot_ref[...] = hot_columns(target_ref[...], rows_dev * height)
        if relay:
            relay_hot_ref[...] = hot_columns(relay_target_ref[...], rows_dev * height)

    slots = slots_ref[...].reshape(depth, lanes)
    for row in range(rows_dev):
        span = slice(row * height, (row + 1) * height)
        total = dot_nn(hot_ref[span, :], slots)
        if relay:
            total += dot_nn(relay_hot_ref[span, :], relayed_ref[0])
        out_ref[row] = total.astype(BF16).reshape(per, blocks, lanes)


def scatter_terms(landing, arrived, rows_dev, blocks, relay_landing=None, relayed=None):
    peers, slots = landing.shape
    _, groups, _, lanes = arrived.shape
    per = rows_per_group(slots)
    high = rows_dev * per * blocks
    specs, operands = [], []
    scratch = [pltpu.VMEM((high, peers * ROWS), BF16)]
    if relayed is not None:
        depth = relayed.shape[1]
        specs = [
            pl.BlockSpec((1, depth), lambda g: (0, 0)),
            pl.BlockSpec((1, depth, lanes), lambda g: (g, 0, 0)),
        ]
        operands = [tile_rows(relay_landing[:, None], per, blocks).reshape(1, depth), relayed]
        scratch += [pltpu.VMEM((high, depth), BF16)]
    return pl.pallas_call(
        functools.partial(scatter_body, relay=relayed is not None),
        grid=(groups,),
        in_specs=[
            *specs,
            pl.BlockSpec((1, peers * ROWS), lambda g: (0, 0)),
            pl.BlockSpec((peers, 1, ROWS, lanes), lambda g: (0, g, 0, 0)),
        ],
        out_specs=pl.BlockSpec((rows_dev, per, blocks, lanes), lambda g: (0, g, 0, 0)),
        out_shape=jax.ShapeDtypeStruct((rows_dev, groups * per, blocks, lanes), BF16),
        scratch_shapes=scratch,
        compiler_params=params(),
        name="scatter_terms",
    )(*operands, tile_rows(landing, per, blocks).reshape(1, peers * ROWS), arrived)


def route_body(list_ref, state_hbm, out_ref, state_ref, sem, *, spare, begin, scale, caps, outward):
    peers = list_ref.shape[0]
    second = peers * peers
    copy = pltpu.make_async_copy(state_hbm, state_ref, sem)
    copy.start()
    copy.wait()

    def first_at(source, middle):
        return source * peers + middle if outward else middle * peers + source

    def one(row, place, failed):
        other = list_ref[row, begin + place] // scale
        source, last = (row, other) if outward else (other, row)

        def search(carry):
            tries, middle, found = carry
            full = state_ref[first_at(source, middle)] >= caps[0]
            taken = state_ref[second + last * peers + middle] >= caps[1]
            found = jnp.where(full | taken, found, middle)
            following = jnp.where(middle + 1 == peers, 0, middle + 1)
            return tries + 1, following, found

        start = source + last
        start = jnp.where(start >= peers, start - peers, start)
        _, _, found = lax.while_loop(
            lambda carry: (carry[0] < peers) & (carry[2] < 0),
            search,
            (jnp.int32(0), start, jnp.int32(-1)),
        )
        index = row * spare + place
        out_ref[index] = -1

        @pl.when(found >= 0)
        def _():
            first, then = first_at(source, found), second + last * peers + found
            out_ref[index] = found * 64 + state_ref[first] * 8 + state_ref[then]
            state_ref[first] = state_ref[first] + 1
            state_ref[then] = state_ref[then] + 1

        return failed + jnp.where(found < 0, 1, 0)

    def each(row, failed):
        count = jnp.minimum(list_ref[row, begin + spare], spare)
        return lax.fori_loop(0, count, functools.partial(lambda p, f, r: one(r, p, f), r=row), failed)

    out_ref[peers * spare] = lax.fori_loop(0, peers, each, jnp.int32(0))


def route(table, begin, spare, first, second, caps, scale, outward):
    peers = table.shape[0]
    state = jnp.concatenate([first, second]).reshape(-1)
    smem = pl.BlockSpec(memory_space=pltpu.SMEM)
    out = pl.pallas_call(
        functools.partial(
            route_body, spare=spare, begin=begin, scale=scale, caps=caps, outward=outward
        ),
        in_specs=[smem, pl.BlockSpec(memory_space=pl.ANY)],
        out_specs=smem,
        out_shape=jax.ShapeDtypeStruct((peers * spare + 1,), jnp.int32),
        scratch_shapes=[pltpu.SMEM((2 * peers * peers,), jnp.int32), pltpu.SemaphoreType.DMA],
        name="route",
    )(table, state)
    routes = out[:-1].reshape(peers, spare)
    listed = (table[:, begin : begin + spare] >= 0) & (routes >= 0)
    routes = jnp.where(listed, routes, -1)
    middles = jnp.where(listed, routes // 64, -1)
    return middles, routes // 8 % 8, routes % 8, out[-1]


def tile_keys(quartets, owner_map):
    blocks = owner_map.shape[0]
    row_blocks = jnp.stack([quartets[:, pick] for pick in ROLE_ROW]).reshape(-1)
    col_blocks = jnp.stack([quartets[:, pick] for pick in ROLE_COL]).reshape(-1)
    ids = jnp.arange(blocks, dtype=jnp.int32)
    storage = jnp.sum(jnp.where(row_blocks[:, None] == ids, owner_map, 0), axis=-1)
    return storage * blocks + col_blocks


def earlier(flags):
    ids = jnp.arange(flags.shape[-1])
    ahead = ids[:, None] < ids[None, :]
    return jnp.sum((flags[..., :, None] & ahead).astype(jnp.int32), axis=-2)


def choose(hit, values, axis):
    return jnp.sum(jnp.where(hit, values + 1, 0), axis=axis) - 1


def spilled(flags, values, spare):
    place = earlier(flags)
    hit = flags[..., None] & (place[..., None] == jnp.arange(spare))
    return choose(hit, values[..., None], -2), jnp.sum(flags.astype(jnp.int32), axis=-1)


def permutation_tables(width):
    lanes = width * width
    low = 128 // width
    index = jnp.arange(lanes, dtype=jnp.int32)
    partner = index % width * width + index // width
    swap = (index[:, None] == partner[None, :]).astype(BF16)
    span = jnp.arange(low * 128, dtype=jnp.int32)
    lead, group, inner = span // 128, span % 128 // width, span % width
    partner = group * 128 + lead * width + inner
    trade = (span[None, :] == partner[:, None]).astype(BF16)
    return swap, trade


def slot_count(most):
    for slots in (4, 8, 16):
        if most <= slots:
            return slots
    raise ValueError(most)


def exchange_slots(array):
    return lax.all_to_all(array, AXES, split_axis=0, concat_axis=0, tiled=True)


def slot_count(most):
    for slots in (4, 8, 16):
        if most <= slots:
            return slots
    raise ValueError(most)


def exchange_slots(array, axis=0):
    return lax.all_to_all(array, AXES, split_axis=axis, concat_axis=axis, tiled=True)


def hand_on(slot_of, received, dens):
    peers = slot_of.shape[0]
    lanes = received.shape[-1]
    groups = dens // RELAY_ROWS
    rows = slot_rows(slot_of, FIRST_SLOTS, dens).reshape(peers, groups, RELAY_ROWS)
    rows = jnp.transpose(rows, (1, 0, 2)).reshape(-1)
    sent = pick_rows(rows, received.reshape(-1, lanes))
    got = exchange_slots(sent.reshape(groups, peers, RELAY_ROWS, lanes), 1)
    return got.reshape(groups, peers * RELAY_ROWS, lanes)


def local(integrals, quartets, density, owner_map):
    rows_dev, blocks, dens, lanes = density.shape
    devices = lax.axis_size(AXES)
    me = lax.axis_index(AXES)
    quartet_count = quartets.shape[0]
    tile_count = ROLES * quartet_count
    span = rows_dev * blocks
    most = 2 * rows_dev
    tag = 1 << (2 * tile_count - 1).bit_length()
    scale = span * tag
    device_ids = jnp.arange(devices, dtype=jnp.int32)
    tile_ids = jnp.arange(tile_count, dtype=jnp.int32)
    density_rows = jnp.transpose(density, (0, 2, 1, 3))
    swap, trade = permutation_tables(math.isqrt(lanes))

    key = tile_keys(quartets, owner_map)
    holder = key // span
    rank = jnp.sum(
        ((holder[:, None] == holder) & (tile_ids[:, None] < tile_ids)).astype(jnp.int32), axis=0
    )
    asked = jnp.sum((holder[:, None] == device_ids).astype(jnp.int32), axis=0)
    spare, spare_count = spilled(rank >= 2 * READ_SLOTS, key * tag + tile_ids, READ_SPARE)
    message = jnp.concatenate([key * 16 + rank, spare, spare_count[None], asked])
    message = jnp.pad(message, (0, -message.shape[0] % 128))
    told = exchange_slots(jnp.broadcast_to(message, (devices,) + message.shape))
    keys, ranks = told[:, :tile_count] // 16, told[:, :tile_count] % 16
    read_list = told[:, tile_count : tile_count + READ_SPARE]
    counts = told[:, tile_count + READ_SPARE + 1 :][:, :devices]
    in_second = jnp.minimum(counts, READ_SLOTS)
    in_first = jnp.minimum(counts - in_second, READ_SLOTS)
    read_middle, read_first, read_second, read_misses = route(
        told, tile_count, READ_SPARE, in_first, in_second, (READ_SLOTS, READ_SLOTS), scale, False
    )
    most_spare = jnp.max(told[:, tile_count + READ_SPARE])
    read_fits = (read_misses == 0) & (most_spare <= READ_SPARE)

    mine = keys // span == me
    local_tile = keys - me * span

    def requests(begin, slots):
        hit = mine[:, :, None] & (ranks[:, :, None] == jnp.arange(slots) + begin)
        return choose(hit, local_tile[:, :, None], 1)

    list_home = read_list // scale
    slot_ids = jnp.arange(devices * READ_SLOTS, dtype=jnp.int32)
    to_send = (read_middle >= 0) & (list_home == me)
    hit = to_send.reshape(-1, 1)
    hit = hit & ((read_middle * READ_SLOTS + read_first).reshape(-1, 1) == slot_ids)
    extra = choose(hit, (read_list // tag - me * span).reshape(-1, 1), 0)
    wanted = jnp.maximum(requests(READ_SLOTS, READ_SLOTS), extra.reshape(devices, READ_SLOTS))
    sent, sent_then = gather_tiles([wanted, requests(0, READ_SLOTS)], density_rows)
    received = exchange_slots(sent)
    first, second = regroup(integrals, swap, trade)
    received, first, second = lax.optimization_barrier((received, first, second))
    passing = (read_middle == me).reshape(-1, 1)
    passing = passing & ((device_ids[:, None] * READ_SLOTS + read_second).reshape(-1, 1) == slot_ids)
    passed = choose(passing, (list_home * READ_SLOTS + read_first).reshape(-1, 1), 0)
    passed_rows = slot_rows(passed, READ_SLOTS, dens).reshape(devices, READ_SLOTS, -1, 4)
    passed_rows = jnp.transpose(passed_rows, (0, 2, 3, 1)).reshape(-1)
    passed_on = pick_rows(
        passed_rows, received.reshape(-1, lanes), base=sent_then.reshape(-1, lanes)
    )
    received_then = exchange_slots(passed_on.reshape(sent_then.shape))
    keys, ranks, _ = lax.optimization_barrier((keys, ranks, passed_on))

    homes = keys // span
    flat = keys.reshape(-1)
    shared = jnp.sum((flat[:, None] == flat).astype(jnp.int32), axis=0) > 1
    shared = shared.reshape(keys.shape)
    together = homes[:, :, None] == homes[:, None, :]
    before = 1 + (shared[:, :, None] & (tile_ids[:, None] < tile_ids)).astype(jnp.int32)
    low_ranks = jnp.where(shared, jnp.sum(jnp.where(together, before, 0), axis=1), -1)
    at_home = homes[:, :, None] == device_ids
    low_counts = jnp.sum((at_home & shared[:, :, None]).astype(jnp.int32), axis=1)
    both_ranks = jnp.concatenate([ranks, low_ranks], axis=1)
    values = keys * tag + tile_ids
    values = jnp.concatenate([values, values + tile_count], axis=1)
    term_list, term_counts = spilled(both_ranks >= FIRST_SLOTS, values, TERM_SPARE)
    term_table = jnp.concatenate([term_list, term_counts[:, None]], axis=1)
    in_use = counts + low_counts
    term_middle, term_first, _, term_misses = route(
        term_table, 0, TERM_SPARE, in_use, jnp.zeros_like(in_use), (FIRST_SLOTS, 1), scale, True
    )
    term_fits = (term_misses == 0) & (jnp.max(term_counts) <= TERM_SPARE)

    def read_two_step():
        my_middle = lax.dynamic_index_in_dim(read_middle, me, 0, keepdims=False)
        my_place = lax.dynamic_index_in_dim(read_second, me, 0, keepdims=False)
        last = (spare[:, None] >= 0) & (spare[:, None] % tag == tile_ids)
        via = choose(last, (my_middle * READ_SLOTS + my_place)[:, None], 0)
        slot = holder * READ_SLOTS + rank
        then = jnp.where(rank < READ_SLOTS, slot, via)
        direct = (rank >= READ_SLOTS) & (rank < 2 * READ_SLOTS)
        now = jnp.where(direct, slot - READ_SLOTS, -1)
        return pick_rows(
            pad_rows(slot_rows(now, READ_SLOTS, dens)),
            received.reshape(-1, lanes),
            swap,
            pad_rows(slot_rows(then, READ_SLOTS, dens)),
            received_then.reshape(-1, lanes),
        )

    def read_one_step():
        slots = slot_count(most)
        (whole,) = gather_tiles([requests(0, slots)], density_rows)
        rows = pad_rows(slot_rows(holder * slots + rank, slots, dens))
        return pick_rows(rows, exchange_slots(whole).reshape(-1, lanes), swap)

    tiles = lax.cond(read_fits, read_two_step, read_one_step)
    tiles = tiles.reshape(ROLES, quartet_count, PAD_N, lanes)
    high, low = contract(tiles, integrals, first, second)
    high = high.reshape(tile_count * PAD_N, lanes)
    low = low.reshape(tile_count * PAD_N, lanes)

    def send(term_of_slot, slots):
        per = rows_per_group(slots)
        ids = jnp.arange(dens, dtype=jnp.int32).reshape(1, dens // per, per, 1)
        term = term_of_slot[:, None, None, :]
        rows = jnp.where(term >= 0, term * PAD_N + ids, -1).reshape(-1)
        packed = pack_terms(rows, swap, high, low)
        return exchange_slots(packed.reshape(devices, dens // per, per * slots, lanes))

    to_holder = holder[:, None] == device_ids
    place_ids = jnp.arange(FIRST_SLOTS, dtype=jnp.int32)
    my_low = lax.dynamic_index_in_dim(low_ranks, me, 0, keepdims=False)
    my_list = lax.dynamic_index_in_dim(term_list, me, 0, keepdims=False)
    routes = jnp.where(term_middle >= 0, term_middle * FIRST_SLOTS + term_first, -1)
    my_routes = lax.dynamic_index_in_dim(routes, me, 0, keepdims=False)
    ends = jnp.concatenate([to_holder, to_holder])[:, :, None]
    places = jnp.concatenate([rank, my_low])[:, None, None] == place_ids
    both_ids = jnp.arange(2 * tile_count, dtype=jnp.int32)
    term_of_slot = choose(ends & places, both_ids[:, None, None], 0)
    slot_ids = jnp.arange(devices * FIRST_SLOTS, dtype=jnp.int32)
    extra = choose(my_routes[:, None] == slot_ids, (my_list % tag)[:, None], 0)
    arrived = send(jnp.maximum(term_of_slot, extra.reshape(devices, FIRST_SLOTS)), FIRST_SLOTS)
    middle = term_middle.reshape(-1, 1)
    term_home = (term_list // scale).reshape(-1, 1)
    came = (device_ids[:, None] * FIRST_SLOTS + term_first).reshape(-1, 1)
    passed = choose((middle == me) & (term_home == device_ids), came, 0)
    relayed = hand_on(passed, arrived, dens)

    def write_two_step():
        hit = (ranks[:, :, None] == place_ids) | (low_ranks[:, :, None] == place_ids)
        landing = choose(mine[:, :, None] & hit, local_tile[:, :, None], 1)
        last = (term_list // tag - me * span).reshape(-1, 1)
        last = choose((term_home == me) & (middle == device_ids), last, 0)
        return scatter_terms(landing, arrived, rows_dev, blocks, last, relayed)

    def write_one_step():
        slots = slot_count(most)
        wide = slot_count(2 * slots)
        places = rank[:, None, None] == jnp.arange(slots)
        term_of_slot = choose(to_holder[:, :, None] & places, tile_ids[:, None, None], 0)
        none = jnp.full((devices, wide // 2 - slots), -1, jnp.int32)
        low_term = jnp.where(term_of_slot >= 0, term_of_slot + tile_count, -1)
        whole = send(jnp.concatenate([term_of_slot, none, low_term, none], axis=1), wide)
        wanted = requests(0, slots)
        landing = jnp.concatenate([wanted, none, wanted, none], axis=1)
        return scatter_terms(landing, whole, rows_dev, blocks)

    fock = lax.cond(term_fits, write_two_step, write_one_step)
    return jnp.transpose(fock, (0, 2, 1, 3))


def solution(mesh):
    return jax.shard_map(
        local,
        mesh=mesh,
        in_specs=(
            P(AXES, None, None),
            P(AXES, None),
            P(AXES, None, None, None),
            P(),
        ),
        out_specs=P(AXES, None, None, None),
        check_vma=False,
    )
```

```python
import functools
import math

import jax
import jax.numpy as jnp
from jax import lax
from jax.experimental import pallas as pl
from jax.experimental.pallas import tpu as pltpu
from jax.sharding import PartitionSpec as P

ORDER = (0, 1, 4, 2, 3, 5)
ROLE_ROW = tuple((0, 0, 1, 1, 2, 3)[role] for role in ORDER)
ROLE_COL = tuple((1, 2, 2, 3, 3, 0)[role] for role in ORDER)
ROLES = 6
PAD_N = 16
ROWS = 16
AXES = ("bra", "ket")
BF16 = jnp.bfloat16
F32 = jnp.float32
VMEM_BYTES = 60 * 1024 * 1024
READ_SLOTS = 2
FIRST_SLOTS = 4
RELAY_ROWS = 4
READ_SPARE = 8
TERM_SPARE = 16


def params(axes=1):
    return pltpu.CompilerParams(
        dimension_semantics=("arbitrary",) * axes, vmem_limit_bytes=VMEM_BYTES
    )


def cost(flops, moved):
    return pl.CostEstimate(flops=int(flops), bytes_accessed=int(moved), transcendentals=0)


def hot_rows(target, width, base=0):
    columns = lax.broadcasted_iota(jnp.int32, (target.shape[0], width), 1) + base
    return jnp.where(columns == target, 1.0, 0.0).astype(BF16)


def hot_columns(target, height, base=0):
    rows = lax.broadcasted_iota(jnp.int32, (height, target.shape[1]), 0) + base
    return jnp.where(rows == target, 1.0, 0.0).astype(BF16)


def dot_nn(left, right):
    return jnp.dot(left, right, preferred_element_type=F32)


def dot_nt(left, right):
    return lax.dot_general(left, right, (((1,), (1,)), ((), ())), preferred_element_type=F32)


def rows_per_group(slots):
    return min(4, ROWS // slots)


def tile_rows(tiles, per, blocks):
    inner = jnp.arange(per, dtype=jnp.int32)[None, :, None]
    rows = (tiles // blocks * (per * blocks) + tiles % blocks)[:, None, :] + inner * blocks
    return jnp.where(tiles[:, None, :] >= 0, rows, -1)


def slot_rows(slot, slots, dens):
    ids = jnp.arange(dens, dtype=jnp.int32)
    per = rows_per_group(slots)
    rows = (slot // slots * (dens * slots) + slot % slots)[..., None]
    rows = rows + ids // per * (per * slots) + ids % per * slots
    return jnp.where(slot[..., None] >= 0, rows, -1)


def pad_rows(rows):
    pad = [(0, 0)] * (rows.ndim - 1) + [(0, PAD_N - rows.shape[-1])]
    return jnp.pad(rows, pad, constant_values=-1).reshape(-1)


def gather_body(target_ref, density_ref, *refs):
    *out_refs, hot_ref = refs
    peers, _, rows, lanes = out_refs[0].shape
    depth = hot_ref.shape[1]

    @pl.when(pl.program_id(0) == 0)
    def _():
        hot_ref[...] = hot_rows(target_ref[...], depth)

    source = density_ref[...].reshape(depth, lanes)
    half = lanes // 2
    for part in range(2):
        span = slice(part * half, (part + 1) * half)
        picked = dot_nn(hot_ref[...], source[:, span]).reshape(-1, rows, half)
        for which, out_ref in enumerate(out_refs):
            mine = picked[which * peers : (which + 1) * peers]
            out_ref[:, 0, :, span] = mine.astype(BF16)


def gather_tiles(wanted, density_rows):
    peers, slots = wanted[0].shape
    rows_dev, dens, blocks, lanes = density_rows.shape
    per = rows_per_group(slots)
    groups, rows = dens // per, per * slots
    depth = rows_dev * per * blocks
    target = jnp.concatenate([tile_rows(each, per, blocks).reshape(-1, 1) for each in wanted])
    out = jax.ShapeDtypeStruct((peers, groups, rows, lanes), BF16)
    return pl.pallas_call(
        gather_body,
        grid=(groups,),
        in_specs=[
            pl.BlockSpec(target.shape, lambda g: (0, 0)),
            pl.BlockSpec((rows_dev, per, blocks, lanes), lambda g: (0, g, 0, 0)),
        ],
        out_specs=[pl.BlockSpec((peers, 1, rows, lanes), lambda g: (0, g, 0, 0))] * len(wanted),
        out_shape=[out] * len(wanted),
        scratch_shapes=[pltpu.VMEM((target.shape[0], depth), BF16)],
        compiler_params=params(),
        name="gather_tiles",
    )(target, density_rows)


def pick_body(*refs, relay, swapped, based):
    if relay:
        relay_target_ref, relayed_ref, *refs = refs
    if based:
        base_ref, *refs = refs
    if swapped:
        swap_ref, *refs = refs
    target_ref, slots_ref, out_ref, total_ref = refs
    step = pl.program_id(0)
    depth = slots_ref.shape[0]

    @pl.when(step == 0)
    def _():
        if relay:
            hot = hot_rows(relay_target_ref[...], relayed_ref.shape[0])
            total_ref[...] = dot_nn(hot, relayed_ref[...])
        elif based:
            total_ref[...] = base_ref[...].astype(F32)
        else:
            total_ref[...] = jnp.zeros_like(total_ref)

    total_ref[...] += dot_nn(hot_rows(target_ref[...], depth, step * depth), slots_ref[...])

    @pl.when(step == pl.num_programs(0) - 1)
    def _():
        if not swapped:
            out_ref[...] = total_ref[...].astype(BF16)
            return
        half = out_ref.shape[0] // 2
        out_ref[:half, :] = total_ref[:half, :].astype(BF16)
        tiles = total_ref[half:, :].astype(BF16)
        out_ref[half:, :] = dot_nn(tiles, swap_ref[...]).astype(BF16)


def pick_rows(row_of, received, swap=None, relay_row_of=None, relayed=None, base=None):
    depth, lanes = received.shape
    chunk = math.gcd(depth, 1024) if depth % 1024 == 0 else math.gcd(depth, 512)
    wanted = row_of.shape[0]
    column = pl.BlockSpec((wanted, 1), lambda k: (0, 0))
    specs, operands = [], []
    if relayed is not None:
        specs += [column, pl.BlockSpec(relayed.shape, lambda k: (0, 0))]
        operands += [relay_row_of.reshape(wanted, 1), relayed]
    if base is not None:
        specs += [pl.BlockSpec(base.shape, lambda k: (0, 0))]
        operands += [base]
    if swap is not None:
        specs += [pl.BlockSpec(swap.shape, lambda k: (0, 0))]
        operands += [swap]
    return pl.pallas_call(
        functools.partial(
            pick_body,
            relay=relayed is not None,
            swapped=swap is not None,
            based=base is not None,
        ),
        grid=(depth // chunk,),
        in_specs=[*specs, column, pl.BlockSpec((chunk, lanes), lambda k: (k, 0))],
        out_specs=pl.BlockSpec((wanted, lanes), lambda k: (0, 0)),
        out_shape=jax.ShapeDtypeStruct((wanted, lanes), BF16),
        scratch_shapes=[pltpu.VMEM((wanted, lanes), F32)],
        compiler_params=params(),
        name="pick_rows",
    )(*operands, row_of.reshape(wanted, 1), received)


def exchange(source_ref, trade, out_ref, width):
    low = 128 // width
    high = width // low

    def one(block, carry):
        piece = source_ref[:, pl.ds(pl.multiple_of(block * 128, 128), 128)]
        piece = piece.reshape(high, low, width, 128)
        wide = jnp.concatenate(
            [piece[:, part].reshape(high * width, 128) for part in range(low)], axis=1
        )
        traded = dot_nn(wide, trade).astype(BF16)
        for part in range(low):
            group = traded[:, part * 128 : (part + 1) * 128].reshape(high, width, 128)
            row = pl.multiple_of((block * low + part) * width, width)
            for lead in range(high):
                out_ref[pl.ds(row, width), lead * 128 : (lead + 1) * 128] = group[lead]
        return carry

    lax.fori_loop(0, width * width // 128, one, 0, unroll=2)


def regroup_body(swap_ref, trade_ref, block_ref, *refs, width):
    first_ref, second_ref, swapped_ref = refs[-3:]
    lanes = width * width
    half = lanes // 2
    for part in range(2):
        span = slice(part * half, (part + 1) * half)
        swapped_ref[:, span] = dot_nn(block_ref[0], swap_ref[:, span]).astype(BF16)
    exchange(swapped_ref, trade_ref[...], first_ref.at[0], width)
    exchange(block_ref.at[0], trade_ref[...], second_ref.at[0], width)


def regroup(integrals, swap, trade, begin, end, into=(), work=1):
    count, lanes, _ = integrals.shape
    width = math.isqrt(lanes)
    whole = pl.BlockSpec((1, lanes, lanes), lambda i: (i + begin, 0, 0))
    out = jax.ShapeDtypeStruct(integrals.shape, BF16)
    return pl.pallas_call(
        functools.partial(regroup_body, width=width),
        grid=(end - begin,),
        in_specs=[
            pl.BlockSpec(swap.shape, lambda i: (0, 0)),
            pl.BlockSpec(trade.shape, lambda i: (0, 0)),
            whole,
            *[pl.BlockSpec(memory_space=pl.ANY)] * len(into),
        ],
        out_specs=[whole, whole],
        out_shape=[out, out],
        scratch_shapes=[pltpu.VMEM((lanes, lanes), BF16)],
        input_output_aliases={3 + which: which for which in range(len(into))},
        compiler_params=params(),
        cost_estimate=cost(work, work),
        name="regroup",
    )(swap, trade, integrals, *into)


def contract_body(tiles_ref, block_ref, first_ref, second_ref, high_ref, low_ref):
    block, first, second = block_ref[0], first_ref[0], second_ref[0]

    def tile(role):
        return tiles_ref[ORDER.index(role), 0]

    def put(role, term):
        top = term.astype(BF16)
        role = ORDER.index(role)
        high_ref[role, 0] = top
        low_ref[role, 0] = (term - top.astype(F32)).astype(BF16)

    put(0, 2.0 * dot_nt(tile(4), block))
    put(4, 2.0 * dot_nn(tile(0), block))
    put(1, -dot_nn(tile(3), first))
    put(3, -dot_nt(tile(1), first))
    put(2, -dot_nt(tile(5), second))
    put(5, -dot_nn(tile(2), second))


def contract(tiles, integrals, first, second):
    count, lanes, _ = integrals.shape
    whole = pl.BlockSpec((1, lanes, lanes), lambda i: (i, 0, 0))
    part = pl.BlockSpec((ROLES, 1, PAD_N, lanes), lambda i: (0, i, 0, 0))
    out = jax.ShapeDtypeStruct((ROLES, count, PAD_N, lanes), BF16)
    return pl.pallas_call(
        contract_body,
        grid=(count,),
        in_specs=[part, whole, whole, whole],
        out_specs=[part, part],
        out_shape=[out, out],
        compiler_params=params(),
        name="contract",
    )(tiles, integrals, first, second)


def pack_body(target_ref, swap_ref, high_ref, low_ref, out_ref, terms_ref):
    half = high_ref.shape[0]

    @pl.when(pl.program_id(0) == 0)
    def _():
        mid = half // 2
        for which, source in enumerate((high_ref, low_ref)):
            start = which * half
            terms_ref[start : start + mid, :] = source[:mid, :]
            swapped = dot_nn(source[mid:, :], swap_ref[...]).astype(BF16)
            terms_ref[start + mid : start + half, :] = swapped

    out_ref[...] = dot_nn(hot_rows(target_ref[...], 2 * half), terms_ref[...]).astype(BF16)


def pack_terms(row_of, swap, high, low):
    count = row_of.shape[0]
    half, lanes = high.shape
    chunk = math.gcd(count, 512)
    return pl.pallas_call(
        pack_body,
        grid=(count // chunk,),
        in_specs=[
            pl.BlockSpec((chunk, 1), lambda k: (k, 0)),
            pl.BlockSpec((lanes, lanes), lambda k: (0, 0)),
            pl.BlockSpec((half, lanes), lambda k: (0, 0)),
            pl.BlockSpec((half, lanes), lambda k: (0, 0)),
        ],
        out_specs=pl.BlockSpec((chunk, lanes), lambda k: (k, 0)),
        out_shape=jax.ShapeDtypeStruct((count, lanes), BF16),
        scratch_shapes=[pltpu.VMEM((2 * half, lanes), BF16)],
        compiler_params=params(),
        name="pack_terms",
    )(row_of.reshape(count, 1), swap, high, low)


def scatter_body(*refs, relay):
    if relay:
        relay_target_ref, relayed_ref, *refs, relay_hot_ref = refs
    target_ref, slots_ref, out_ref, hot_ref = refs
    rows_dev, per, blocks, lanes = out_ref.shape
    height = per * blocks
    depth = hot_ref.shape[1]

    @pl.when(pl.program_id(0) == 0)
    def _():
        hot_ref[...] = hot_columns(target_ref[...], rows_dev * height)
        if relay:
            for part in range(relay_hot_ref.shape[0]):
                target = relay_target_ref[part : part + 1, :]
                relay_hot_ref[part] = hot_columns(target, rows_dev * height)

    slots = slots_ref[...].reshape(depth, lanes)
    for row in range(rows_dev):
        span = slice(row * height, (row + 1) * height)
        total = dot_nn(hot_ref[span, :], slots)
        if relay:
            part = pl.program_id(0) % relay_hot_ref.shape[0]
            total += dot_nn(relay_hot_ref[part, span, :], relayed_ref[0])
        out_ref[row] = total.astype(BF16).reshape(per, blocks, lanes)


def scatter_split(slots):
    return max(slots, 8)


def landing_rows(landing, blocks):
    slots = landing.shape[1]
    return tile_rows(landing, scatter_split(slots) // slots, blocks).reshape(1, -1)


def relay_landing_rows(landing, slots, blocks):
    per = scatter_split(slots) // slots
    inner = jnp.arange(RELAY_ROWS, dtype=jnp.int32)
    rows = (landing // blocks * (per * blocks) + landing % blocks)[:, None] + inner % per * blocks
    kind = jnp.arange(RELAY_ROWS // per, dtype=jnp.int32)[:, None, None]
    rows = jnp.where((landing[:, None] >= 0) & (inner // per == kind), rows, -1)
    return rows.reshape(kind.shape[0], -1)


def scatter_terms(target, arrived, slots, rows_dev, blocks, relay_target=None, relayed=None):
    peers, groups, rows, lanes = arrived.shape
    split = scatter_split(slots)
    steps, per = groups * rows // split, split // slots
    high = rows_dev * per * blocks
    specs, operands = [], []
    scratch = [pltpu.VMEM((high, peers * split), BF16)]
    if relayed is not None:
        depth = relayed.shape[1]
        kinds = relay_target.shape[0]
        specs = [
            pl.BlockSpec((kinds, depth), lambda g: (0, 0)),
            pl.BlockSpec((1, depth, lanes), lambda g: (g // kinds, 0, 0)),
        ]
        operands = [relay_target, relayed]
        scratch += [pltpu.VMEM((kinds, high, depth), BF16)]
    return pl.pallas_call(
        functools.partial(scatter_body, relay=relayed is not None),
        grid=(steps,),
        in_specs=[
            *specs,
            pl.BlockSpec((1, peers * split), lambda g: (0, 0)),
            pl.BlockSpec((peers, 1, split, lanes), lambda g: (0, g, 0, 0)),
        ],
        out_specs=pl.BlockSpec((rows_dev, per, blocks, lanes), lambda g: (0, g, 0, 0)),
        out_shape=jax.ShapeDtypeStruct((rows_dev, steps * per, blocks, lanes), BF16),
        scratch_shapes=scratch,
        compiler_params=params(),
        name="scatter_terms",
    )(*operands, target, arrived.reshape(peers, steps, split, lanes))


def route_body(list_ref, state_hbm, out_ref, state_ref, sem, *, spare, begin, scale, caps, outward):
    peers = list_ref.shape[0]
    second = peers * peers
    copy = pltpu.make_async_copy(state_hbm, state_ref, sem)
    copy.start()
    copy.wait()

    def first_at(source, middle):
        return source * peers + middle if outward else middle * peers + source

    def one(row, place, failed):
        other = list_ref[row, begin + place] // scale
        source, last = (row, other) if outward else (other, row)

        def search(carry):
            tries, middle, found = carry
            full = state_ref[first_at(source, middle)] >= caps[0]
            taken = state_ref[second + last * peers + middle] >= caps[1]
            found = jnp.where(full | taken, found, middle)
            following = jnp.where(middle + 1 == peers, 0, middle + 1)
            return tries + 1, following, found

        start = source + last
        start = jnp.where(start >= peers, start - peers, start)
        _, _, found = lax.while_loop(
            lambda carry: (carry[0] < peers) & (carry[2] < 0),
            search,
            (jnp.int32(0), start, jnp.int32(-1)),
        )
        index = row * spare + place
        out_ref[index] = -1

        @pl.when(found >= 0)
        def _():
            first, then = first_at(source, found), second + last * peers + found
            out_ref[index] = found * 64 + state_ref[first] * 8 + state_ref[then]
            state_ref[first] = state_ref[first] + 1
            state_ref[then] = state_ref[then] + 1

        return failed + jnp.where(found < 0, 1, 0)

    def each(row, failed):
        count = jnp.minimum(list_ref[row, begin + spare], spare)
        return lax.fori_loop(0, count, functools.partial(lambda p, f, r: one(r, p, f), r=row), failed)

    out_ref[peers * spare] = lax.fori_loop(0, peers, each, jnp.int32(0))


def route(table, begin, spare, first, second, caps, scale, outward):
    peers = table.shape[0]
    state = jnp.concatenate([first, second]).reshape(-1)
    smem = pl.BlockSpec(memory_space=pltpu.SMEM)
    out = pl.pallas_call(
        functools.partial(
            route_body, spare=spare, begin=begin, scale=scale, caps=caps, outward=outward
        ),
        in_specs=[smem, pl.BlockSpec(memory_space=pl.ANY)],
        out_specs=smem,
        out_shape=jax.ShapeDtypeStruct((peers * spare + 1,), jnp.int32),
        scratch_shapes=[pltpu.SMEM((2 * peers * peers,), jnp.int32), pltpu.SemaphoreType.DMA],
        name="route",
    )(table, state)
    routes = out[:-1].reshape(peers, spare)
    listed = (table[:, begin : begin + spare] >= 0) & (routes >= 0)
    routes = jnp.where(listed, routes, -1)
    middles = jnp.where(listed, routes // 64, -1)
    return middles, routes // 8 % 8, routes % 8, out[-1]


def tile_keys(quartets, owner_map):
    blocks = owner_map.shape[0]
    row_blocks = jnp.stack([quartets[:, pick] for pick in ROLE_ROW]).reshape(-1)
    col_blocks = jnp.stack([quartets[:, pick] for pick in ROLE_COL]).reshape(-1)
    ids = jnp.arange(blocks, dtype=jnp.int32)
    storage = jnp.sum(jnp.where(row_blocks[:, None] == ids, owner_map, 0), axis=-1)
    return storage * blocks + col_blocks


def earlier(flags):
    ids = jnp.arange(flags.shape[-1])
    ahead = ids[:, None] < ids[None, :]
    return jnp.sum((flags[..., :, None] & ahead).astype(jnp.int32), axis=-2)


def choose(hit, values, axis):
    return jnp.sum(jnp.where(hit, values + 1, 0), axis=axis) - 1


def spilled(flags, values, spare):
    place = earlier(flags)
    hit = flags[..., None] & (place[..., None] == jnp.arange(spare))
    return choose(hit, values[..., None], -2), jnp.sum(flags.astype(jnp.int32), axis=-1)


def permutation_tables(width):
    lanes = width * width
    low = 128 // width
    index = jnp.arange(lanes, dtype=jnp.int32)
    partner = index % width * width + index // width
    swap = (index[:, None] == partner[None, :]).astype(BF16)
    span = jnp.arange(low * 128, dtype=jnp.int32)
    lead, group, inner = span // 128, span % 128 // width, span % width
    partner = group * 128 + lead * width + inner
    trade = (span[None, :] == partner[:, None]).astype(BF16)
    return swap, trade


def slot_count(most):
    for slots in (4, 8, 16):
        if most <= slots:
            return slots
    raise ValueError(most)


def exchange_slots(array):
    return lax.all_to_all(array, AXES, split_axis=0, concat_axis=0, tiled=True)


def slot_count(most):
    for slots in (4, 8, 16):
        if most <= slots:
            return slots
    raise ValueError(most)


def exchange_slots(array, axis=0):
    return lax.all_to_all(array, AXES, split_axis=axis, concat_axis=axis, tiled=True)


def hand_on(slot_of, received, dens):
    peers = slot_of.shape[0]
    lanes = received.shape[-1]
    groups = dens // RELAY_ROWS
    rows = slot_rows(slot_of, FIRST_SLOTS, dens).reshape(peers, groups, RELAY_ROWS)
    rows = jnp.transpose(rows, (1, 0, 2)).reshape(-1)
    sent = pick_rows(rows, received.reshape(-1, lanes))
    got = exchange_slots(sent.reshape(groups, peers, RELAY_ROWS, lanes), 1)
    return got.reshape(groups, peers * RELAY_ROWS, lanes)


def local(integrals, quartets, density, owner_map):
    rows_dev, blocks, dens, lanes = density.shape
    devices = lax.axis_size(AXES)
    me = lax.axis_index(AXES)
    quartet_count = quartets.shape[0]
    tile_count = ROLES * quartet_count
    span = rows_dev * blocks
    most = 2 * rows_dev
    tag = 1 << (2 * tile_count - 1).bit_length()
    scale = span * tag
    device_ids = jnp.arange(devices, dtype=jnp.int32)
    tile_ids = jnp.arange(tile_count, dtype=jnp.int32)
    density_rows = jnp.transpose(density, (0, 2, 1, 3))
    swap, trade = permutation_tables(math.isqrt(lanes))

    key = tile_keys(quartets, owner_map)
    holder = key // span
    rank = jnp.sum(
        ((holder[:, None] == holder) & (tile_ids[:, None] < tile_ids)).astype(jnp.int32), axis=0
    )
    asked = jnp.sum((holder[:, None] == device_ids).astype(jnp.int32), axis=0)
    spare, spare_count = spilled(rank >= 2 * READ_SLOTS, key * tag + tile_ids, READ_SPARE)
    message = jnp.concatenate([key * 16 + rank, spare, spare_count[None], asked])
    message = jnp.pad(message, (0, -message.shape[0] % 128))
    told = exchange_slots(jnp.broadcast_to(message, (devices,) + message.shape))
    keys, ranks = told[:, :tile_count] // 16, told[:, :tile_count] % 16
    read_list = told[:, tile_count : tile_count + READ_SPARE]
    counts = told[:, tile_count + READ_SPARE + 1 :][:, :devices]
    in_second = jnp.minimum(counts, READ_SLOTS)
    in_first = jnp.minimum(counts - in_second, READ_SLOTS)
    read_middle, read_first, read_second, read_misses = route(
        told, tile_count, READ_SPARE, in_first, in_second, (READ_SLOTS, READ_SLOTS), scale, False
    )
    most_spare = jnp.max(told[:, tile_count + READ_SPARE])
    read_fits = (read_misses == 0) & (most_spare <= READ_SPARE)

    mine = keys // span == me
    local_tile = keys - me * span

    def requests(begin, slots):
        hit = mine[:, :, None] & (ranks[:, :, None] == jnp.arange(slots) + begin)
        return choose(hit, local_tile[:, :, None], 1)

    list_home = read_list // scale
    slot_ids = jnp.arange(devices * READ_SLOTS, dtype=jnp.int32)
    to_send = (read_middle >= 0) & (list_home == me)
    hit = to_send.reshape(-1, 1)
    hit = hit & ((read_middle * READ_SLOTS + read_first).reshape(-1, 1) == slot_ids)
    extra = choose(hit, (read_list // tag - me * span).reshape(-1, 1), 0)
    wanted = jnp.maximum(requests(READ_SLOTS, READ_SLOTS), extra.reshape(devices, READ_SLOTS))
    sent, sent_then = gather_tiles([wanted, requests(0, READ_SLOTS)], density_rows)
    received = exchange_slots(sent)
    early = quartet_count * 5 // 8
    work = 2 * lanes**3 * early
    first, second = regroup(integrals, swap, trade, 0, early, work=work)
    received, first, second = lax.optimization_barrier((received, first, second))
    passing = (read_middle == me).reshape(-1, 1)
    passing = passing & ((device_ids[:, None] * READ_SLOTS + read_second).reshape(-1, 1) == slot_ids)
    passed = choose(passing, (list_home * READ_SLOTS + read_first).reshape(-1, 1), 0)
    passed_rows = slot_rows(passed, READ_SLOTS, dens).reshape(devices, READ_SLOTS, -1, 4)
    passed_rows = jnp.transpose(passed_rows, (0, 2, 3, 1)).reshape(-1)
    passed_on = pick_rows(
        passed_rows, received.reshape(-1, lanes), base=sent_then.reshape(-1, lanes)
    )
    received_then = exchange_slots(passed_on.reshape(sent_then.shape))
    keys, ranks, first, second, _ = lax.optimization_barrier((keys, ranks, first, second, passed_on))
    first, second = regroup(integrals, swap, trade, early, quartet_count, (first, second))

    homes = keys // span
    flat = keys.reshape(-1)
    shared = jnp.sum((flat[:, None] == flat).astype(jnp.int32), axis=0) > 1
    shared = shared.reshape(keys.shape)
    together = homes[:, :, None] == homes[:, None, :]
    before = 1 + (shared[:, :, None] & (tile_ids[:, None] < tile_ids)).astype(jnp.int32)
    low_ranks = jnp.where(shared, jnp.sum(jnp.where(together, before, 0), axis=1), -1)
    at_home = homes[:, :, None] == device_ids
    low_counts = jnp.sum((at_home & shared[:, :, None]).astype(jnp.int32), axis=1)
    both_ranks = jnp.concatenate([ranks, low_ranks], axis=1)
    values = keys * tag + tile_ids
    values = jnp.concatenate([values, values + tile_count], axis=1)
    term_list, term_counts = spilled(both_ranks >= FIRST_SLOTS, values, TERM_SPARE)
    term_table = jnp.concatenate([term_list, term_counts[:, None]], axis=1)
    in_use = counts + low_counts
    term_middle, term_first, _, term_misses = route(
        term_table, 0, TERM_SPARE, in_use, jnp.zeros_like(in_use), (FIRST_SLOTS, 1), scale, True
    )
    term_fits = (term_misses == 0) & (jnp.max(term_counts) <= TERM_SPARE)

    my_middle = lax.dynamic_index_in_dim(read_middle, me, 0, keepdims=False)
    my_place = lax.dynamic_index_in_dim(read_second, me, 0, keepdims=False)
    last = (spare[:, None] >= 0) & (spare[:, None] % tag == tile_ids)
    via = choose(last, (my_middle * READ_SLOTS + my_place)[:, None], 0)
    slot = holder * READ_SLOTS + rank
    then_slot = jnp.where(rank < READ_SLOTS, slot, via)
    direct = (rank >= READ_SLOTS) & (rank < 2 * READ_SLOTS)
    now_slot = jnp.where(direct, slot - READ_SLOTS, -1)
    now_rows = pad_rows(slot_rows(now_slot, READ_SLOTS, dens)).reshape(-1, 1)
    then_rows = pad_rows(slot_rows(then_slot, READ_SLOTS, dens)).reshape(-1, 1)
    now_rows, then_rows = lax.optimization_barrier((now_rows, then_rows))

    def read_two_step():
        return pick_rows(
            now_rows,
            received.reshape(-1, lanes),
            swap,
            then_rows,
            received_then.reshape(-1, lanes),
        )

    def read_one_step():
        slots = slot_count(most)
        (whole,) = gather_tiles([requests(0, slots)], density_rows)
        rows = pad_rows(slot_rows(holder * slots + rank, slots, dens))
        return pick_rows(rows, exchange_slots(whole).reshape(-1, lanes), swap)

    tiles = lax.cond(read_fits, read_two_step, read_one_step)
    tiles = tiles.reshape(ROLES, quartet_count, PAD_N, lanes)
    high, low = contract(tiles, integrals, first, second)
    high = high.reshape(tile_count * PAD_N, lanes)
    low = low.reshape(tile_count * PAD_N, lanes)

    def send(term_of_slot, slots):
        per = rows_per_group(slots)
        ids = jnp.arange(dens, dtype=jnp.int32).reshape(1, dens // per, per, 1)
        term = term_of_slot[:, None, None, :]
        rows = jnp.where(term >= 0, term * PAD_N + ids, -1).reshape(-1)
        packed = pack_terms(rows, swap, high, low)
        return exchange_slots(packed.reshape(devices, dens // per, per * slots, lanes))

    to_holder = holder[:, None] == device_ids
    place_ids = jnp.arange(FIRST_SLOTS, dtype=jnp.int32)
    my_low = lax.dynamic_index_in_dim(low_ranks, me, 0, keepdims=False)
    my_list = lax.dynamic_index_in_dim(term_list, me, 0, keepdims=False)
    routes = jnp.where(term_middle >= 0, term_middle * FIRST_SLOTS + term_first, -1)
    my_routes = lax.dynamic_index_in_dim(routes, me, 0, keepdims=False)
    ends = jnp.concatenate([to_holder, to_holder])[:, :, None]
    places = jnp.concatenate([rank, my_low])[:, None, None] == place_ids
    both_ids = jnp.arange(2 * tile_count, dtype=jnp.int32)
    term_of_slot = choose(ends & places, both_ids[:, None, None], 0)
    slot_ids = jnp.arange(devices * FIRST_SLOTS, dtype=jnp.int32)
    extra = choose(my_routes[:, None] == slot_ids, (my_list % tag)[:, None], 0)
    arrived = send(jnp.maximum(term_of_slot, extra.reshape(devices, FIRST_SLOTS)), FIRST_SLOTS)
    middle = term_middle.reshape(-1, 1)
    term_home = (term_list // scale).reshape(-1, 1)
    came = (device_ids[:, None] * FIRST_SLOTS + term_first).reshape(-1, 1)
    passed = choose((middle == me) & (term_home == device_ids), came, 0)
    relayed = hand_on(passed, arrived, dens)

    hit = (ranks[:, :, None] == place_ids) | (low_ranks[:, :, None] == place_ids)
    landing = landing_rows(choose(mine[:, :, None] & hit, local_tile[:, :, None], 1), blocks)
    last = (term_list // tag - me * span).reshape(-1, 1)
    last = choose((term_home == me) & (middle == device_ids), last, 0)
    relay_landing = relay_landing_rows(last, FIRST_SLOTS, blocks)
    landing, relay_landing = lax.optimization_barrier((landing, relay_landing))

    def write_two_step():
        return scatter_terms(
            landing, arrived, FIRST_SLOTS, rows_dev, blocks, relay_landing, relayed
        )

    def write_one_step():
        slots = slot_count(most)
        wide = slot_count(2 * slots)
        places = rank[:, None, None] == jnp.arange(slots)
        term_of_slot = choose(to_holder[:, :, None] & places, tile_ids[:, None, None], 0)
        none = jnp.full((devices, wide // 2 - slots), -1, jnp.int32)
        low_term = jnp.where(term_of_slot >= 0, term_of_slot + tile_count, -1)
        whole = send(jnp.concatenate([term_of_slot, none, low_term, none], axis=1), wide)
        wanted = requests(0, slots)
        landing = jnp.concatenate([wanted, none, wanted, none], axis=1)
        return scatter_terms(landing_rows(landing, blocks), whole, wide, rows_dev, blocks)

    fock = lax.cond(term_fits, write_two_step, write_one_step)
    return jnp.transpose(fock, (0, 2, 1, 3))


def solution(mesh):
    return jax.shard_map(
        local,
        mesh=mesh,
        in_specs=(
            P(AXES, None, None),
            P(AXES, None),
            P(AXES, None, None, None),
            P(),
        ),
        out_specs=P(AXES, None, None, None),
        check_vma=False,
    )
```

```python
import functools
import math

import jax
import jax.numpy as jnp
from jax import lax
from jax.experimental import pallas as pl
from jax.experimental.pallas import tpu as pltpu
from jax.sharding import PartitionSpec as P

ORDER = (0, 1, 4, 2, 3, 5)
ROLE_ROW = tuple((0, 0, 1, 1, 2, 3)[role] for role in ORDER)
ROLE_COL = tuple((1, 2, 2, 3, 3, 0)[role] for role in ORDER)
ROLES = 6
PAD_N = 16
ROWS = 16
AXES = ("bra", "ket")
BF16 = jnp.bfloat16
F32 = jnp.float32
VMEM_BYTES = 60 * 1024 * 1024
READ_SLOTS = 2
FIRST_SLOTS = 4
RELAY_ROWS = 4
READ_SPARE = 8
TERM_SPARE = 16


def params(axes=1):
    return pltpu.CompilerParams(
        dimension_semantics=("arbitrary",) * axes, vmem_limit_bytes=VMEM_BYTES
    )


def cost(flops, moved):
    return pl.CostEstimate(flops=int(flops), bytes_accessed=int(moved), transcendentals=0)


def hot_rows(target, width, base=0):
    columns = lax.broadcasted_iota(jnp.int32, (target.shape[0], width), 1) + base
    return jnp.where(columns == target, 1.0, 0.0).astype(BF16)


def hot_columns(target, height, base=0):
    rows = lax.broadcasted_iota(jnp.int32, (height, target.shape[1]), 0) + base
    return jnp.where(rows == target, 1.0, 0.0).astype(BF16)


def dot_nn(left, right):
    return jnp.dot(left, right, preferred_element_type=F32)


def dot_nt(left, right):
    return lax.dot_general(left, right, (((1,), (1,)), ((), ())), preferred_element_type=F32)


def rows_per_group(slots):
    return min(4, ROWS // slots)


def tile_rows(tiles, per, blocks):
    inner = jnp.arange(per, dtype=jnp.int32)[None, :, None]
    rows = (tiles // blocks * (per * blocks) + tiles % blocks)[:, None, :] + inner * blocks
    return jnp.where(tiles[:, None, :] >= 0, rows, -1)


def slot_rows(slot, slots, dens):
    ids = jnp.arange(dens, dtype=jnp.int32)
    per = rows_per_group(slots)
    rows = (slot // slots * (dens * slots) + slot % slots)[..., None]
    rows = rows + ids // per * (per * slots) + ids % per * slots
    return jnp.where(slot[..., None] >= 0, rows, -1)


def pad_rows(rows):
    pad = [(0, 0)] * (rows.ndim - 1) + [(0, PAD_N - rows.shape[-1])]
    return jnp.pad(rows, pad, constant_values=-1).reshape(-1)


def gather_body(target_ref, density_ref, *refs):
    *out_refs, hot_ref = refs
    peers, _, rows, lanes = out_refs[0].shape
    depth = hot_ref.shape[1]

    @pl.when(pl.program_id(0) == 0)
    def _():
        hot_ref[...] = hot_rows(target_ref[...], depth)

    source = density_ref[...].reshape(depth, lanes)
    half = lanes // 2
    for part in range(2):
        span = slice(part * half, (part + 1) * half)
        picked = dot_nn(hot_ref[...], source[:, span]).reshape(-1, rows, half)
        for which, out_ref in enumerate(out_refs):
            mine = picked[which * peers : (which + 1) * peers]
            out_ref[:, 0, :, span] = mine.astype(BF16)


def gather_tiles(wanted, density_rows):
    peers, slots = wanted[0].shape
    rows_dev, dens, blocks, lanes = density_rows.shape
    per = rows_per_group(slots)
    groups, rows = dens // per, per * slots
    depth = rows_dev * per * blocks
    target = jnp.concatenate([tile_rows(each, per, blocks).reshape(-1, 1) for each in wanted])
    out = jax.ShapeDtypeStruct((peers, groups, rows, lanes), BF16)
    return pl.pallas_call(
        gather_body,
        grid=(groups,),
        in_specs=[
            pl.BlockSpec(target.shape, lambda g: (0, 0)),
            pl.BlockSpec((rows_dev, per, blocks, lanes), lambda g: (0, g, 0, 0)),
        ],
        out_specs=[pl.BlockSpec((peers, 1, rows, lanes), lambda g: (0, g, 0, 0))] * len(wanted),
        out_shape=[out] * len(wanted),
        scratch_shapes=[pltpu.VMEM((target.shape[0], depth), BF16)],
        compiler_params=params(),
        name="gather_tiles",
    )(target, density_rows)


def pick_body(*refs, relay, swapped, based):
    if relay:
        relay_target_ref, relayed_ref, *refs = refs
    if based:
        base_ref, *refs = refs
    if swapped:
        swap_ref, *refs = refs
    target_ref, slots_ref, out_ref, total_ref = refs
    step = pl.program_id(0)
    depth = slots_ref.shape[0]

    def fresh():
        total = dot_nn(hot_rows(target_ref[...], depth, step * depth), slots_ref[...])
        if relay:
            hot = hot_rows(relay_target_ref[...], relayed_ref.shape[0])
            total += dot_nn(hot, relayed_ref[...])
        elif based:
            total += base_ref[...].astype(F32)
        return total

    def finish(total):
        if not swapped:
            total = total.reshape(out_ref.shape)
            out_ref[...] = total.astype(BF16)
            return
        half = out_ref.shape[0] // 2
        out_ref[:half, :] = total[:half, :].astype(BF16)
        out_ref[half:, :] = dot_nn(total[half:, :].astype(BF16), swap_ref[...]).astype(BF16)

    if total_ref.shape[0] == 8:
        finish(fresh())
        return

    @pl.when(step == 0)
    def _():
        total_ref[...] = fresh()

    @pl.when(step > 0)
    def _():
        hot = hot_rows(target_ref[...], depth, step * depth)
        total_ref[...] += dot_nn(hot, slots_ref[...])

    @pl.when(step == pl.num_programs(0) - 1)
    def _():
        finish(total_ref[...])


def pick_rows(row_of, received, swap=None, relay_row_of=None, relayed=None, base=None, shape=None):
    depth, lanes = received.shape
    chunk = depth
    if depth > 1536:
        chunk = math.gcd(depth, 1024) if depth % 1024 == 0 else math.gcd(depth, 512)
    wanted = row_of.shape[0]
    column = pl.BlockSpec((wanted, 1), lambda k: (0, 0))
    specs, operands = [], []
    if relayed is not None:
        specs += [column, pl.BlockSpec(relayed.shape, lambda k: (0, 0))]
        operands += [relay_row_of.reshape(wanted, 1), relayed]
    if base is not None:
        specs += [pl.BlockSpec(base.shape, lambda k: (0, 0))]
        operands += [base]
    if swap is not None:
        specs += [pl.BlockSpec(swap.shape, lambda k: (0, 0))]
        operands += [swap]
    return pl.pallas_call(
        functools.partial(
            pick_body,
            relay=relayed is not None,
            swapped=swap is not None,
            based=base is not None,
        ),
        grid=(depth // chunk,),
        in_specs=[*specs, column, pl.BlockSpec((chunk, lanes), lambda k: (k, 0))],
        out_specs=pl.BlockSpec(shape or (wanted, lanes), lambda k: (0,) * len(shape or (0, 0))),
        out_shape=jax.ShapeDtypeStruct(shape or (wanted, lanes), BF16),
        scratch_shapes=[pltpu.VMEM((8 if chunk == depth else wanted, lanes), F32)],
        compiler_params=params(),
        name="pick_rows",
    )(*operands, row_of.reshape(wanted, 1), received)


def exchange(source_ref, trade, out_ref, width):
    low = 128 // width
    high = width // low

    def one(block, carry):
        piece = source_ref[:, pl.ds(pl.multiple_of(block * 128, 128), 128)]
        piece = piece.reshape(high, low, width, 128)
        wide = jnp.concatenate(
            [piece[:, part].reshape(high * width, 128) for part in range(low)], axis=1
        )
        traded = dot_nn(wide, trade).astype(BF16)
        for part in range(low):
            group = traded[:, part * 128 : (part + 1) * 128].reshape(high, width, 128)
            row = pl.multiple_of((block * low + part) * width, width)
            for lead in range(high):
                out_ref[pl.ds(row, width), lead * 128 : (lead + 1) * 128] = group[lead]
        return carry

    lax.fori_loop(0, width * width // 128, one, 0, unroll=4)


def regroup_body(swap_ref, trade_ref, block_ref, *refs, width):
    first_ref, second_ref, swapped_ref = refs[-3:]
    lanes = width * width
    half = lanes // 2
    for part in range(2):
        span = slice(part * half, (part + 1) * half)
        swapped_ref[:, span] = dot_nn(block_ref[0], swap_ref[:, span]).astype(BF16)
    exchange(swapped_ref, trade_ref[...], first_ref.at[0], width)
    exchange(block_ref.at[0], trade_ref[...], second_ref.at[0], width)


def regroup(integrals, swap, trade, begin, end, into=(), work=1):
    count, lanes, _ = integrals.shape
    width = math.isqrt(lanes)
    whole = pl.BlockSpec((1, lanes, lanes), lambda i: (i + begin, 0, 0))
    out = jax.ShapeDtypeStruct(integrals.shape, BF16)
    return pl.pallas_call(
        functools.partial(regroup_body, width=width),
        grid=(end - begin,),
        in_specs=[
            pl.BlockSpec(swap.shape, lambda i: (0, 0)),
            pl.BlockSpec(trade.shape, lambda i: (0, 0)),
            whole,
            *[pl.BlockSpec(memory_space=pl.ANY)] * len(into),
        ],
        out_specs=[whole, whole],
        out_shape=[out, out],
        scratch_shapes=[pltpu.VMEM((lanes, lanes), BF16)],
        input_output_aliases={3 + which: which for which in range(len(into))},
        compiler_params=params(),
        cost_estimate=cost(work, work),
        name="regroup",
    )(swap, trade, integrals, *into)


def contract_body(tiles_ref, block_ref, first_ref, second_ref, high_ref, low_ref):
    block, first, second = block_ref[0], first_ref[0], second_ref[0]

    def tile(role):
        return tiles_ref[ORDER.index(role), 0]

    def put(role, term):
        top = term.astype(BF16)
        role = ORDER.index(role)
        high_ref[role, 0] = top
        low_ref[role, 0] = (term - top.astype(F32)).astype(BF16)

    put(0, 2.0 * dot_nt(tile(4), block))
    put(4, 2.0 * dot_nn(tile(0), block))
    put(1, -dot_nn(tile(3), first))
    put(3, -dot_nt(tile(1), first))
    put(2, -dot_nt(tile(5), second))
    put(5, -dot_nn(tile(2), second))


def contract(tiles, integrals, first, second):
    count, lanes, _ = integrals.shape
    whole = pl.BlockSpec((1, lanes, lanes), lambda i: (i, 0, 0))
    part = pl.BlockSpec((ROLES, 1, PAD_N, lanes), lambda i: (0, i, 0, 0))
    out = jax.ShapeDtypeStruct((ROLES, count, PAD_N, lanes), BF16)
    return pl.pallas_call(
        contract_body,
        grid=(count,),
        in_specs=[part, whole, whole, whole],
        out_specs=[part, part],
        out_shape=[out, out],
        compiler_params=params(),
        name="contract",
    )(tiles, integrals, first, second)


def pack_body(target_ref, swap_ref, high_ref, low_ref, out_ref, terms_ref):
    half = high_ref.shape[0]

    @pl.when(pl.program_id(0) == 0)
    def _():
        mid = half // 2
        for which, source in enumerate((high_ref, low_ref)):
            start = which * half
            terms_ref[start : start + mid, :] = source[:mid, :]
            swapped = dot_nn(source[mid:, :], swap_ref[...]).astype(BF16)
            terms_ref[start + mid : start + half, :] = swapped

    out_ref[...] = dot_nn(hot_rows(target_ref[...], 2 * half), terms_ref[...]).astype(BF16)


def pack_terms(row_of, swap, high, low):
    count = row_of.shape[0]
    half, lanes = high.shape
    chunk = math.gcd(count, 512)
    return pl.pallas_call(
        pack_body,
        grid=(count // chunk,),
        in_specs=[
            pl.BlockSpec((chunk, 1), lambda k: (k, 0)),
            pl.BlockSpec((lanes, lanes), lambda k: (0, 0)),
            pl.BlockSpec((half, lanes), lambda k: (0, 0)),
            pl.BlockSpec((half, lanes), lambda k: (0, 0)),
        ],
        out_specs=pl.BlockSpec((chunk, lanes), lambda k: (k, 0)),
        out_shape=jax.ShapeDtypeStruct((count, lanes), BF16),
        scratch_shapes=[pltpu.VMEM((2 * half, lanes), BF16)],
        compiler_params=params(),
        name="pack_terms",
    )(row_of.reshape(count, 1), swap, high, low)


def scatter_body(*refs, relay):
    if relay:
        relay_target_ref, relayed_ref, *refs, relay_hot_ref = refs
    target_ref, slots_ref, out_ref, hot_ref = refs
    rows_dev, per, blocks, lanes = out_ref.shape
    height = per * blocks
    depth = hot_ref.shape[1]

    @pl.when(pl.program_id(0) == 0)
    def _():
        hot_ref[...] = hot_columns(target_ref[...], rows_dev * height)
        if relay:
            for part in range(relay_hot_ref.shape[0]):
                target = relay_target_ref[part : part + 1, :]
                relay_hot_ref[part] = hot_columns(target, rows_dev * height)

    slots = slots_ref[...].reshape(depth, lanes)
    for row in range(rows_dev):
        span = slice(row * height, (row + 1) * height)
        total = dot_nn(hot_ref[span, :], slots)
        if relay:
            part = pl.program_id(0) % relay_hot_ref.shape[0]
            relayed = relayed_ref[...].astype(F32).reshape(-1, lanes).astype(BF16)
            total += dot_nn(relay_hot_ref[part, span, :], relayed)
        out_ref[row] = total.astype(BF16).reshape(per, blocks, lanes)


def scatter_split(slots):
    return max(slots, 8)


def landing_rows(landing, blocks):
    slots = landing.shape[1]
    return tile_rows(landing, scatter_split(slots) // slots, blocks).reshape(1, -1)


def relay_landing_rows(landing, slots, blocks):
    per = scatter_split(slots) // slots
    inner = jnp.arange(RELAY_ROWS, dtype=jnp.int32)
    rows = (landing // blocks * (per * blocks) + landing % blocks)[:, None] + inner % per * blocks
    kind = jnp.arange(RELAY_ROWS // per, dtype=jnp.int32)[:, None, None]
    rows = jnp.where((landing[:, None] >= 0) & (inner // per == kind), rows, -1)
    return rows.reshape(kind.shape[0], -1)


def scatter_terms(target, arrived, slots, rows_dev, blocks, relay_target=None, relayed=None):
    peers, groups, rows, lanes = arrived.shape
    split = scatter_split(slots)
    steps, per = groups * rows // split, split // slots
    high = rows_dev * per * blocks
    specs, operands = [], []
    scratch = [pltpu.VMEM((high, peers * split), BF16)]
    if relayed is not None:
        depth = peers * RELAY_ROWS
        kinds = relay_target.shape[0]
        specs = [
            pl.BlockSpec((kinds, depth), lambda g: (0, 0)),
            pl.BlockSpec((peers, 1, RELAY_ROWS, lanes), lambda g: (0, g // kinds, 0, 0)),
        ]
        operands = [relay_target, relayed]
        scratch += [pltpu.VMEM((kinds, high, depth), BF16)]
    return pl.pallas_call(
        functools.partial(scatter_body, relay=relayed is not None),
        grid=(steps,),
        in_specs=[
            *specs,
            pl.BlockSpec((1, peers * split), lambda g: (0, 0)),
            pl.BlockSpec((peers, 1, split, lanes), lambda g: (0, g, 0, 0)),
        ],
        out_specs=pl.BlockSpec((rows_dev, per, blocks, lanes), lambda g: (0, g, 0, 0)),
        out_shape=jax.ShapeDtypeStruct((rows_dev, steps * per, blocks, lanes), BF16),
        scratch_shapes=scratch,
        compiler_params=params(),
        name="scatter_terms",
    )(*operands, target, arrived.reshape(peers, steps, split, lanes))


def route_body(
    me_ref, list_ref, state_hbm, out_ref, sent_ref, passed_ref, landed_ref, state_ref, sem,
    *, spare, begin, tag, span, caps, outward
):
    peers = list_ref.shape[0]
    second = peers * peers
    copy = pltpu.make_async_copy(state_hbm, state_ref, sem)
    copy.start()
    me = me_ref[0]

    for ref in (sent_ref, passed_ref, landed_ref):

        def clear(index, carry, ref=ref):
            ref[index] = -1
            return carry

        lax.fori_loop(0, ref.shape[0], clear, 0, unroll=8)
    copy.wait()

    def first_at(source, middle):
        return source * peers + middle if outward else middle * peers + source

    def one(row, place, failed):
        value = list_ref[row, begin + place]
        other = value // (span * tag)
        source, last = (row, other) if outward else (other, row)

        def search(carry):
            tries, middle, found = carry
            full = state_ref[first_at(source, middle)] >= caps[0]
            taken = state_ref[second + last * peers + middle] >= caps[1]
            found = jnp.where(full | taken, found, middle)
            following = jnp.where(middle + 1 == peers, 0, middle + 1)
            return tries + 1, following, found

        start = source + last
        start = jnp.where(start >= peers, start - peers, start)
        _, _, found = lax.while_loop(
            lambda carry: (carry[0] < peers) & (carry[2] < 0),
            search,
            (jnp.int32(0), start, jnp.int32(-1)),
        )
        index = row * spare + place
        out_ref[index] = -1

        @pl.when(found >= 0)
        def _():
            first_state, then_state = first_at(source, found), second + last * peers + found
            first, then = state_ref[first_state], state_ref[then_state]
            out_ref[index] = found * caps[1] + then
            state_ref[first_state] = first + 1
            state_ref[then_state] = then + 1
            tile = value // tag - me * span

            @pl.when(source == me)
            def _():
                sent_ref[found * caps[0] + first] = value % tag if outward else tile

            @pl.when(found == me)
            def _():
                passed_ref[last * caps[1] + then] = source * caps[0] + first

            @pl.when(last == me)
            def _():
                landed_ref[found * caps[1] + then] = tile if outward else value % tag

        return failed + jnp.where(found < 0, 1, 0)

    def each(row, failed):
        count = jnp.minimum(list_ref[row, begin + spare], spare)
        return lax.fori_loop(0, count, functools.partial(lambda p, f, r: one(r, p, f), r=row), failed)

    out_ref[peers * spare] = lax.fori_loop(0, peers, each, jnp.int32(0))


def route(me, table, begin, spare, first, second, caps, tag, span, outward):
    peers = table.shape[0]
    state = jnp.concatenate([first, second]).reshape(-1)
    smem = pl.BlockSpec(memory_space=pltpu.SMEM)
    counts = (peers * spare + 1, peers * caps[0], peers * caps[1], peers * caps[1])
    out, sent, passed, landed = pl.pallas_call(
        functools.partial(
            route_body, spare=spare, begin=begin, tag=tag, span=span, caps=caps, outward=outward
        ),
        in_specs=[smem, smem, pl.BlockSpec(memory_space=pl.ANY)],
        out_specs=[smem] * 4,
        out_shape=[jax.ShapeDtypeStruct((count,), jnp.int32) for count in counts],
        scratch_shapes=[pltpu.SMEM((2 * peers * peers,), jnp.int32), pltpu.SemaphoreType.DMA],
        name="route",
    )(me[None], table, state)
    return sent.reshape(peers, caps[0]), passed, landed, out[-1]


def tile_keys(quartets, owner_map):
    blocks = owner_map.shape[0]
    row_blocks = jnp.stack([quartets[:, pick] for pick in ROLE_ROW]).reshape(-1)
    col_blocks = jnp.stack([quartets[:, pick] for pick in ROLE_COL]).reshape(-1)
    ids = jnp.arange(blocks, dtype=jnp.int32)
    storage = jnp.sum(jnp.where(row_blocks[:, None] == ids, owner_map, 0), axis=-1)
    return storage * blocks + col_blocks


def earlier(flags):
    ids = jnp.arange(flags.shape[-1])
    ahead = ids[:, None] < ids[None, :]
    return jnp.sum((flags[..., :, None] & ahead).astype(jnp.int32), axis=-2)


def choose(hit, values, axis):
    return jnp.sum(jnp.where(hit, values + 1, 0), axis=axis) - 1


def spilled(flags, values, spare):
    place = earlier(flags)
    hit = flags[..., None] & (place[..., None] == jnp.arange(spare))
    return choose(hit, values[..., None], -2), jnp.sum(flags.astype(jnp.int32), axis=-1)


def permutation_tables(width):
    lanes = width * width
    low = 128 // width
    index = jnp.arange(lanes, dtype=jnp.int32)
    partner = index % width * width + index // width
    swap = (index[:, None] == partner[None, :]).astype(BF16)
    span = jnp.arange(low * 128, dtype=jnp.int32)
    lead, group, inner = span // 128, span % 128 // width, span % width
    partner = group * 128 + lead * width + inner
    trade = (span[None, :] == partner[:, None]).astype(BF16)
    return swap, trade


def slot_count(most):
    for slots in (4, 8, 16):
        if most <= slots:
            return slots
    raise ValueError(most)


def exchange_slots(array):
    return lax.all_to_all(array, AXES, split_axis=0, concat_axis=0, tiled=True)


def slot_count(most):
    for slots in (4, 8, 16):
        if most <= slots:
            return slots
    raise ValueError(most)


def exchange_slots(array, axis=0):
    return lax.all_to_all(array, AXES, split_axis=axis, concat_axis=axis, tiled=True)


def hand_on(slot_of, received, dens):
    peers = slot_of.shape[0]
    lanes = received.shape[-1]
    shape = (peers, dens // RELAY_ROWS, RELAY_ROWS, lanes)
    rows = slot_rows(slot_of, FIRST_SLOTS, dens).reshape(-1)
    return exchange_slots(pick_rows(rows, received.reshape(-1, lanes), shape=shape))


def local(integrals, quartets, density, owner_map):
    rows_dev, blocks, dens, lanes = density.shape
    devices = lax.axis_size(AXES)
    me = lax.axis_index(AXES)
    quartet_count = quartets.shape[0]
    tile_count = ROLES * quartet_count
    span = rows_dev * blocks
    most = 2 * rows_dev
    tag = 1 << (2 * tile_count - 1).bit_length()
    device_ids = jnp.arange(devices, dtype=jnp.int32)
    tile_ids = jnp.arange(tile_count, dtype=jnp.int32)
    density_rows = jnp.transpose(density, (0, 2, 1, 3))
    swap, trade = permutation_tables(math.isqrt(lanes))

    key = tile_keys(quartets, owner_map)
    holder = key // span
    rank = jnp.sum(
        ((holder[:, None] == holder) & (tile_ids[:, None] < tile_ids)).astype(jnp.int32), axis=0
    )
    asked = jnp.sum((holder[:, None] == device_ids).astype(jnp.int32), axis=0)
    spare, spare_count = spilled(rank >= 2 * READ_SLOTS, key * tag + tile_ids, READ_SPARE)
    message = jnp.concatenate([key * 16 + rank, spare, spare_count[None], asked])
    message = jnp.pad(message, (0, -message.shape[0] % 128))
    told = exchange_slots(jnp.broadcast_to(message, (devices,) + message.shape))
    keys, ranks = told[:, :tile_count] // 16, told[:, :tile_count] % 16
    counts = told[:, tile_count + READ_SPARE + 1 :][:, :devices]
    in_second = jnp.minimum(counts, READ_SLOTS)
    in_first = jnp.minimum(counts - in_second, READ_SLOTS)
    caps = (READ_SLOTS, READ_SLOTS)
    extra, passed, landed, read_misses = route(
        me, told, tile_count, READ_SPARE, in_first, in_second, caps, tag, span, False
    )
    most_spare = jnp.max(told[:, tile_count + READ_SPARE])
    read_fits = (read_misses == 0) & (most_spare <= READ_SPARE)

    mine = keys // span == me
    local_tile = keys - me * span

    def requests(begin, slots):
        hit = mine[:, :, None] & (ranks[:, :, None] == jnp.arange(slots) + begin)
        return choose(hit, local_tile[:, :, None], 1)

    wanted = jnp.maximum(requests(READ_SLOTS, READ_SLOTS), extra)
    sent, sent_then = gather_tiles([wanted, requests(0, READ_SLOTS)], density_rows)
    received = exchange_slots(sent)
    early = quartet_count * 5 // 8
    work = 2 * lanes**3 * early
    first, second = regroup(integrals, swap, trade, 0, early, work=work)
    received, first, second = lax.optimization_barrier((received, first, second))
    passed_rows = slot_rows(passed, READ_SLOTS, dens).reshape(devices, READ_SLOTS, -1, 4)
    passed_rows = jnp.transpose(passed_rows, (0, 2, 3, 1)).reshape(-1)
    passed_on = pick_rows(
        passed_rows, received.reshape(-1, lanes), base=sent_then.reshape(-1, lanes)
    )
    received_then = exchange_slots(passed_on.reshape(sent_then.shape))
    keys, ranks, first, second, _ = lax.optimization_barrier((keys, ranks, first, second, passed_on))
    first, second = regroup(integrals, swap, trade, early, quartet_count, (first, second))

    homes = keys // span
    flat = keys.reshape(-1)
    shared = jnp.sum((flat[:, None] == flat).astype(jnp.int32), axis=0) > 1
    shared = shared.reshape(keys.shape)
    together = homes[:, :, None] == homes[:, None, :]
    before = 1 + (shared[:, :, None] & (tile_ids[:, None] < tile_ids)).astype(jnp.int32)
    low_ranks = jnp.where(shared, jnp.sum(jnp.where(together, before, 0), axis=1), -1)
    at_home = homes[:, :, None] == device_ids
    low_counts = jnp.sum((at_home & shared[:, :, None]).astype(jnp.int32), axis=1)
    both_ranks = jnp.concatenate([ranks, low_ranks], axis=1)
    values = keys * tag + tile_ids
    values = jnp.concatenate([values, values + tile_count], axis=1)
    term_list, term_counts = spilled(both_ranks >= FIRST_SLOTS, values, TERM_SPARE)
    term_table = jnp.concatenate([term_list, term_counts[:, None]], axis=1)
    in_use = counts + low_counts
    caps = (FIRST_SLOTS, 1)
    term_extra, term_passed, term_landed, term_misses = route(
        me, term_table, 0, TERM_SPARE, in_use, jnp.zeros_like(in_use), caps, tag, span, True
    )
    term_fits = (term_misses == 0) & (jnp.max(term_counts) <= TERM_SPARE)

    slot_ids = jnp.arange(devices * READ_SLOTS, dtype=jnp.int32)
    via = choose(landed[:, None] == tile_ids, slot_ids[:, None], 0)
    slot = holder * READ_SLOTS + rank
    then_slot = jnp.where(rank < READ_SLOTS, slot, via)
    direct = (rank >= READ_SLOTS) & (rank < 2 * READ_SLOTS)
    now_slot = jnp.where(direct, slot - READ_SLOTS, -1)
    now_rows = pad_rows(slot_rows(now_slot, READ_SLOTS, dens)).reshape(-1, 1)
    then_rows = pad_rows(slot_rows(then_slot, READ_SLOTS, dens)).reshape(-1, 1)
    now_rows, then_rows = lax.optimization_barrier((now_rows, then_rows))

    def read_two_step():
        return pick_rows(
            now_rows,
            received.reshape(-1, lanes),
            swap,
            then_rows,
            received_then.reshape(-1, lanes),
        )

    def read_one_step():
        slots = slot_count(most)
        (whole,) = gather_tiles([requests(0, slots)], density_rows)
        rows = pad_rows(slot_rows(holder * slots + rank, slots, dens))
        return pick_rows(rows, exchange_slots(whole).reshape(-1, lanes), swap)

    tiles = lax.cond(read_fits, read_two_step, read_one_step)
    tiles = tiles.reshape(ROLES, quartet_count, PAD_N, lanes)
    high, low = contract(tiles, integrals, first, second)
    high = high.reshape(tile_count * PAD_N, lanes)
    low = low.reshape(tile_count * PAD_N, lanes)

    def send(term_of_slot, slots):
        per = rows_per_group(slots)
        ids = jnp.arange(dens, dtype=jnp.int32).reshape(1, dens // per, per, 1)
        term = term_of_slot[:, None, None, :]
        rows = jnp.where(term >= 0, term * PAD_N + ids, -1).reshape(-1)
        packed = pack_terms(rows, swap, high, low)
        return exchange_slots(packed.reshape(devices, dens // per, per * slots, lanes))

    to_holder = holder[:, None] == device_ids
    place_ids = jnp.arange(FIRST_SLOTS, dtype=jnp.int32)
    my_low = lax.dynamic_index_in_dim(low_ranks, me, 0, keepdims=False)
    ends = jnp.concatenate([to_holder, to_holder])[:, :, None]
    places = jnp.concatenate([rank, my_low])[:, None, None] == place_ids
    both_ids = jnp.arange(2 * tile_count, dtype=jnp.int32)
    term_of_slot = choose(ends & places, both_ids[:, None, None], 0)
    arrived = send(jnp.maximum(term_of_slot, term_extra), FIRST_SLOTS)
    relayed = hand_on(term_passed, arrived, dens)

    hit = (ranks[:, :, None] == place_ids) | (low_ranks[:, :, None] == place_ids)
    landing = landing_rows(choose(mine[:, :, None] & hit, local_tile[:, :, None], 1), blocks)
    relay_landing = relay_landing_rows(term_landed, FIRST_SLOTS, blocks)
    landing, relay_landing = lax.optimization_barrier((landing, relay_landing))

    def write_two_step():
        return scatter_terms(
            landing, arrived, FIRST_SLOTS, rows_dev, blocks, relay_landing, relayed
        )

    def write_one_step():
        slots = slot_count(most)
        wide = slot_count(2 * slots)
        places = rank[:, None, None] == jnp.arange(slots)
        term_of_slot = choose(to_holder[:, :, None] & places, tile_ids[:, None, None], 0)
        none = jnp.full((devices, wide // 2 - slots), -1, jnp.int32)
        low_term = jnp.where(term_of_slot >= 0, term_of_slot + tile_count, -1)
        whole = send(jnp.concatenate([term_of_slot, none, low_term, none], axis=1), wide)
        wanted = requests(0, slots)
        landing = jnp.concatenate([wanted, none, wanted, none], axis=1)
        return scatter_terms(landing_rows(landing, blocks), whole, wide, rows_dev, blocks)

    fock = lax.cond(term_fits, write_two_step, write_one_step)
    return jnp.transpose(fock, (0, 2, 1, 3))


def solution(mesh):
    return jax.shard_map(
        local,
        mesh=mesh,
        in_specs=(
            P(AXES, None, None),
            P(AXES, None),
            P(AXES, None, None, None),
            P(),
        ),
        out_specs=P(AXES, None, None, None),
        check_vma=False,
    )
```

```python
import functools
import math

import jax
import jax.numpy as jnp
from jax import lax
from jax.experimental import pallas as pl
from jax.experimental.pallas import tpu as pltpu
from jax.sharding import PartitionSpec as P

ORDER = (0, 1, 4, 2, 3, 5)
ROLE_ROW = tuple((0, 0, 1, 1, 2, 3)[role] for role in ORDER)
ROLE_COL = tuple((1, 2, 2, 3, 3, 0)[role] for role in ORDER)
ROLES = 6
PAD_N = 16
ROWS = 16
AXES = ("bra", "ket")
BF16 = jnp.bfloat16
F32 = jnp.float32
VMEM_BYTES = 60 * 1024 * 1024
READ_SLOTS = 2
FIRST_SLOTS = 4
RELAY_ROWS = 4
READ_SPARE = 8
TERM_SPARE = 16


def params(axes=1):
    return pltpu.CompilerParams(
        dimension_semantics=("arbitrary",) * axes, vmem_limit_bytes=VMEM_BYTES
    )


def cost(flops, moved):
    return pl.CostEstimate(flops=int(flops), bytes_accessed=int(moved), transcendentals=0)


def hot_rows(target, width, base=0):
    columns = lax.broadcasted_iota(jnp.int32, (target.shape[0], width), 1) + base
    return jnp.where(columns == target, 1.0, 0.0).astype(BF16)


def hot_columns(target, height, base=0):
    rows = lax.broadcasted_iota(jnp.int32, (height, target.shape[1]), 0) + base
    return jnp.where(rows == target, 1.0, 0.0).astype(BF16)


def dot_nn(left, right):
    return jnp.dot(left, right, preferred_element_type=F32)


def dot_nt(left, right):
    return lax.dot_general(left, right, (((1,), (1,)), ((), ())), preferred_element_type=F32)


def rows_per_group(slots):
    return min(4, ROWS // slots)


def tile_rows(tiles, per, blocks):
    inner = jnp.arange(per, dtype=jnp.int32)[None, :, None]
    rows = (tiles // blocks * (per * blocks) + tiles % blocks)[:, None, :] + inner * blocks
    return jnp.where(tiles[:, None, :] >= 0, rows, -1)


def slot_rows(slot, slots, dens):
    ids = jnp.arange(dens, dtype=jnp.int32)
    per = rows_per_group(slots)
    rows = (slot // slots * (dens * slots) + slot % slots)[..., None]
    rows = rows + ids // per * (per * slots) + ids % per * slots
    return jnp.where(slot[..., None] >= 0, rows, -1)


def pad_rows(rows):
    pad = [(0, 0)] * (rows.ndim - 1) + [(0, PAD_N - rows.shape[-1])]
    return jnp.pad(rows, pad, constant_values=-1).reshape(-1)


def gather_body(target_ref, density_ref, *refs):
    *out_refs, hot_ref = refs
    peers, _, rows, lanes = out_refs[0].shape
    depth = hot_ref.shape[1]

    @pl.when((pl.program_id(0) == 0) & (pl.program_id(1) == 0))
    def _():
        hot_ref[...] = hot_rows(target_ref[...], depth)

    source = density_ref[...].reshape(depth, lanes)
    picked = dot_nn(hot_ref[...], source).reshape(-1, rows, lanes)
    for which, out_ref in enumerate(out_refs):
        out_ref[:, 0] = picked[which * peers : (which + 1) * peers].astype(BF16)


def gather_tiles(wanted, density_rows):
    peers, slots = wanted[0].shape
    rows_dev, dens, blocks, lanes = density_rows.shape
    per = rows_per_group(slots)
    groups, rows = dens // per, per * slots
    depth = rows_dev * per * blocks
    target = jnp.concatenate([tile_rows(each, per, blocks).reshape(-1, 1) for each in wanted])
    out = jax.ShapeDtypeStruct((peers, groups, rows, lanes), BF16)
    return pl.pallas_call(
        gather_body,
        grid=(groups, 2),
        in_specs=[
            pl.BlockSpec(target.shape, lambda g, h: (0, 0)),
            pl.BlockSpec((rows_dev, per, blocks, lanes // 2), lambda g, h: (0, g, 0, h)),
        ],
        out_specs=[pl.BlockSpec((peers, 1, rows, lanes // 2), lambda g, h: (0, g, 0, h))] * len(wanted),
        out_shape=[out] * len(wanted),
        scratch_shapes=[pltpu.VMEM((target.shape[0], depth), BF16)],
        compiler_params=params(2),
        name="gather_tiles",
    )(target, density_rows)


def pick_body(*refs, relay, swapped, based):
    if relay:
        relay_target_ref, relayed_ref, *refs = refs
    if based:
        base_ref, *refs = refs
    if swapped:
        swap_ref, *refs = refs
    target_ref, slots_ref, out_ref, total_ref = refs
    step = pl.program_id(0)
    depth = slots_ref.shape[0]

    def fresh():
        total = dot_nn(hot_rows(target_ref[...], depth, step * depth), slots_ref[...])
        if relay:
            hot = hot_rows(relay_target_ref[...], relayed_ref.shape[0])
            total += dot_nn(hot, relayed_ref[...])
        elif based:
            total += base_ref[...].astype(F32)
        return total

    def finish(total):
        if not swapped:
            total = total.reshape(out_ref.shape)
            out_ref[...] = total.astype(BF16)
            return
        half = out_ref.shape[0] // 2
        out_ref[:half, :] = total[:half, :].astype(BF16)
        out_ref[half:, :] = dot_nn(total[half:, :].astype(BF16), swap_ref[...]).astype(BF16)

    if total_ref.shape[0] == 8:
        finish(fresh())
        return

    @pl.when(step == 0)
    def _():
        total_ref[...] = fresh()

    @pl.when(step > 0)
    def _():
        hot = hot_rows(target_ref[...], depth, step * depth)
        total_ref[...] += dot_nn(hot, slots_ref[...])

    @pl.when(step == pl.num_programs(0) - 1)
    def _():
        finish(total_ref[...])


def pick_rows(row_of, received, swap=None, relay_row_of=None, relayed=None, base=None, shape=None):
    depth, lanes = received.shape
    chunk = depth
    if depth > 1536:
        chunk = math.gcd(depth, 256)
    wanted = row_of.shape[0]
    column = pl.BlockSpec((wanted, 1), lambda k: (0, 0))
    specs, operands = [], []
    if relayed is not None:
        specs += [column, pl.BlockSpec(relayed.shape, lambda k: (0, 0))]
        operands += [relay_row_of.reshape(wanted, 1), relayed]
    if base is not None:
        specs += [pl.BlockSpec(base.shape, lambda k: (0, 0))]
        operands += [base]
    if swap is not None:
        specs += [pl.BlockSpec(swap.shape, lambda k: (0, 0))]
        operands += [swap]
    return pl.pallas_call(
        functools.partial(
            pick_body,
            relay=relayed is not None,
            swapped=swap is not None,
            based=base is not None,
        ),
        grid=(depth // chunk,),
        in_specs=[*specs, column, pl.BlockSpec((chunk, lanes), lambda k: (k, 0))],
        out_specs=pl.BlockSpec(shape or (wanted, lanes), lambda k: (0,) * len(shape or (0, 0))),
        out_shape=jax.ShapeDtypeStruct(shape or (wanted, lanes), BF16),
        scratch_shapes=[pltpu.VMEM((8 if chunk == depth else wanted, lanes), F32)],
        compiler_params=params(),
        name="pick_rows",
    )(*operands, row_of.reshape(wanted, 1), received)


def exchange(source_ref, trade, out_ref, width):
    low = 128 // width
    high = width // low

    def one(block, carry):
        piece = source_ref[:, pl.ds(pl.multiple_of(block * 128, 128), 128)]
        piece = piece.reshape(high, low, width, 128)
        wide = jnp.concatenate(
            [piece[:, part].reshape(high * width, 128) for part in range(low)], axis=1
        )
        traded = dot_nn(wide, trade).astype(BF16)
        for part in range(low):
            group = traded[:, part * 128 : (part + 1) * 128].reshape(high, width, 128)
            row = pl.multiple_of((block * low + part) * width, width)
            for lead in range(high):
                out_ref[pl.ds(row, width), lead * 128 : (lead + 1) * 128] = group[lead]
        return carry

    lax.fori_loop(0, width * width // 128, one, 0, unroll=4)


def regroup_body(swap_ref, trade_ref, block_ref, *refs, width):
    first_ref, second_ref, swapped_ref = refs[-3:]
    quarter = width * width // 4

    def swap(part, carry):
        span = pl.ds(pl.multiple_of(part * quarter, quarter), quarter)
        swapped_ref[span, :] = dot_nn(block_ref[0, span, :], swap_ref[...]).astype(BF16)
        return carry

    lax.fori_loop(0, 4, swap, 0)
    exchange(swapped_ref, trade_ref[...], first_ref.at[0], width)
    exchange(block_ref.at[0], trade_ref[...], second_ref.at[0], width)


def regroup(integrals, swap, trade, begin, end, into=(), work=1):
    count, lanes, _ = integrals.shape
    width = math.isqrt(lanes)
    whole = pl.BlockSpec((1, lanes, lanes), lambda i: (i + begin, 0, 0))
    out = jax.ShapeDtypeStruct(integrals.shape, BF16)
    return pl.pallas_call(
        functools.partial(regroup_body, width=width),
        grid=(end - begin,),
        in_specs=[
            pl.BlockSpec(swap.shape, lambda i: (0, 0)),
            pl.BlockSpec(trade.shape, lambda i: (0, 0)),
            whole,
            *[pl.BlockSpec(memory_space=pl.ANY)] * len(into),
        ],
        out_specs=[whole, whole],
        out_shape=[out, out],
        scratch_shapes=[pltpu.VMEM((lanes, lanes), BF16)],
        input_output_aliases={3 + which: which for which in range(len(into))},
        compiler_params=params(),
        cost_estimate=cost(work, work),
        name="regroup",
    )(swap, trade, integrals, *into)


def contract_body(tiles_ref, block_ref, first_ref, second_ref, high_ref, low_ref):
    block, first, second = block_ref[0], first_ref[0], second_ref[0]

    def tile(role):
        return tiles_ref[ORDER.index(role), 0]

    def put(role, term):
        top = term.astype(BF16)
        role = ORDER.index(role)
        high_ref[role, 0] = top
        low_ref[role, 0] = (term - top.astype(F32)).astype(BF16)

    put(0, 2.0 * dot_nt(tile(4), block))
    put(4, 2.0 * dot_nn(tile(0), block))
    put(1, -dot_nn(tile(3), first))
    put(3, -dot_nt(tile(1), first))
    put(2, -dot_nt(tile(5), second))
    put(5, -dot_nn(tile(2), second))


def contract(tiles, integrals, first, second):
    count, lanes, _ = integrals.shape
    whole = pl.BlockSpec((1, lanes, lanes), lambda i: (i, 0, 0))
    part = pl.BlockSpec((ROLES, 1, PAD_N, lanes), lambda i: (0, i, 0, 0))
    out = jax.ShapeDtypeStruct((ROLES, count, PAD_N, lanes), BF16)
    return pl.pallas_call(
        contract_body,
        grid=(count,),
        in_specs=[part, whole, whole, whole],
        out_specs=[part, part],
        out_shape=[out, out],
        compiler_params=params(),
        name="contract",
    )(tiles, integrals, first, second)


def pack_body(target_ref, swap_ref, high_ref, low_ref, out_ref, terms_ref):
    half = high_ref.shape[0]

    @pl.when(pl.program_id(0) == 0)
    def _():
        mid = half // 2
        for which, source in enumerate((high_ref, low_ref)):
            start = which * half
            terms_ref[start : start + mid, :] = source[:mid, :]
            swapped = dot_nn(source[mid:, :], swap_ref[...]).astype(BF16)
            terms_ref[start + mid : start + half, :] = swapped

    out_ref[...] = dot_nn(hot_rows(target_ref[...], 2 * half), terms_ref[...]).astype(BF16)


def pack_terms(row_of, swap, high, low):
    count = row_of.shape[0]
    half, lanes = high.shape
    chunk = math.gcd(count, 256)
    return pl.pallas_call(
        pack_body,
        grid=(count // chunk,),
        in_specs=[
            pl.BlockSpec((chunk, 1), lambda k: (k, 0)),
            pl.BlockSpec((lanes, lanes), lambda k: (0, 0)),
            pl.BlockSpec((half, lanes), lambda k: (0, 0)),
            pl.BlockSpec((half, lanes), lambda k: (0, 0)),
        ],
        out_specs=pl.BlockSpec((chunk, lanes), lambda k: (k, 0)),
        out_shape=jax.ShapeDtypeStruct((count, lanes), BF16),
        scratch_shapes=[pltpu.VMEM((2 * half, lanes), BF16)],
        compiler_params=params(),
        name="pack_terms",
    )(row_of.reshape(count, 1), swap, high, low)


def scatter_body(*refs, relay):
    if relay:
        relay_target_ref, relayed_ref, *refs, relay_hot_ref = refs
    target_ref, slots_ref, out_ref, hot_ref = refs
    rows_dev, per, blocks, lanes = out_ref.shape
    height = per * blocks
    depth = hot_ref.shape[1]

    @pl.when(pl.program_id(0) == 0)
    def _():
        hot_ref[...] = hot_columns(target_ref[...], rows_dev * height)
        if relay:
            for part in range(relay_hot_ref.shape[0]):
                target = relay_target_ref[part : part + 1, :]
                relay_hot_ref[part] = hot_columns(target, rows_dev * height)

    slots = slots_ref[...].reshape(depth, lanes)
    if relay:
        part = pl.program_id(0) % relay_hot_ref.shape[0]
        relayed = relayed_ref[...].astype(F32).reshape(-1, lanes).astype(BF16)

    def one(row, carry):
        span = pl.ds(pl.multiple_of(row * height, height), height)
        total = dot_nn(hot_ref[span, :], slots)
        if relay:
            total += dot_nn(relay_hot_ref[part, span, :], relayed)
        out_ref[row] = total.astype(BF16).reshape(per, blocks, lanes)
        return carry

    lax.fori_loop(0, rows_dev, one, 0)


def scatter_split(slots):
    return max(slots, 8)


def landing_rows(landing, blocks):
    slots = landing.shape[1]
    return tile_rows(landing, scatter_split(slots) // slots, blocks).reshape(1, -1)


def relay_landing_rows(landing, slots, blocks):
    per = scatter_split(slots) // slots
    inner = jnp.arange(RELAY_ROWS, dtype=jnp.int32)
    rows = (landing // blocks * (per * blocks) + landing % blocks)[:, None] + inner % per * blocks
    kind = jnp.arange(RELAY_ROWS // per, dtype=jnp.int32)[:, None, None]
    rows = jnp.where((landing[:, None] >= 0) & (inner // per == kind), rows, -1)
    return rows.reshape(kind.shape[0], -1)


def scatter_terms(target, arrived, slots, rows_dev, blocks, relay_target=None, relayed=None):
    peers, groups, rows, lanes = arrived.shape
    split = scatter_split(slots)
    steps, per = groups * rows // split, split // slots
    high = rows_dev * per * blocks
    specs, operands = [], []
    scratch = [pltpu.VMEM((high, peers * split), BF16)]
    if relayed is not None:
        depth = peers * RELAY_ROWS
        kinds = relay_target.shape[0]
        specs = [
            pl.BlockSpec((kinds, depth), lambda g: (0, 0)),
            pl.BlockSpec((peers, 1, RELAY_ROWS, lanes), lambda g: (0, g // kinds, 0, 0)),
        ]
        operands = [relay_target, relayed]
        scratch += [pltpu.VMEM((kinds, high, depth), BF16)]
    return pl.pallas_call(
        functools.partial(scatter_body, relay=relayed is not None),
        grid=(steps,),
        in_specs=[
            *specs,
            pl.BlockSpec((1, peers * split), lambda g: (0, 0)),
            pl.BlockSpec((peers, 1, split, lanes), lambda g: (0, g, 0, 0)),
        ],
        out_specs=pl.BlockSpec((rows_dev, per, blocks, lanes), lambda g: (0, g, 0, 0)),
        out_shape=jax.ShapeDtypeStruct((rows_dev, steps * per, blocks, lanes), BF16),
        scratch_shapes=scratch,
        compiler_params=params(),
        name="scatter_terms",
    )(*operands, target, arrived.reshape(peers, steps, split, lanes))


def route_body(
    me_ref, list_ref, state_hbm, out_ref, sent_ref, passed_ref, landed_ref, state_ref, sem,
    *, spare, begin, tag, span, caps, outward
):
    peers = list_ref.shape[0]
    second = peers * peers
    copy = pltpu.make_async_copy(state_hbm, state_ref, sem)
    copy.start()
    me = me_ref[0]

    for ref in (sent_ref, passed_ref, landed_ref):

        def clear(index, carry, ref=ref):
            ref[index] = -1
            return carry

        lax.fori_loop(0, ref.shape[0], clear, 0, unroll=8)
    copy.wait()

    def first_at(source, middle):
        return source * peers + middle if outward else middle * peers + source

    def one(row, place, failed):
        value = list_ref[row, begin + place]
        other = value // (span * tag)
        source, last = (row, other) if outward else (other, row)

        def search(carry):
            tries, middle, found = carry
            full = state_ref[first_at(source, middle)] >= caps[0]
            taken = state_ref[second + last * peers + middle] >= caps[1]
            found = jnp.where(full | taken, found, middle)
            following = jnp.where(middle + 1 == peers, 0, middle + 1)
            return tries + 1, following, found

        start = source + last
        start = jnp.where(start >= peers, start - peers, start)
        _, _, found = lax.while_loop(
            lambda carry: (carry[0] < peers) & (carry[2] < 0),
            search,
            (jnp.int32(0), start, jnp.int32(-1)),
        )
        index = row * spare + place
        out_ref[index] = -1

        @pl.when(found >= 0)
        def _():
            first_state, then_state = first_at(source, found), second + last * peers + found
            first, then = state_ref[first_state], state_ref[then_state]
            out_ref[index] = found * caps[1] + then
            state_ref[first_state] = first + 1
            state_ref[then_state] = then + 1
            tile = value // tag - me * span

            @pl.when(source == me)
            def _():
                sent_ref[found * caps[0] + first] = value % tag if outward else tile

            @pl.when(found == me)
            def _():
                passed_ref[last * caps[1] + then] = source * caps[0] + first

            @pl.when(last == me)
            def _():
                landed_ref[found * caps[1] + then] = tile if outward else value % tag

        return failed + jnp.where(found < 0, 1, 0)

    def each(row, failed):
        count = jnp.minimum(list_ref[row, begin + spare], spare)
        return lax.fori_loop(0, count, functools.partial(lambda p, f, r: one(r, p, f), r=row), failed)

    out_ref[peers * spare] = lax.fori_loop(0, peers, each, jnp.int32(0))


def route(me, table, begin, spare, first, second, caps, tag, span, outward):
    peers = table.shape[0]
    state = jnp.concatenate([first, second]).reshape(-1)
    smem = pl.BlockSpec(memory_space=pltpu.SMEM)
    counts = (peers * spare + 1, peers * caps[0], peers * caps[1], peers * caps[1])
    out, sent, passed, landed = pl.pallas_call(
        functools.partial(
            route_body, spare=spare, begin=begin, tag=tag, span=span, caps=caps, outward=outward
        ),
        in_specs=[smem, smem, pl.BlockSpec(memory_space=pl.ANY)],
        out_specs=[smem] * 4,
        out_shape=[jax.ShapeDtypeStruct((count,), jnp.int32) for count in counts],
        scratch_shapes=[pltpu.SMEM((2 * peers * peers,), jnp.int32), pltpu.SemaphoreType.DMA],
        name="route",
    )(me[None], table, state)
    return sent.reshape(peers, caps[0]), passed, landed, out[-1]


def tile_keys(quartets, owner_map):
    blocks = owner_map.shape[0]
    row_blocks = jnp.stack([quartets[:, pick] for pick in ROLE_ROW]).reshape(-1)
    col_blocks = jnp.stack([quartets[:, pick] for pick in ROLE_COL]).reshape(-1)
    ids = jnp.arange(blocks, dtype=jnp.int32)
    storage = jnp.sum(jnp.where(row_blocks[:, None] == ids, owner_map, 0), axis=-1)
    return storage * blocks + col_blocks


def earlier(flags):
    ids = jnp.arange(flags.shape[-1])
    ahead = ids[:, None] < ids[None, :]
    return jnp.sum((flags[..., :, None] & ahead).astype(jnp.int32), axis=-2)


def choose(hit, values, axis):
    return jnp.sum(jnp.where(hit, values + 1, 0), axis=axis) - 1


def spilled(flags, values, spare):
    place = earlier(flags)
    hit = flags[..., None] & (place[..., None] == jnp.arange(spare))
    return choose(hit, values[..., None], -2), jnp.sum(flags.astype(jnp.int32), axis=-1)


def permutation_tables(width):
    lanes = width * width
    low = 128 // width
    index = jnp.arange(lanes, dtype=jnp.int32)
    partner = index % width * width + index // width
    swap = (index[:, None] == partner[None, :]).astype(BF16)
    span = jnp.arange(low * 128, dtype=jnp.int32)
    lead, group, inner = span // 128, span % 128 // width, span % width
    partner = group * 128 + lead * width + inner
    trade = (span[None, :] == partner[:, None]).astype(BF16)
    return swap, trade


def slot_count(most):
    for slots in (4, 8, 16):
        if most <= slots:
            return slots
    raise ValueError(most)


def exchange_slots(array):
    return lax.all_to_all(array, AXES, split_axis=0, concat_axis=0, tiled=True)


def slot_count(most):
    for slots in (4, 8, 16):
        if most <= slots:
            return slots
    raise ValueError(most)


def exchange_slots(array, axis=0):
    return lax.all_to_all(array, AXES, split_axis=axis, concat_axis=axis, tiled=True)


def hand_on(slot_of, received, dens):
    peers = slot_of.shape[0]
    lanes = received.shape[-1]
    shape = (peers, dens // RELAY_ROWS, RELAY_ROWS, lanes)
    rows = slot_rows(slot_of, FIRST_SLOTS, dens).reshape(-1)
    return exchange_slots(pick_rows(rows, received.reshape(-1, lanes), shape=shape))


def local(integrals, quartets, density, owner_map):
    rows_dev, blocks, dens, lanes = density.shape
    devices = lax.axis_size(AXES)
    me = lax.axis_index(AXES)
    quartet_count = quartets.shape[0]
    tile_count = ROLES * quartet_count
    span = rows_dev * blocks
    most = 2 * rows_dev
    tag = 1 << (2 * tile_count - 1).bit_length()
    device_ids = jnp.arange(devices, dtype=jnp.int32)
    tile_ids = jnp.arange(tile_count, dtype=jnp.int32)
    density_rows = jnp.transpose(density, (0, 2, 1, 3))
    swap, trade = permutation_tables(math.isqrt(lanes))

    key = tile_keys(quartets, owner_map)
    holder = key // span
    rank = jnp.sum(
        ((holder[:, None] == holder) & (tile_ids[:, None] < tile_ids)).astype(jnp.int32), axis=0
    )
    asked = jnp.sum((holder[:, None] == device_ids).astype(jnp.int32), axis=0)
    spare, spare_count = spilled(rank >= 2 * READ_SLOTS, key * tag + tile_ids, READ_SPARE)
    message = jnp.concatenate([key * 16 + rank, spare, spare_count[None], asked])
    message = jnp.pad(message, (0, -message.shape[0] % 128))
    told = exchange_slots(jnp.broadcast_to(message, (devices,) + message.shape))
    keys, ranks = told[:, :tile_count] // 16, told[:, :tile_count] % 16
    counts = told[:, tile_count + READ_SPARE + 1 :][:, :devices]
    in_second = jnp.minimum(counts, READ_SLOTS)
    in_first = jnp.minimum(counts - in_second, READ_SLOTS)
    caps = (READ_SLOTS, READ_SLOTS)
    extra, passed, landed, read_misses = route(
        me, told, tile_count, READ_SPARE, in_first, in_second, caps, tag, span, False
    )
    most_spare = jnp.max(told[:, tile_count + READ_SPARE])
    read_fits = (read_misses == 0) & (most_spare <= READ_SPARE)

    mine = keys // span == me
    local_tile = keys - me * span

    def requests(begin, slots):
        hit = mine[:, :, None] & (ranks[:, :, None] == jnp.arange(slots) + begin)
        return choose(hit, local_tile[:, :, None], 1)

    wanted = jnp.maximum(requests(READ_SLOTS, READ_SLOTS), extra)
    sent, sent_then = gather_tiles([wanted, requests(0, READ_SLOTS)], density_rows)
    received = exchange_slots(sent)
    early = quartet_count * 5 // 8
    work = 2 * lanes**3 * early
    first, second = regroup(integrals, swap, trade, 0, early, work=work)
    received, first, second = lax.optimization_barrier((received, first, second))
    passed_rows = slot_rows(passed, READ_SLOTS, dens).reshape(devices, READ_SLOTS, -1, 4)
    passed_rows = jnp.transpose(passed_rows, (0, 2, 3, 1)).reshape(-1)
    passed_on = pick_rows(
        passed_rows, received.reshape(-1, lanes), base=sent_then.reshape(-1, lanes)
    )
    received_then = exchange_slots(passed_on.reshape(sent_then.shape))
    keys, ranks, first, second, _ = lax.optimization_barrier((keys, ranks, first, second, passed_on))
    first, second = regroup(integrals, swap, trade, early, quartet_count, (first, second))

    homes = keys // span
    flat = keys.reshape(-1)
    shared = jnp.sum((flat[:, None] == flat).astype(jnp.int32), axis=0) > 1
    shared = shared.reshape(keys.shape)
    together = homes[:, :, None] == homes[:, None, :]
    before = 1 + (shared[:, :, None] & (tile_ids[:, None] < tile_ids)).astype(jnp.int32)
    low_ranks = jnp.where(shared, jnp.sum(jnp.where(together, before, 0), axis=1), -1)
    at_home = homes[:, :, None] == device_ids
    low_counts = jnp.sum((at_home & shared[:, :, None]).astype(jnp.int32), axis=1)
    both_ranks = jnp.concatenate([ranks, low_ranks], axis=1)
    values = keys * tag + tile_ids
    values = jnp.concatenate([values, values + tile_count], axis=1)
    term_list, term_counts = spilled(both_ranks >= FIRST_SLOTS, values, TERM_SPARE)
    term_table = jnp.concatenate([term_list, term_counts[:, None]], axis=1)
    in_use = counts + low_counts
    caps = (FIRST_SLOTS, 1)
    term_extra, term_passed, term_landed, term_misses = route(
        me, term_table, 0, TERM_SPARE, in_use, jnp.zeros_like(in_use), caps, tag, span, True
    )
    term_fits = (term_misses == 0) & (jnp.max(term_counts) <= TERM_SPARE)

    slot_ids = jnp.arange(devices * READ_SLOTS, dtype=jnp.int32)
    via = choose(landed[:, None] == tile_ids, slot_ids[:, None], 0)
    slot = holder * READ_SLOTS + rank
    then_slot = jnp.where(rank < READ_SLOTS, slot, via)
    direct = (rank >= READ_SLOTS) & (rank < 2 * READ_SLOTS)
    now_slot = jnp.where(direct, slot - READ_SLOTS, -1)
    now_rows = pad_rows(slot_rows(now_slot, READ_SLOTS, dens)).reshape(-1, 1)
    then_rows = pad_rows(slot_rows(then_slot, READ_SLOTS, dens)).reshape(-1, 1)
    now_rows, then_rows = lax.optimization_barrier((now_rows, then_rows))

    def read_two_step():
        return pick_rows(
            now_rows,
            received.reshape(-1, lanes),
            swap,
            then_rows,
            received_then.reshape(-1, lanes),
        )

    def read_one_step():
        slots = slot_count(most)
        (whole,) = gather_tiles([requests(0, slots)], density_rows)
        rows = pad_rows(slot_rows(holder * slots + rank, slots, dens))
        return pick_rows(rows, exchange_slots(whole).reshape(-1, lanes), swap)

    tiles = lax.cond(read_fits, read_two_step, read_one_step)
    tiles = tiles.reshape(ROLES, quartet_count, PAD_N, lanes)
    high, low = contract(tiles, integrals, first, second)
    high = high.reshape(tile_count * PAD_N, lanes)
    low = low.reshape(tile_count * PAD_N, lanes)

    def send(term_of_slot, slots):
        per = rows_per_group(slots)
        ids = jnp.arange(dens, dtype=jnp.int32).reshape(1, dens // per, per, 1)
        term = term_of_slot[:, None, None, :]
        rows = jnp.where(term >= 0, term * PAD_N + ids, -1).reshape(-1)
        packed = pack_terms(rows, swap, high, low)
        return exchange_slots(packed.reshape(devices, dens // per, per * slots, lanes))

    to_holder = holder[:, None] == device_ids
    place_ids = jnp.arange(FIRST_SLOTS, dtype=jnp.int32)
    my_low = lax.dynamic_index_in_dim(low_ranks, me, 0, keepdims=False)
    ends = jnp.concatenate([to_holder, to_holder])[:, :, None]
    places = jnp.concatenate([rank, my_low])[:, None, None] == place_ids
    both_ids = jnp.arange(2 * tile_count, dtype=jnp.int32)
    term_of_slot = choose(ends & places, both_ids[:, None, None], 0)
    arrived = send(jnp.maximum(term_of_slot, term_extra), FIRST_SLOTS)
    relayed = hand_on(term_passed, arrived, dens)

    hit = (ranks[:, :, None] == place_ids) | (low_ranks[:, :, None] == place_ids)
    landing = landing_rows(choose(mine[:, :, None] & hit, local_tile[:, :, None], 1), blocks)
    relay_landing = relay_landing_rows(term_landed, FIRST_SLOTS, blocks)
    landing, relay_landing = lax.optimization_barrier((landing, relay_landing))

    def write_two_step():
        return scatter_terms(
            landing, arrived, FIRST_SLOTS, rows_dev, blocks, relay_landing, relayed
        )

    def write_one_step():
        slots = slot_count(most)
        wide = slot_count(2 * slots)
        places = rank[:, None, None] == jnp.arange(slots)
        term_of_slot = choose(to_holder[:, :, None] & places, tile_ids[:, None, None], 0)
        none = jnp.full((devices, wide // 2 - slots), -1, jnp.int32)
        low_term = jnp.where(term_of_slot >= 0, term_of_slot + tile_count, -1)
        whole = send(jnp.concatenate([term_of_slot, none, low_term, none], axis=1), wide)
        wanted = requests(0, slots)
        landing = jnp.concatenate([wanted, none, wanted, none], axis=1)
        return scatter_terms(landing_rows(landing, blocks), whole, wide, rows_dev, blocks)

    fock = lax.cond(term_fits, write_two_step, write_one_step)
    return jnp.transpose(fock, (0, 2, 1, 3))


def solution(mesh):
    return jax.shard_map(
        local,
        mesh=mesh,
        in_specs=(
            P(AXES, None, None),
            P(AXES, None),
            P(AXES, None, None, None),
            P(),
        ),
        out_specs=P(AXES, None, None, None),
        check_vma=False,
    )
```

```python
import functools
import math

import jax
import jax.numpy as jnp
from jax import lax
from jax.experimental import pallas as pl
from jax.experimental.pallas import tpu as pltpu
from jax.sharding import PartitionSpec as P

ORDER = (0, 1, 4, 2, 3, 5)
ROLE_ROW = tuple((0, 0, 1, 1, 2, 3)[role] for role in ORDER)
ROLE_COL = tuple((1, 2, 2, 3, 3, 0)[role] for role in ORDER)
ROLES = 6
PAD_N = 16
ROWS = 16
AXES = ("bra", "ket")
BF16 = jnp.bfloat16
F32 = jnp.float32
VMEM_BYTES = 60 * 1024 * 1024
READ_SLOTS = 2
FIRST_SLOTS = 4
RELAY_ROWS = 4
READ_SPARE = 8
TERM_SPARE = 16


def params(axes=1):
    return pltpu.CompilerParams(
        dimension_semantics=("arbitrary",) * axes, vmem_limit_bytes=VMEM_BYTES
    )


def cost(flops, moved):
    return pl.CostEstimate(flops=int(flops), bytes_accessed=int(moved), transcendentals=0)


def hot_rows(target, width, base=0):
    columns = lax.broadcasted_iota(jnp.int32, (target.shape[0], width), 1) + base
    return jnp.where(columns == target, 1.0, 0.0).astype(BF16)


def hot_columns(target, height, base=0):
    rows = lax.broadcasted_iota(jnp.int32, (height, target.shape[1]), 0) + base
    return jnp.where(rows == target, 1.0, 0.0).astype(BF16)


def dot_nn(left, right):
    return jnp.dot(left, right, preferred_element_type=F32)


def dot_nt(left, right):
    return lax.dot_general(left, right, (((1,), (1,)), ((), ())), preferred_element_type=F32)


def rows_per_group(slots):
    return min(4, ROWS // slots)


def tile_rows(tiles, per, blocks):
    inner = jnp.arange(per, dtype=jnp.int32)[None, :, None]
    rows = (tiles // blocks * (per * blocks) + tiles % blocks)[:, None, :] + inner * blocks
    return jnp.where(tiles[:, None, :] >= 0, rows, -1)


def slot_rows(slot, slots, dens):
    ids = jnp.arange(dens, dtype=jnp.int32)
    per = rows_per_group(slots)
    rows = (slot // slots * (dens * slots) + slot % slots)[..., None]
    rows = rows + ids // per * (per * slots) + ids % per * slots
    return jnp.where(slot[..., None] >= 0, rows, -1)


def pad_rows(rows):
    pad = [(0, 0)] * (rows.ndim - 1) + [(0, PAD_N - rows.shape[-1])]
    return jnp.pad(rows, pad, constant_values=-1).reshape(-1)


def gather_body(target_ref, density_ref, *refs):
    *out_refs, hot_ref = refs
    peers, _, rows, lanes = out_refs[0].shape
    depth = hot_ref.shape[1]

    @pl.when(pl.program_id(0) == 0)
    def _():
        hot_ref[...] = hot_rows(target_ref[...], depth)

    source = density_ref[...].reshape(depth, lanes)
    half = lanes // 2
    for part in range(2):
        span = slice(part * half, (part + 1) * half)
        picked = dot_nn(hot_ref[...], source[:, span]).reshape(-1, rows, half)
        for which, out_ref in enumerate(out_refs):
            mine = picked[which * peers : (which + 1) * peers]
            out_ref[:, 0, :, span] = mine.astype(BF16)


def gather_tiles(wanted, density_rows):
    peers, slots = wanted[0].shape
    rows_dev, dens, blocks, lanes = density_rows.shape
    per = rows_per_group(slots)
    groups, rows = dens // per, per * slots
    depth = rows_dev * per * blocks
    target = jnp.concatenate([tile_rows(each, per, blocks).reshape(-1, 1) for each in wanted])
    out = jax.ShapeDtypeStruct((peers, groups, rows, lanes), BF16)
    return pl.pallas_call(
        gather_body,
        grid=(groups,),
        in_specs=[
            pl.BlockSpec(target.shape, lambda g: (0, 0)),
            pl.BlockSpec((rows_dev, per, blocks, lanes), lambda g: (0, g, 0, 0)),
        ],
        out_specs=[pl.BlockSpec((peers, 1, rows, lanes), lambda g: (0, g, 0, 0))] * len(wanted),
        out_shape=[out] * len(wanted),
        scratch_shapes=[pltpu.VMEM((target.shape[0], depth), BF16)],
        compiler_params=params(),
        name="gather_tiles",
    )(target, density_rows)


def pick_body(*refs, relay, swapped, based):
    if relay:
        relay_target_ref, relayed_ref, *refs = refs
    if based:
        base_ref, *refs = refs
    if swapped:
        swap_ref, *refs = refs
    target_ref, slots_ref, out_ref, total_ref = refs
    step = pl.program_id(0)
    depth = slots_ref.shape[0]

    def fresh():
        total = dot_nn(hot_rows(target_ref[...], depth, step * depth), slots_ref[...])
        if relay:
            hot = hot_rows(relay_target_ref[...], relayed_ref.shape[0])
            total += dot_nn(hot, relayed_ref[...])
        elif based:
            total += base_ref[...].astype(F32)
        return total

    def finish(total):
        if not swapped:
            total = total.reshape(out_ref.shape)
            out_ref[...] = total.astype(BF16)
            return
        half = out_ref.shape[0] // 2
        out_ref[:half, :] = total[:half, :].astype(BF16)
        out_ref[half:, :] = dot_nn(total[half:, :].astype(BF16), swap_ref[...]).astype(BF16)

    if total_ref.shape[0] == 8:
        finish(fresh())
        return

    @pl.when(step == 0)
    def _():
        total_ref[...] = fresh()

    @pl.when(step > 0)
    def _():
        hot = hot_rows(target_ref[...], depth, step * depth)
        total_ref[...] += dot_nn(hot, slots_ref[...])

    @pl.when(step == pl.num_programs(0) - 1)
    def _():
        finish(total_ref[...])


def pick_rows(row_of, received, swap=None, relay_row_of=None, relayed=None, base=None, shape=None):
    depth, lanes = received.shape
    chunk = depth
    if depth > 1536:
        chunk = math.gcd(depth, 128)
    wanted = row_of.shape[0]
    column = pl.BlockSpec((wanted, 1), lambda k: (0, 0))
    specs, operands = [], []
    if relayed is not None:
        specs += [column, pl.BlockSpec(relayed.shape, lambda k: (0, 0))]
        operands += [relay_row_of.reshape(wanted, 1), relayed]
    if base is not None:
        specs += [pl.BlockSpec(base.shape, lambda k: (0, 0))]
        operands += [base]
    if swap is not None:
        specs += [pl.BlockSpec(swap.shape, lambda k: (0, 0))]
        operands += [swap]
    return pl.pallas_call(
        functools.partial(
            pick_body,
            relay=relayed is not None,
            swapped=swap is not None,
            based=base is not None,
        ),
        grid=(depth // chunk,),
        in_specs=[*specs, column, pl.BlockSpec((chunk, lanes), lambda k: (k, 0))],
        out_specs=pl.BlockSpec(shape or (wanted, lanes), lambda k: (0,) * len(shape or (0, 0))),
        out_shape=jax.ShapeDtypeStruct(shape or (wanted, lanes), BF16),
        scratch_shapes=[pltpu.VMEM((8 if chunk == depth else wanted, lanes), F32)],
        compiler_params=params(),
        name="pick_rows",
    )(*operands, row_of.reshape(wanted, 1), received)


def exchange(read_lanes, trade, write, width):
    lanes = width * width
    blocks = lanes // 128
    low = 128 // width
    high = width // low
    for block in range(blocks):
        piece = read_lanes(block).reshape(high, low, width, 128)
        wide = jnp.concatenate(
            [piece[:, part].reshape(high * width, 128) for part in range(low)], axis=1
        )
        traded = dot_nn(wide, trade).astype(BF16)
        for part in range(low):
            group = traded[:, part * 128 : (part + 1) * 128].reshape(high, width, 128)
            for lead in range(high):
                write(block * low + part, lead, group[lead])


def regroup_body(swap_ref, trade_ref, block_ref, *refs, width):
    first_ref, second_ref, swapped_ref = refs[-3:]
    lanes = width * width
    half = lanes // 2
    for part in range(2):
        span = slice(part * half, (part + 1) * half)
        swapped_ref[:, span] = dot_nn(block_ref[0], swap_ref[:, span]).astype(BF16)

    def writer(out_ref):
        def write(row_block, lane_block, value):
            out_ref[
                0,
                row_block * width : (row_block + 1) * width,
                lane_block * 128 : (lane_block + 1) * 128,
            ] = value

        return write

    exchange(
        lambda b: swapped_ref[:, b * 128 : (b + 1) * 128],
        trade_ref[...],
        writer(first_ref),
        width,
    )
    exchange(
        lambda b: block_ref[0, :, b * 128 : (b + 1) * 128],
        trade_ref[...],
        writer(second_ref),
        width,
    )


def regroup(integrals, swap, trade, begin, end, into=(), work=1):
    count, lanes, _ = integrals.shape
    width = math.isqrt(lanes)
    whole = pl.BlockSpec((1, lanes, lanes), lambda i: (i + begin, 0, 0))
    out = jax.ShapeDtypeStruct(integrals.shape, BF16)
    return pl.pallas_call(
        functools.partial(regroup_body, width=width),
        grid=(end - begin,),
        in_specs=[
            pl.BlockSpec(swap.shape, lambda i: (0, 0)),
            pl.BlockSpec(trade.shape, lambda i: (0, 0)),
            whole,
            *[pl.BlockSpec(memory_space=pl.ANY)] * len(into),
        ],
        out_specs=[whole, whole],
        out_shape=[out, out],
        scratch_shapes=[pltpu.VMEM((lanes, lanes), BF16)],
        input_output_aliases={3 + which: which for which in range(len(into))},
        compiler_params=params(),
        cost_estimate=cost(work, work),
        name="regroup",
    )(swap, trade, integrals, *into)


def contract_body(tiles_ref, block_ref, first_ref, second_ref, high_ref, low_ref):
    block, first, second = block_ref[0], first_ref[0], second_ref[0]

    def tile(role):
        return tiles_ref[ORDER.index(role), 0]

    def put(role, term):
        top = term.astype(BF16)
        role = ORDER.index(role)
        high_ref[role, 0] = top
        low_ref[role, 0] = (term - top.astype(F32)).astype(BF16)

    put(0, 2.0 * dot_nt(tile(4), block))
    put(4, 2.0 * dot_nn(tile(0), block))
    put(1, -dot_nn(tile(3), first))
    put(3, -dot_nt(tile(1), first))
    put(2, -dot_nt(tile(5), second))
    put(5, -dot_nn(tile(2), second))


def contract(tiles, integrals, first, second):
    count, lanes, _ = integrals.shape
    whole = pl.BlockSpec((1, lanes, lanes), lambda i: (i, 0, 0))
    part = pl.BlockSpec((ROLES, 1, PAD_N, lanes), lambda i: (0, i, 0, 0))
    out = jax.ShapeDtypeStruct((ROLES, count, PAD_N, lanes), BF16)
    return pl.pallas_call(
        contract_body,
        grid=(count,),
        in_specs=[part, whole, whole, whole],
        out_specs=[part, part],
        out_shape=[out, out],
        compiler_params=params(),
        name="contract",
    )(tiles, integrals, first, second)


def pack_body(target_ref, swap_ref, high_ref, low_ref, out_ref, terms_ref):
    half = high_ref.shape[0]

    @pl.when(pl.program_id(0) == 0)
    def _():
        mid = half // 2
        for which, source in enumerate((high_ref, low_ref)):
            start = which * half
            terms_ref[start : start + mid, :] = source[:mid, :]
            swapped = dot_nn(source[mid:, :], swap_ref[...]).astype(BF16)
            terms_ref[start + mid : start + half, :] = swapped

    out_ref[...] = dot_nn(hot_rows(target_ref[...], 2 * half), terms_ref[...]).astype(BF16)


def pack_terms(row_of, swap, high, low):
    count = row_of.shape[0]
    half, lanes = high.shape
    chunk = math.gcd(count, 256 if count <= 2048 else 64)
    return pl.pallas_call(
        pack_body,
        grid=(count // chunk,),
        in_specs=[
            pl.BlockSpec((chunk, 1), lambda k: (k, 0)),
            pl.BlockSpec((lanes, lanes), lambda k: (0, 0)),
            pl.BlockSpec((half, lanes), lambda k: (0, 0)),
            pl.BlockSpec((half, lanes), lambda k: (0, 0)),
        ],
        out_specs=pl.BlockSpec((chunk, lanes), lambda k: (k, 0)),
        out_shape=jax.ShapeDtypeStruct((count, lanes), BF16),
        scratch_shapes=[pltpu.VMEM((2 * half, lanes), BF16)],
        compiler_params=params(),
        name="pack_terms",
    )(row_of.reshape(count, 1), swap, high, low)


def scatter_body(*refs, relay):
    if relay:
        relay_target_ref, relayed_ref, *refs, relay_hot_ref = refs
    target_ref, slots_ref, out_ref, hot_ref = refs
    rows_dev, per, blocks, lanes = out_ref.shape
    height = per * blocks
    depth = hot_ref.shape[1]

    @pl.when(pl.program_id(0) == 0)
    def _():
        hot_ref[...] = hot_columns(target_ref[...], rows_dev * height)
        if relay:
            for part in range(relay_hot_ref.shape[0]):
                target = relay_target_ref[part : part + 1, :]
                relay_hot_ref[part] = hot_columns(target, rows_dev * height)

    slots = slots_ref[...].reshape(depth, lanes)
    for row in range(rows_dev):
        span = slice(row * height, (row + 1) * height)
        total = dot_nn(hot_ref[span, :], slots)
        if relay:
            part = pl.program_id(0) % relay_hot_ref.shape[0]
            relayed = relayed_ref[...].astype(F32).reshape(-1, lanes).astype(BF16)
            total += dot_nn(relay_hot_ref[part, span, :], relayed)
        out_ref[row] = total.astype(BF16).reshape(per, blocks, lanes)


def scatter_split(slots):
    return max(slots, 8)


def landing_rows(landing, blocks):
    slots = landing.shape[1]
    return tile_rows(landing, scatter_split(slots) // slots, blocks).reshape(1, -1)


def relay_landing_rows(landing, slots, blocks):
    per = scatter_split(slots) // slots
    inner = jnp.arange(RELAY_ROWS, dtype=jnp.int32)
    rows = (landing // blocks * (per * blocks) + landing % blocks)[:, None] + inner % per * blocks
    kind = jnp.arange(RELAY_ROWS // per, dtype=jnp.int32)[:, None, None]
    rows = jnp.where((landing[:, None] >= 0) & (inner // per == kind), rows, -1)
    return rows.reshape(kind.shape[0], -1)


def scatter_terms(target, arrived, slots, rows_dev, blocks, relay_target=None, relayed=None):
    peers, groups, rows, lanes = arrived.shape
    split = scatter_split(slots)
    steps, per = groups * rows // split, split // slots
    high = rows_dev * per * blocks
    specs, operands = [], []
    scratch = [pltpu.VMEM((high, peers * split), BF16)]
    if relayed is not None:
        depth = peers * RELAY_ROWS
        kinds = relay_target.shape[0]
        specs = [
            pl.BlockSpec((kinds, depth), lambda g: (0, 0)),
            pl.BlockSpec((peers, 1, RELAY_ROWS, lanes), lambda g: (0, g // kinds, 0, 0)),
        ]
        operands = [relay_target, relayed]
        scratch += [pltpu.VMEM((kinds, high, depth), BF16)]
    return pl.pallas_call(
        functools.partial(scatter_body, relay=relayed is not None),
        grid=(steps,),
        in_specs=[
            *specs,
            pl.BlockSpec((1, peers * split), lambda g: (0, 0)),
            pl.BlockSpec((peers, 1, split, lanes), lambda g: (0, g, 0, 0)),
        ],
        out_specs=pl.BlockSpec((rows_dev, per, blocks, lanes), lambda g: (0, g, 0, 0)),
        out_shape=jax.ShapeDtypeStruct((rows_dev, steps * per, blocks, lanes), BF16),
        scratch_shapes=scratch,
        compiler_params=params(),
        name="scatter_terms",
    )(*operands, target, arrived.reshape(peers, steps, split, lanes))


def route_body(
    me_ref, list_ref, state_hbm, out_ref, sent_ref, passed_ref, landed_ref, state_ref, sem,
    *, spare, begin, tag, span, caps, outward
):
    peers = list_ref.shape[0]
    second = peers * peers
    copy = pltpu.make_async_copy(state_hbm, state_ref, sem)
    copy.start()
    me = me_ref[0]

    for ref in (sent_ref, passed_ref, landed_ref):

        def clear(index, carry, ref=ref):
            ref[index] = -1
            return carry

        lax.fori_loop(0, ref.shape[0], clear, 0, unroll=8)
    copy.wait()

    def first_at(source, middle):
        return source * peers + middle if outward else middle * peers + source

    def one(row, place, failed):
        value = list_ref[row, begin + place]
        other = value // (span * tag)
        source, last = (row, other) if outward else (other, row)

        def search(carry):
            tries, middle, found = carry
            full = state_ref[first_at(source, middle)] >= caps[0]
            taken = state_ref[second + last * peers + middle] >= caps[1]
            found = jnp.where(full | taken, found, middle)
            following = jnp.where(middle + 1 == peers, 0, middle + 1)
            return tries + 1, following, found

        start = source + last
        start = jnp.where(start >= peers, start - peers, start)
        _, _, found = lax.while_loop(
            lambda carry: (carry[0] < peers) & (carry[2] < 0),
            search,
            (jnp.int32(0), start, jnp.int32(-1)),
        )
        index = row * spare + place
        out_ref[index] = -1

        @pl.when(found >= 0)
        def _():
            first_state, then_state = first_at(source, found), second + last * peers + found
            first, then = state_ref[first_state], state_ref[then_state]
            out_ref[index] = found * caps[1] + then
            state_ref[first_state] = first + 1
            state_ref[then_state] = then + 1
            tile = value // tag - me * span

            @pl.when(source == me)
            def _():
                sent_ref[found * caps[0] + first] = value % tag if outward else tile

            @pl.when(found == me)
            def _():
                passed_ref[last * caps[1] + then] = source * caps[0] + first

            @pl.when(last == me)
            def _():
                landed_ref[found * caps[1] + then] = tile if outward else value % tag

        return failed + jnp.where(found < 0, 1, 0)

    def each(row, failed):
        count = jnp.minimum(list_ref[row, begin + spare], spare)
        return lax.fori_loop(0, count, functools.partial(lambda p, f, r: one(r, p, f), r=row), failed)

    out_ref[peers * spare] = lax.fori_loop(0, peers, each, jnp.int32(0))


def route(me, table, begin, spare, first, second, caps, tag, span, outward):
    peers = table.shape[0]
    state = jnp.concatenate([first, second]).reshape(-1)
    smem = pl.BlockSpec(memory_space=pltpu.SMEM)
    counts = (peers * spare + 1, peers * caps[0], peers * caps[1], peers * caps[1])
    out, sent, passed, landed = pl.pallas_call(
        functools.partial(
            route_body, spare=spare, begin=begin, tag=tag, span=span, caps=caps, outward=outward
        ),
        in_specs=[smem, smem, pl.BlockSpec(memory_space=pl.ANY)],
        out_specs=[smem] * 4,
        out_shape=[jax.ShapeDtypeStruct((count,), jnp.int32) for count in counts],
        scratch_shapes=[pltpu.SMEM((2 * peers * peers,), jnp.int32), pltpu.SemaphoreType.DMA],
        name="route",
    )(me[None], table, state)
    return sent.reshape(peers, caps[0]), passed, landed, out[-1]


def tile_keys(quartets, owner_map):
    blocks = owner_map.shape[0]
    row_blocks = jnp.stack([quartets[:, pick] for pick in ROLE_ROW]).reshape(-1)
    col_blocks = jnp.stack([quartets[:, pick] for pick in ROLE_COL]).reshape(-1)
    ids = jnp.arange(blocks, dtype=jnp.int32)
    storage = jnp.sum(jnp.where(row_blocks[:, None] == ids, owner_map, 0), axis=-1)
    return storage * blocks + col_blocks


def earlier(flags):
    ids = jnp.arange(flags.shape[-1])
    ahead = ids[:, None] < ids[None, :]
    return jnp.sum((flags[..., :, None] & ahead).astype(jnp.int32), axis=-2)


def choose(hit, values, axis):
    return jnp.sum(jnp.where(hit, values + 1, 0), axis=axis) - 1


def spilled(flags, values, spare):
    place = earlier(flags)
    hit = flags[..., None] & (place[..., None] == jnp.arange(spare))
    return choose(hit, values[..., None], -2), jnp.sum(flags.astype(jnp.int32), axis=-1)


def permutation_tables(width):
    lanes = width * width
    low = 128 // width
    index = jnp.arange(lanes, dtype=jnp.int32)
    partner = index % width * width + index // width
    swap = (index[:, None] == partner[None, :]).astype(BF16)
    span = jnp.arange(low * 128, dtype=jnp.int32)
    lead, group, inner = span // 128, span % 128 // width, span % width
    partner = group * 128 + lead * width + inner
    trade = (span[None, :] == partner[:, None]).astype(BF16)
    return swap, trade


def slot_count(most):
    for slots in (4, 8, 16):
        if most <= slots:
            return slots
    raise ValueError(most)


def exchange_slots(array):
    return lax.all_to_all(array, AXES, split_axis=0, concat_axis=0, tiled=True)


def slot_count(most):
    for slots in (4, 8, 16):
        if most <= slots:
            return slots
    raise ValueError(most)


def exchange_slots(array, axis=0):
    return lax.all_to_all(array, AXES, split_axis=axis, concat_axis=axis, tiled=True)


def hand_on(slot_of, received, dens):
    peers = slot_of.shape[0]
    lanes = received.shape[-1]
    shape = (peers, dens // RELAY_ROWS, RELAY_ROWS, lanes)
    rows = slot_rows(slot_of, FIRST_SLOTS, dens).reshape(-1)
    return exchange_slots(pick_rows(rows, received.reshape(-1, lanes), shape=shape))


def local(integrals, quartets, density, owner_map):
    rows_dev, blocks, dens, lanes = density.shape
    devices = lax.axis_size(AXES)
    me = lax.axis_index(AXES)
    quartet_count = quartets.shape[0]
    tile_count = ROLES * quartet_count
    span = rows_dev * blocks
    most = 2 * rows_dev
    tag = 1 << (2 * tile_count - 1).bit_length()
    device_ids = jnp.arange(devices, dtype=jnp.int32)
    tile_ids = jnp.arange(tile_count, dtype=jnp.int32)
    density_rows = jnp.transpose(density, (0, 2, 1, 3))
    swap, trade = permutation_tables(math.isqrt(lanes))

    key = tile_keys(quartets, owner_map)
    holder = key // span
    rank = jnp.sum(
        ((holder[:, None] == holder) & (tile_ids[:, None] < tile_ids)).astype(jnp.int32), axis=0
    )
    asked = jnp.sum((holder[:, None] == device_ids).astype(jnp.int32), axis=0)
    spare, spare_count = spilled(rank >= 2 * READ_SLOTS, key * tag + tile_ids, READ_SPARE)
    message = jnp.concatenate([key * 16 + rank, spare, spare_count[None], asked])
    message = jnp.pad(message, (0, -message.shape[0] % 128))
    told = exchange_slots(jnp.broadcast_to(message, (devices,) + message.shape))
    keys, ranks = told[:, :tile_count] // 16, told[:, :tile_count] % 16
    counts = told[:, tile_count + READ_SPARE + 1 :][:, :devices]
    in_second = jnp.minimum(counts, READ_SLOTS)
    in_first = jnp.minimum(counts - in_second, READ_SLOTS)
    caps = (READ_SLOTS, READ_SLOTS)
    extra, passed, landed, read_misses = route(
        me, told, tile_count, READ_SPARE, in_first, in_second, caps, tag, span, False
    )
    most_spare = jnp.max(told[:, tile_count + READ_SPARE])
    read_fits = (read_misses == 0) & (most_spare <= READ_SPARE)

    mine = keys // span == me
    local_tile = keys - me * span

    def requests(begin, slots):
        hit = mine[:, :, None] & (ranks[:, :, None] == jnp.arange(slots) + begin)
        return choose(hit, local_tile[:, :, None], 1)

    wanted = jnp.maximum(requests(READ_SLOTS, READ_SLOTS), extra)
    sent, sent_then = gather_tiles([wanted, requests(0, READ_SLOTS)], density_rows)
    received = exchange_slots(sent)
    early = quartet_count * 5 // 8
    work = 2 * lanes**3 * early
    first, second = regroup(integrals, swap, trade, 0, early, work=work)
    received, first, second = lax.optimization_barrier((received, first, second))
    passed_rows = slot_rows(passed, READ_SLOTS, dens).reshape(devices, READ_SLOTS, -1, 4)
    passed_rows = jnp.transpose(passed_rows, (0, 2, 3, 1)).reshape(-1)
    passed_on = pick_rows(
        passed_rows, received.reshape(-1, lanes), base=sent_then.reshape(-1, lanes)
    )
    received_then = exchange_slots(passed_on.reshape(sent_then.shape))
    keys, ranks, first, second, _ = lax.optimization_barrier((keys, ranks, first, second, passed_on))
    first, second = regroup(integrals, swap, trade, early, quartet_count, (first, second))

    homes = keys // span
    flat = keys.reshape(-1)
    shared = jnp.sum((flat[:, None] == flat).astype(jnp.int32), axis=0) > 1
    shared = shared.reshape(keys.shape)
    together = homes[:, :, None] == homes[:, None, :]
    before = 1 + (shared[:, :, None] & (tile_ids[:, None] < tile_ids)).astype(jnp.int32)
    low_ranks = jnp.where(shared, jnp.sum(jnp.where(together, before, 0), axis=1), -1)
    at_home = homes[:, :, None] == device_ids
    low_counts = jnp.sum((at_home & shared[:, :, None]).astype(jnp.int32), axis=1)
    both_ranks = jnp.concatenate([ranks, low_ranks], axis=1)
    values = keys * tag + tile_ids
    values = jnp.concatenate([values, values + tile_count], axis=1)
    term_list, term_counts = spilled(both_ranks >= FIRST_SLOTS, values, TERM_SPARE)
    term_table = jnp.concatenate([term_list, term_counts[:, None]], axis=1)
    in_use = counts + low_counts
    caps = (FIRST_SLOTS, 1)
    term_extra, term_passed, term_landed, term_misses = route(
        me, term_table, 0, TERM_SPARE, in_use, jnp.zeros_like(in_use), caps, tag, span, True
    )
    term_fits = (term_misses == 0) & (jnp.max(term_counts) <= TERM_SPARE)

    slot_ids = jnp.arange(devices * READ_SLOTS, dtype=jnp.int32)
    via = choose(landed[:, None] == tile_ids, slot_ids[:, None], 0)
    slot = holder * READ_SLOTS + rank
    then_slot = jnp.where(rank < READ_SLOTS, slot, via)
    direct = (rank >= READ_SLOTS) & (rank < 2 * READ_SLOTS)
    now_slot = jnp.where(direct, slot - READ_SLOTS, -1)
    now_rows = pad_rows(slot_rows(now_slot, READ_SLOTS, dens)).reshape(-1, 1)
    then_rows = pad_rows(slot_rows(then_slot, READ_SLOTS, dens)).reshape(-1, 1)
    now_rows, then_rows = lax.optimization_barrier((now_rows, then_rows))

    def read_two_step():
        return pick_rows(
            now_rows,
            received.reshape(-1, lanes),
            swap,
            then_rows,
            received_then.reshape(-1, lanes),
        )

    def read_one_step():
        slots = slot_count(most)
        (whole,) = gather_tiles([requests(0, slots)], density_rows)
        rows = pad_rows(slot_rows(holder * slots + rank, slots, dens))
        return pick_rows(rows, exchange_slots(whole).reshape(-1, lanes), swap)

    tiles = lax.cond(read_fits, read_two_step, read_one_step)
    tiles = tiles.reshape(ROLES, quartet_count, PAD_N, lanes)
    high, low = contract(tiles, integrals, first, second)
    high = high.reshape(tile_count * PAD_N, lanes)
    low = low.reshape(tile_count * PAD_N, lanes)

    def send(term_of_slot, slots):
        per = rows_per_group(slots)
        ids = jnp.arange(dens, dtype=jnp.int32).reshape(1, dens // per, per, 1)
        term = term_of_slot[:, None, None, :]
        rows = jnp.where(term >= 0, term * PAD_N + ids, -1).reshape(-1)
        packed = pack_terms(rows, swap, high, low)
        return exchange_slots(packed.reshape(devices, dens // per, per * slots, lanes))

    to_holder = holder[:, None] == device_ids
    place_ids = jnp.arange(FIRST_SLOTS, dtype=jnp.int32)
    my_low = lax.dynamic_index_in_dim(low_ranks, me, 0, keepdims=False)
    ends = jnp.concatenate([to_holder, to_holder])[:, :, None]
    places = jnp.concatenate([rank, my_low])[:, None, None] == place_ids
    both_ids = jnp.arange(2 * tile_count, dtype=jnp.int32)
    term_of_slot = choose(ends & places, both_ids[:, None, None], 0)
    arrived = send(jnp.maximum(term_of_slot, term_extra), FIRST_SLOTS)
    relayed = hand_on(term_passed, arrived, dens)

    hit = (ranks[:, :, None] == place_ids) | (low_ranks[:, :, None] == place_ids)
    landing = landing_rows(choose(mine[:, :, None] & hit, local_tile[:, :, None], 1), blocks)
    relay_landing = relay_landing_rows(term_landed, FIRST_SLOTS, blocks)
    landing, relay_landing = lax.optimization_barrier((landing, relay_landing))

    def write_two_step():
        return scatter_terms(
            landing, arrived, FIRST_SLOTS, rows_dev, blocks, relay_landing, relayed
        )

    def write_one_step():
        slots = slot_count(most)
        wide = slot_count(2 * slots)
        places = rank[:, None, None] == jnp.arange(slots)
        term_of_slot = choose(to_holder[:, :, None] & places, tile_ids[:, None, None], 0)
        none = jnp.full((devices, wide // 2 - slots), -1, jnp.int32)
        low_term = jnp.where(term_of_slot >= 0, term_of_slot + tile_count, -1)
        whole = send(jnp.concatenate([term_of_slot, none, low_term, none], axis=1), wide)
        wanted = requests(0, slots)
        landing = jnp.concatenate([wanted, none, wanted, none], axis=1)
        return scatter_terms(landing_rows(landing, blocks), whole, wide, rows_dev, blocks)

    fock = lax.cond(term_fits, write_two_step, write_one_step)
    return jnp.transpose(fock, (0, 2, 1, 3))


def solution(mesh):
    return jax.shard_map(
        local,
        mesh=mesh,
        in_specs=(
            P(AXES, None, None),
            P(AXES, None),
            P(AXES, None, None, None),
            P(),
        ),
        out_specs=P(AXES, None, None, None),
        check_vma=False,
    )
```

```python
import functools
import math

import jax
import jax.numpy as jnp
from jax import lax
from jax.experimental import pallas as pl
from jax.experimental.pallas import tpu as pltpu
from jax.sharding import PartitionSpec as P

ORDER = (0, 1, 4, 2, 3, 5)
ROLE_ROW = tuple((0, 0, 1, 1, 2, 3)[role] for role in ORDER)
ROLE_COL = tuple((1, 2, 2, 3, 3, 0)[role] for role in ORDER)
ROLES = 6
PAD_N = 16
ROWS = 16
AXES = ("bra", "ket")
BF16 = jnp.bfloat16
F32 = jnp.float32
VMEM_BYTES = 60 * 1024 * 1024
READ_SLOTS = 2
FIRST_SLOTS = 4
RELAY_ROWS = 4
READ_SPARE = 8
TERM_SPARE = 16


def params(axes=1):
    return pltpu.CompilerParams(
        dimension_semantics=("arbitrary",) * axes, vmem_limit_bytes=VMEM_BYTES
    )


def cost(flops, moved):
    return pl.CostEstimate(flops=int(flops), bytes_accessed=int(moved), transcendentals=0)


def hot_rows(target, width, base=0):
    columns = lax.broadcasted_iota(jnp.int32, (target.shape[0], width), 1) + base
    return jnp.where(columns == target, 1.0, 0.0).astype(BF16)


def hot_columns(target, height, base=0):
    rows = lax.broadcasted_iota(jnp.int32, (height, target.shape[1]), 0) + base
    return jnp.where(rows == target, 1.0, 0.0).astype(BF16)


def dot_nn(left, right):
    return jnp.dot(left, right, preferred_element_type=F32)


def dot_nt(left, right):
    return lax.dot_general(left, right, (((1,), (1,)), ((), ())), preferred_element_type=F32)


def rows_per_group(slots):
    return min(4, ROWS // slots)


def tile_rows(tiles, per, blocks):
    inner = jnp.arange(per, dtype=jnp.int32)[None, :, None]
    rows = (tiles // blocks * (per * blocks) + tiles % blocks)[:, None, :] + inner * blocks
    return jnp.where(tiles[:, None, :] >= 0, rows, -1)


def slot_rows(slot, slots, dens):
    ids = jnp.arange(dens, dtype=jnp.int32)
    per = rows_per_group(slots)
    rows = (slot // slots * (dens * slots) + slot % slots)[..., None]
    rows = rows + ids // per * (per * slots) + ids % per * slots
    return jnp.where(slot[..., None] >= 0, rows, -1)


def pad_rows(rows):
    pad = [(0, 0)] * (rows.ndim - 1) + [(0, PAD_N - rows.shape[-1])]
    return jnp.pad(rows, pad, constant_values=-1).reshape(-1)


def gather_body(target_ref, density_ref, *refs):
    *out_refs, hot_ref = refs
    peers, _, rows, lanes = out_refs[0].shape
    depth = hot_ref.shape[1]

    @pl.when(pl.program_id(0) == 0)
    def _():
        hot_ref[...] = hot_rows(target_ref[...], depth)

    source = density_ref[...].reshape(depth, lanes)
    half = lanes // 2
    for part in range(2):
        span = slice(part * half, (part + 1) * half)
        picked = dot_nn(hot_ref[...], source[:, span]).reshape(-1, rows, half)
        for which, out_ref in enumerate(out_refs):
            mine = picked[which * peers : (which + 1) * peers]
            out_ref[:, 0, :, span] = mine.astype(BF16)


def gather_tiles(wanted, density_rows):
    peers, slots = wanted[0].shape
    rows_dev, dens, blocks, lanes = density_rows.shape
    per = rows_per_group(slots)
    groups, rows = dens // per, per * slots
    depth = rows_dev * per * blocks
    target = jnp.concatenate([tile_rows(each, per, blocks).reshape(-1, 1) for each in wanted])
    out = jax.ShapeDtypeStruct((peers, groups, rows, lanes), BF16)
    return pl.pallas_call(
        gather_body,
        grid=(groups,),
        in_specs=[
            pl.BlockSpec(target.shape, lambda g: (0, 0)),
            pl.BlockSpec((rows_dev, per, blocks, lanes), lambda g: (0, g, 0, 0)),
        ],
        out_specs=[pl.BlockSpec((peers, 1, rows, lanes), lambda g: (0, g, 0, 0))] * len(wanted),
        out_shape=[out] * len(wanted),
        scratch_shapes=[pltpu.VMEM((target.shape[0], depth), BF16)],
        compiler_params=params(),
        name="gather_tiles",
    )(target, density_rows)


def pick_body(*refs, relay, swapped, based):
    if relay:
        relay_target_ref, relayed_ref, *refs = refs
    if based:
        base_ref, *refs = refs
    if swapped:
        swap_ref, *refs = refs
    target_ref, slots_ref, out_ref, total_ref = refs
    step = pl.program_id(0)
    depth = slots_ref.shape[0]

    def fresh():
        total = dot_nn(hot_rows(target_ref[...], depth, step * depth), slots_ref[...])
        if relay:
            hot = hot_rows(relay_target_ref[...], relayed_ref.shape[0])
            total += dot_nn(hot, relayed_ref[...])
        elif based:
            total += base_ref[...].astype(F32)
        return total

    def finish(total):
        if not swapped:
            total = total.reshape(out_ref.shape)
            out_ref[...] = total.astype(BF16)
            return
        half = out_ref.shape[0] // 2
        out_ref[:half, :] = total[:half, :].astype(BF16)
        out_ref[half:, :] = dot_nn(total[half:, :].astype(BF16), swap_ref[...]).astype(BF16)

    if total_ref.shape[0] == 8:
        finish(fresh())
        return

    @pl.when(step == 0)
    def _():
        total_ref[...] = fresh()

    @pl.when(step > 0)
    def _():
        hot = hot_rows(target_ref[...], depth, step * depth)
        total_ref[...] += dot_nn(hot, slots_ref[...])

    @pl.when(step == pl.num_programs(0) - 1)
    def _():
        finish(total_ref[...])


def pick_rows(row_of, received, swap=None, relay_row_of=None, relayed=None, base=None, shape=None):
    depth, lanes = received.shape
    chunk = depth
    if depth > 1536:
        chunk = math.gcd(depth, 128)
    wanted = row_of.shape[0]
    column = pl.BlockSpec((wanted, 1), lambda k: (0, 0))
    specs, operands = [], []
    if relayed is not None:
        specs += [column, pl.BlockSpec(relayed.shape, lambda k: (0, 0))]
        operands += [relay_row_of.reshape(wanted, 1), relayed]
    if base is not None:
        specs += [pl.BlockSpec(base.shape, lambda k: (0, 0))]
        operands += [base]
    if swap is not None:
        specs += [pl.BlockSpec(swap.shape, lambda k: (0, 0))]
        operands += [swap]
    return pl.pallas_call(
        functools.partial(
            pick_body,
            relay=relayed is not None,
            swapped=swap is not None,
            based=base is not None,
        ),
        grid=(depth // chunk,),
        in_specs=[*specs, column, pl.BlockSpec((chunk, lanes), lambda k: (k, 0))],
        out_specs=pl.BlockSpec(shape or (wanted, lanes), lambda k: (0,) * len(shape or (0, 0))),
        out_shape=jax.ShapeDtypeStruct(shape or (wanted, lanes), BF16),
        scratch_shapes=[pltpu.VMEM((8 if chunk == depth else wanted, lanes), F32)],
        compiler_params=params(),
        name="pick_rows",
    )(*operands, row_of.reshape(wanted, 1), received)


def exchange(read_lanes, trade, write, width):
    lanes = width * width
    blocks = lanes // 128
    low = 128 // width
    high = width // low
    for block in range(blocks):
        piece = read_lanes(block).reshape(high, low, width, 128)
        wide = jnp.concatenate(
            [piece[:, part].reshape(high * width, 128) for part in range(low)], axis=1
        )
        traded = dot_nn(wide, trade).astype(BF16)
        for part in range(low):
            group = traded[:, part * 128 : (part + 1) * 128].reshape(high, width, 128)
            for lead in range(high):
                write(block * low + part, lead, group[lead])


def regroup_body(swap_ref, trade_ref, block_ref, *refs, width):
    first_ref, second_ref, swapped_ref = refs[-3:]
    lanes = width * width
    half = lanes // 2
    for part in range(2):
        span = slice(part * half, (part + 1) * half)
        swapped_ref[:, span] = dot_nn(block_ref[0], swap_ref[:, span]).astype(BF16)

    def writer(out_ref):
        def write(row_block, lane_block, value):
            out_ref[
                0,
                row_block * width : (row_block + 1) * width,
                lane_block * 128 : (lane_block + 1) * 128,
            ] = value

        return write

    exchange(
        lambda b: swapped_ref[:, b * 128 : (b + 1) * 128],
        trade_ref[...],
        writer(first_ref),
        width,
    )
    exchange(
        lambda b: block_ref[0, :, b * 128 : (b + 1) * 128],
        trade_ref[...],
        writer(second_ref),
        width,
    )


def regroup(integrals, swap, trade, begin, end, into=(), work=1):
    count, lanes, _ = integrals.shape
    width = math.isqrt(lanes)
    whole = pl.BlockSpec((1, lanes, lanes), lambda i: (i + begin, 0, 0))
    out = jax.ShapeDtypeStruct(integrals.shape, BF16)
    return pl.pallas_call(
        functools.partial(regroup_body, width=width),
        grid=(end - begin,),
        in_specs=[
            pl.BlockSpec(swap.shape, lambda i: (0, 0)),
            pl.BlockSpec(trade.shape, lambda i: (0, 0)),
            whole,
            *[pl.BlockSpec(memory_space=pl.ANY)] * len(into),
        ],
        out_specs=[whole, whole],
        out_shape=[out, out],
        scratch_shapes=[pltpu.VMEM((lanes, lanes), BF16)],
        input_output_aliases={3 + which: which for which in range(len(into))},
        compiler_params=params(),
        cost_estimate=cost(work, work),
        name="regroup",
    )(swap, trade, integrals, *into)


def contract_body(tiles_ref, block_ref, first_ref, second_ref, high_ref, low_ref):
    block, first, second = block_ref[0], first_ref[0], second_ref[0]

    def tile(role):
        return tiles_ref[ORDER.index(role), 0]

    def put(role, term):
        top = term.astype(BF16)
        role = ORDER.index(role)
        high_ref[role, 0] = top
        low_ref[role, 0] = (term - top.astype(F32)).astype(BF16)

    put(0, 2.0 * dot_nt(tile(4), block))
    put(4, 2.0 * dot_nn(tile(0), block))
    put(1, -dot_nn(tile(3), first))
    put(3, -dot_nt(tile(1), first))
    put(2, -dot_nt(tile(5), second))
    put(5, -dot_nn(tile(2), second))


def contract(tiles, integrals, first, second):
    count, lanes, _ = integrals.shape
    whole = pl.BlockSpec((1, lanes, lanes), lambda i: (i, 0, 0))
    part = pl.BlockSpec((ROLES, 1, PAD_N, lanes), lambda i: (0, i, 0, 0))
    out = jax.ShapeDtypeStruct((ROLES, count, PAD_N, lanes), BF16)
    return pl.pallas_call(
        contract_body,
        grid=(count,),
        in_specs=[part, whole, whole, whole],
        out_specs=[part, part],
        out_shape=[out, out],
        compiler_params=params(),
        name="contract",
    )(tiles, integrals, first, second)


def pack_body(target_ref, swap_ref, high_ref, low_ref, out_ref, terms_ref):
    half = high_ref.shape[0]

    @pl.when(pl.program_id(0) == 0)
    def _():
        mid = half // 2
        for which, source in enumerate((high_ref, low_ref)):
            start = which * half
            terms_ref[start : start + mid, :] = source[:mid, :]
            swapped = dot_nn(source[mid:, :], swap_ref[...]).astype(BF16)
            terms_ref[start + mid : start + half, :] = swapped

    out_ref[...] = dot_nn(hot_rows(target_ref[...], 2 * half), terms_ref[...]).astype(BF16)


def pack_terms(row_of, swap, high, low):
    count = row_of.shape[0]
    half, lanes = high.shape
    chunk = math.gcd(count, 512 if count <= 2048 else 64)
    return pl.pallas_call(
        pack_body,
        grid=(count // chunk,),
        in_specs=[
            pl.BlockSpec((chunk, 1), lambda k: (k, 0)),
            pl.BlockSpec((lanes, lanes), lambda k: (0, 0)),
            pl.BlockSpec((half, lanes), lambda k: (0, 0)),
            pl.BlockSpec((half, lanes), lambda k: (0, 0)),
        ],
        out_specs=pl.BlockSpec((chunk, lanes), lambda k: (k, 0)),
        out_shape=jax.ShapeDtypeStruct((count, lanes), BF16),
        scratch_shapes=[pltpu.VMEM((2 * half, lanes), BF16)],
        compiler_params=params(),
        name="pack_terms",
    )(row_of.reshape(count, 1), swap, high, low)


def scatter_body(*refs, relay):
    if relay:
        relay_target_ref, relayed_ref, *refs, relay_hot_ref = refs
    target_ref, slots_ref, out_ref, hot_ref = refs
    rows_dev, per, blocks, lanes = out_ref.shape
    height = per * blocks
    depth = hot_ref.shape[1]

    @pl.when(pl.program_id(0) == 0)
    def _():
        hot_ref[...] = hot_columns(target_ref[...], rows_dev * height)
        if relay:
            for part in range(relay_hot_ref.shape[0]):
                target = relay_target_ref[part : part + 1, :]
                relay_hot_ref[part] = hot_columns(target, rows_dev * height)

    slots = slots_ref[...].reshape(depth, lanes)
    for row in range(rows_dev):
        span = slice(row * height, (row + 1) * height)
        total = dot_nn(hot_ref[span, :], slots)
        if relay:
            part = pl.program_id(0) % relay_hot_ref.shape[0]
            relayed = relayed_ref[...].astype(F32).reshape(-1, lanes).astype(BF16)
            total += dot_nn(relay_hot_ref[part, span, :], relayed)
        out_ref[row] = total.astype(BF16).reshape(per, blocks, lanes)


def scatter_split(slots):
    return max(slots, 8)


def landing_rows(landing, blocks):
    slots = landing.shape[1]
    return tile_rows(landing, scatter_split(slots) // slots, blocks).reshape(1, -1)


def relay_landing_rows(landing, slots, blocks):
    per = scatter_split(slots) // slots
    inner = jnp.arange(RELAY_ROWS, dtype=jnp.int32)
    rows = (landing // blocks * (per * blocks) + landing % blocks)[:, None] + inner % per * blocks
    kind = jnp.arange(RELAY_ROWS // per, dtype=jnp.int32)[:, None, None]
    rows = jnp.where((landing[:, None] >= 0) & (inner // per == kind), rows, -1)
    return rows.reshape(kind.shape[0], -1)


def scatter_terms(target, arrived, slots, rows_dev, blocks, relay_target=None, relayed=None):
    peers, groups, rows, lanes = arrived.shape
    split = scatter_split(slots)
    steps, per = groups * rows // split, split // slots
    high = rows_dev * per * blocks
    specs, operands = [], []
    scratch = [pltpu.VMEM((high, peers * split), BF16)]
    if relayed is not None:
        depth = peers * RELAY_ROWS
        kinds = relay_target.shape[0]
        specs = [
            pl.BlockSpec((kinds, depth), lambda g: (0, 0)),
            pl.BlockSpec((peers, 1, RELAY_ROWS, lanes), lambda g: (0, g // kinds, 0, 0)),
        ]
        operands = [relay_target, relayed]
        scratch += [pltpu.VMEM((kinds, high, depth), BF16)]
    return pl.pallas_call(
        functools.partial(scatter_body, relay=relayed is not None),
        grid=(steps,),
        in_specs=[
            *specs,
            pl.BlockSpec((1, peers * split), lambda g: (0, 0)),
            pl.BlockSpec((peers, 1, split, lanes), lambda g: (0, g, 0, 0)),
        ],
        out_specs=pl.BlockSpec((rows_dev, per, blocks, lanes), lambda g: (0, g, 0, 0)),
        out_shape=jax.ShapeDtypeStruct((rows_dev, steps * per, blocks, lanes), BF16),
        scratch_shapes=scratch,
        compiler_params=params(),
        name="scatter_terms",
    )(*operands, target, arrived.reshape(peers, steps, split, lanes))


def route_body(
    me_ref, list_ref, state_hbm, out_ref, sent_ref, passed_ref, landed_ref, state_ref, sem,
    *, spare, begin, tag, span, caps, outward
):
    peers = list_ref.shape[0]
    second = peers * peers
    copy = pltpu.make_async_copy(state_hbm, state_ref, sem)
    copy.start()
    me = me_ref[0]

    for ref in (sent_ref, passed_ref, landed_ref):

        def clear(index, carry, ref=ref):
            ref[index] = -1
            return carry

        lax.fori_loop(0, ref.shape[0], clear, 0, unroll=8)
    copy.wait()

    def first_at(source, middle):
        return source * peers + middle if outward else middle * peers + source

    def one(row, place, failed):
        value = list_ref[row, begin + place]
        other = value // (span * tag)
        source, last = (row, other) if outward else (other, row)

        def search(carry):
            tries, middle, found = carry
            full = state_ref[first_at(source, middle)] >= caps[0]
            taken = state_ref[second + last * peers + middle] >= caps[1]
            found = jnp.where(full | taken, found, middle)
            following = jnp.where(middle + 1 == peers, 0, middle + 1)
            return tries + 1, following, found

        start = source + last
        start = jnp.where(start >= peers, start - peers, start)
        _, _, found = lax.while_loop(
            lambda carry: (carry[0] < peers) & (carry[2] < 0),
            search,
            (jnp.int32(0), start, jnp.int32(-1)),
        )
        index = row * spare + place
        out_ref[index] = -1

        @pl.when(found >= 0)
        def _():
            first_state, then_state = first_at(source, found), second + last * peers + found
            first, then = state_ref[first_state], state_ref[then_state]
            out_ref[index] = found * caps[1] + then
            state_ref[first_state] = first + 1
            state_ref[then_state] = then + 1
            tile = value // tag - me * span

            @pl.when(source == me)
            def _():
                sent_ref[found * caps[0] + first] = value % tag if outward else tile

            @pl.when(found == me)
            def _():
                passed_ref[last * caps[1] + then] = source * caps[0] + first

            @pl.when(last == me)
            def _():
                landed_ref[found * caps[1] + then] = tile if outward else value % tag

        return failed + jnp.where(found < 0, 1, 0)

    def each(row, failed):
        count = jnp.minimum(list_ref[row, begin + spare], spare)
        return lax.fori_loop(0, count, functools.partial(lambda p, f, r: one(r, p, f), r=row), failed)

    out_ref[peers * spare] = lax.fori_loop(0, peers, each, jnp.int32(0))


def route(me, table, begin, spare, first, second, caps, tag, span, outward):
    peers = table.shape[0]
    state = jnp.concatenate([first, second]).reshape(-1)
    smem = pl.BlockSpec(memory_space=pltpu.SMEM)
    counts = (peers * spare + 1, peers * caps[0], peers * caps[1], peers * caps[1])
    out, sent, passed, landed = pl.pallas_call(
        functools.partial(
            route_body, spare=spare, begin=begin, tag=tag, span=span, caps=caps, outward=outward
        ),
        in_specs=[smem, smem, pl.BlockSpec(memory_space=pl.ANY)],
        out_specs=[smem] * 4,
        out_shape=[jax.ShapeDtypeStruct((count,), jnp.int32) for count in counts],
        scratch_shapes=[pltpu.SMEM((2 * peers * peers,), jnp.int32), pltpu.SemaphoreType.DMA],
        name="route",
    )(me[None], table, state)
    return sent.reshape(peers, caps[0]), passed, landed, out[-1]


def tile_keys(quartets, owner_map):
    blocks = owner_map.shape[0]
    row_blocks = jnp.stack([quartets[:, pick] for pick in ROLE_ROW]).reshape(-1)
    col_blocks = jnp.stack([quartets[:, pick] for pick in ROLE_COL]).reshape(-1)
    ids = jnp.arange(blocks, dtype=jnp.int32)
    storage = jnp.sum(jnp.where(row_blocks[:, None] == ids, owner_map, 0), axis=-1)
    return storage * blocks + col_blocks


def earlier(flags):
    ids = jnp.arange(flags.shape[-1])
    ahead = ids[:, None] < ids[None, :]
    return jnp.sum((flags[..., :, None] & ahead).astype(jnp.int32), axis=-2)


def choose(hit, values, axis):
    return jnp.sum(jnp.where(hit, values + 1, 0), axis=axis) - 1


def spilled(flags, values, spare):
    place = earlier(flags)
    hit = flags[..., None] & (place[..., None] == jnp.arange(spare))
    return choose(hit, values[..., None], -2), jnp.sum(flags.astype(jnp.int32), axis=-1)


def permutation_tables(width):
    lanes = width * width
    low = 128 // width
    index = jnp.arange(lanes, dtype=jnp.int32)
    partner = index % width * width + index // width
    swap = (index[:, None] == partner[None, :]).astype(BF16)
    span = jnp.arange(low * 128, dtype=jnp.int32)
    lead, group, inner = span // 128, span % 128 // width, span % width
    partner = group * 128 + lead * width + inner
    trade = (span[None, :] == partner[:, None]).astype(BF16)
    return swap, trade


def slot_count(most):
    for slots in (4, 8, 16):
        if most <= slots:
            return slots
    raise ValueError(most)


def exchange_slots(array):
    return lax.all_to_all(array, AXES, split_axis=0, concat_axis=0, tiled=True)


def slot_count(most):
    for slots in (4, 8, 16):
        if most <= slots:
            return slots
    raise ValueError(most)


def exchange_slots(array, axis=0):
    return lax.all_to_all(array, AXES, split_axis=axis, concat_axis=axis, tiled=True)


def hand_on(slot_of, received, dens):
    peers = slot_of.shape[0]
    lanes = received.shape[-1]
    shape = (peers, dens // RELAY_ROWS, RELAY_ROWS, lanes)
    rows = slot_rows(slot_of, FIRST_SLOTS, dens).reshape(-1)
    return exchange_slots(pick_rows(rows, received.reshape(-1, lanes), shape=shape))


def local(integrals, quartets, density, owner_map):
    rows_dev, blocks, dens, lanes = density.shape
    devices = lax.axis_size(AXES)
    me = lax.axis_index(AXES)
    quartet_count = quartets.shape[0]
    tile_count = ROLES * quartet_count
    span = rows_dev * blocks
    most = 2 * rows_dev
    tag = 1 << (2 * tile_count - 1).bit_length()
    device_ids = jnp.arange(devices, dtype=jnp.int32)
    tile_ids = jnp.arange(tile_count, dtype=jnp.int32)
    density_rows = jnp.transpose(density, (0, 2, 1, 3))
    swap, trade = permutation_tables(math.isqrt(lanes))

    key = tile_keys(quartets, owner_map)
    holder = key // span
    rank = jnp.sum(
        ((holder[:, None] == holder) & (tile_ids[:, None] < tile_ids)).astype(jnp.int32), axis=0
    )
    asked = jnp.sum((holder[:, None] == device_ids).astype(jnp.int32), axis=0)
    spare, spare_count = spilled(rank >= 2 * READ_SLOTS, key * tag + tile_ids, READ_SPARE)
    message = jnp.concatenate([key * 16 + rank, spare, spare_count[None], asked])
    message = jnp.pad(message, (0, -message.shape[0] % 128))
    told = exchange_slots(jnp.broadcast_to(message, (devices,) + message.shape))
    keys, ranks = told[:, :tile_count] // 16, told[:, :tile_count] % 16
    counts = told[:, tile_count + READ_SPARE + 1 :][:, :devices]
    in_second = jnp.minimum(counts, READ_SLOTS)
    in_first = jnp.minimum(counts - in_second, READ_SLOTS)
    caps = (READ_SLOTS, READ_SLOTS)
    extra, passed, landed, read_misses = route(
        me, told, tile_count, READ_SPARE, in_first, in_second, caps, tag, span, False
    )
    most_spare = jnp.max(told[:, tile_count + READ_SPARE])
    read_fits = (read_misses == 0) & (most_spare <= READ_SPARE)

    mine = keys // span == me
    local_tile = keys - me * span

    def requests(begin, slots):
        hit = mine[:, :, None] & (ranks[:, :, None] == jnp.arange(slots) + begin)
        return choose(hit, local_tile[:, :, None], 1)

    wanted = jnp.maximum(requests(READ_SLOTS, READ_SLOTS), extra)
    sent, sent_then = gather_tiles([wanted, requests(0, READ_SLOTS)], density_rows)
    received = exchange_slots(sent)
    early = quartet_count * 5 // 8
    work = 2 * lanes**3 * early
    first, second = regroup(integrals, swap, trade, 0, early, work=work)
    received, first, second = lax.optimization_barrier((received, first, second))
    passed_rows = slot_rows(passed, READ_SLOTS, dens).reshape(devices, READ_SLOTS, -1, 4)
    passed_rows = jnp.transpose(passed_rows, (0, 2, 3, 1)).reshape(-1)
    passed_on = pick_rows(
        passed_rows, received.reshape(-1, lanes), base=sent_then.reshape(-1, lanes)
    )
    received_then = exchange_slots(passed_on.reshape(sent_then.shape))
    keys, ranks, first, second, _ = lax.optimization_barrier((keys, ranks, first, second, passed_on))
    first, second = regroup(integrals, swap, trade, early, quartet_count, (first, second))

    homes = keys // span
    flat = keys.reshape(-1)
    shared = jnp.sum((flat[:, None] == flat).astype(jnp.int32), axis=0) > 1
    shared = shared.reshape(keys.shape)
    together = homes[:, :, None] == homes[:, None, :]
    before = 1 + (shared[:, :, None] & (tile_ids[:, None] < tile_ids)).astype(jnp.int32)
    low_ranks = jnp.where(shared, jnp.sum(jnp.where(together, before, 0), axis=1), -1)
    at_home = homes[:, :, None] == device_ids
    low_counts = jnp.sum((at_home & shared[:, :, None]).astype(jnp.int32), axis=1)
    both_ranks = jnp.concatenate([ranks, low_ranks], axis=1)
    values = keys * tag + tile_ids
    values = jnp.concatenate([values, values + tile_count], axis=1)
    term_list, term_counts = spilled(both_ranks >= FIRST_SLOTS, values, TERM_SPARE)
    term_table = jnp.concatenate([term_list, term_counts[:, None]], axis=1)
    in_use = counts + low_counts
    caps = (FIRST_SLOTS, 1)
    term_extra, term_passed, term_landed, term_misses = route(
        me, term_table, 0, TERM_SPARE, in_use, jnp.zeros_like(in_use), caps, tag, span, True
    )
    term_fits = (term_misses == 0) & (jnp.max(term_counts) <= TERM_SPARE)

    slot_ids = jnp.arange(devices * READ_SLOTS, dtype=jnp.int32)
    via = choose(landed[:, None] == tile_ids, slot_ids[:, None], 0)
    slot = holder * READ_SLOTS + rank
    then_slot = jnp.where(rank < READ_SLOTS, slot, via)
    direct = (rank >= READ_SLOTS) & (rank < 2 * READ_SLOTS)
    now_slot = jnp.where(direct, slot - READ_SLOTS, -1)
    now_rows = pad_rows(slot_rows(now_slot, READ_SLOTS, dens)).reshape(-1, 1)
    then_rows = pad_rows(slot_rows(then_slot, READ_SLOTS, dens)).reshape(-1, 1)

    two_step = pick_rows(
        now_rows,
        received.reshape(-1, lanes),
        swap,
        then_rows,
        received_then.reshape(-1, lanes),
    )

    def read_one_step():
        slots = slot_count(most)
        (whole,) = gather_tiles([requests(0, slots)], density_rows)
        rows = pad_rows(slot_rows(holder * slots + rank, slots, dens))
        return pick_rows(rows, exchange_slots(whole).reshape(-1, lanes), swap)

    tiles = lax.cond(read_fits, lambda: two_step, read_one_step)
    tiles = tiles.reshape(ROLES, quartet_count, PAD_N, lanes)
    high, low = contract(tiles, integrals, first, second)
    high = high.reshape(tile_count * PAD_N, lanes)
    low = low.reshape(tile_count * PAD_N, lanes)

    def send(term_of_slot, slots):
        per = rows_per_group(slots)
        ids = jnp.arange(dens, dtype=jnp.int32).reshape(1, dens // per, per, 1)
        term = term_of_slot[:, None, None, :]
        rows = jnp.where(term >= 0, term * PAD_N + ids, -1).reshape(-1)
        packed = pack_terms(rows, swap, high, low)
        return exchange_slots(packed.reshape(devices, dens // per, per * slots, lanes))

    to_holder = holder[:, None] == device_ids
    place_ids = jnp.arange(FIRST_SLOTS, dtype=jnp.int32)
    my_low = lax.dynamic_index_in_dim(low_ranks, me, 0, keepdims=False)
    ends = jnp.concatenate([to_holder, to_holder])[:, :, None]
    places = jnp.concatenate([rank, my_low])[:, None, None] == place_ids
    both_ids = jnp.arange(2 * tile_count, dtype=jnp.int32)
    term_of_slot = choose(ends & places, both_ids[:, None, None], 0)
    arrived = send(jnp.maximum(term_of_slot, term_extra), FIRST_SLOTS)
    relayed = hand_on(term_passed, arrived, dens)

    hit = (ranks[:, :, None] == place_ids) | (low_ranks[:, :, None] == place_ids)
    landing = landing_rows(choose(mine[:, :, None] & hit, local_tile[:, :, None], 1), blocks)
    relay_landing = relay_landing_rows(term_landed, FIRST_SLOTS, blocks)
    landing, relay_landing = lax.optimization_barrier((landing, relay_landing))

    def write_two_step():
        return scatter_terms(
            landing, arrived, FIRST_SLOTS, rows_dev, blocks, relay_landing, relayed
        )

    def write_one_step():
        slots = slot_count(most)
        wide = slot_count(2 * slots)
        places = rank[:, None, None] == jnp.arange(slots)
        term_of_slot = choose(to_holder[:, :, None] & places, tile_ids[:, None, None], 0)
        none = jnp.full((devices, wide // 2 - slots), -1, jnp.int32)
        low_term = jnp.where(term_of_slot >= 0, term_of_slot + tile_count, -1)
        whole = send(jnp.concatenate([term_of_slot, none, low_term, none], axis=1), wide)
        wanted = requests(0, slots)
        landing = jnp.concatenate([wanted, none, wanted, none], axis=1)
        return scatter_terms(landing_rows(landing, blocks), whole, wide, rows_dev, blocks)

    fock = lax.cond(term_fits, write_two_step, write_one_step)
    return jnp.transpose(fock, (0, 2, 1, 3))


def solution(mesh):
    return jax.shard_map(
        local,
        mesh=mesh,
        in_specs=(
            P(AXES, None, None),
            P(AXES, None),
            P(AXES, None, None, None),
            P(),
        ),
        out_specs=P(AXES, None, None, None),
        check_vma=False,
    )
```
